32 devices in a mesh: dp: 8 (over y, x, core), mp: 4 (over z).
Axes of the slice: x: 2, y: 2, z: 4, core: 2. Of those that a mesh axis runs over, the one named last changes fastest.
Arguments:
- hidden: bfloat16 [192, 256, 4096], P(('dp', 'mp')), may hold values from -6 to 6
- lengths: int32 [192], P(('dp', 'mp')), may hold values from 32 to 256, as said below
- list_ids: int32 [192], P('dp'), may hold values from 0 to 65535, as said below
- gain: bfloat16 [4096], replicated, may hold values from 0.099609375 to 1.8984375
- head: bfloat16 [4096, 1024], P('dp', 'mp'), may hold values from -0.09375 to 0.09375
- list_slot: int32 [65536], replicated, may hold values from 0 to 65535, as said below
- centroids: bfloat16 [65536, 1024], P('dp'), may hold values from -0.59765625 to 0.59765625
- rotation: bfloat16 [1024, 1024], P('mp'), may hold values from -0.1875 to 0.1875
Outputs:
- codes: bfloat16 [192, 1024], P('dp', 'mp')
- scales: bfloat16 [192, 16], P('dp', 'mp')
The draws below stay inside these ranges and needn't reach their ends.
Inputs may be any that keep to these rules, and one draw needn't show every extreme that they name: `list_ids`: in each aligned block of 24 passages, at most 6 have lists in one range of 8192 lists (list id // 8192); one range holds exactly 6 of them in every block. Each list's row in the centroid table; list_slot[l] // 8192 equals l // 8192, and each row of a range once. `lengths`: some passage has exactly 256 valid tokens.
All inputs are finite; a program needn't handle non-finite values. Where the reference program divides by a largest or mean magnitude, that divisor is 1e-20 or more.
Results may differ from the reference program's by a relative error of at most 0.013.
Values may be sent and summed in bfloat16 or wider, within the bound.
No kernel may reach another device: no remote copies, remote signals or barrier semaphores. Data moves between devices by JAX's collectives and lax.ppermute only.
A program may use at most 64 MiB of HBM per device.

```python
import jax
import jax.numpy as jnp
from jax import lax

D = 4096
EMB = 1024
BLOCK = 64
LISTS = 65536
LEN = 256
PASS_DEV = 24
PASSAGES = 192
LISTS_OWN = 8192
CAP = 6


def draw_lengths(key, part):
    values = jax.random.randint(key, (PASSAGES,), LEN // 8, LEN + 1)
    return values.at[0].set(LEN).astype(jnp.int32)


def draw_list_slot(key, part):
    ranges = LISTS // LISTS_OWN
    keys = jax.random.split(key, ranges)
    perms = jax.vmap(lambda k: jax.random.permutation(k, LISTS_OWN))(keys)
    offsets = jnp.arange(ranges, dtype=jnp.int32)[:, None] * LISTS_OWN
    return (perms.astype(jnp.int32) + offsets).reshape(-1).astype(jnp.int32)


def draw_list_ids(key, part):
    ranges = LISTS // LISTS_OWN
    total_slots = ranges * CAP
    busiest = jax.random.randint(jax.random.fold_in(key, 7), (), 0, ranges)
    blocks = PASSAGES // PASS_DEV

    def one_block(block_key):
        first_key, second_key = jax.random.split(block_key)
        shuffled = jax.random.permutation(first_key, total_slots).astype(jnp.int32)
        places = jnp.arange(total_slots, dtype=jnp.int32)
        score = jnp.where(places // CAP == busiest, places - total_slots, shuffled)
        order = jnp.argsort(score, stable=True).astype(jnp.int32)
        chosen = order[:PASS_DEV] // CAP
        mixing = jax.random.permutation(second_key, PASS_DEV)
        return chosen[mixing]
    owners = jax.vmap(one_block)(jax.random.split(jax.random.fold_in(key, 1), blocks)).reshape(-1)
    within = jax.random.randint(jax.random.fold_in(key, 2), (PASSAGES,), 0, LISTS_OWN)
    return (owners * LISTS_OWN + within).astype(jnp.int32)


def level_of(rng, extent, pieces, low, top_value):
    def one(axis_at, blocks):
        draws = jax.random.uniform(jax.random.fold_in(jax.random.fold_in(rng, 6), axis_at), (blocks,), jnp.float32, low / len(pieces), top_value / len(pieces))
        return jnp.repeat(jnp.exp(draws), extent[axis_at] // blocks).reshape((-1,) + (1,) * (len(extent) - axis_at - 1))

    loudness = one(*pieces[0])
    for cut in pieces[1:]:
        loudness = loudness * one(*cut)
    return loudness


def gaussian(key, dims, width, bound, shards=(), kind=jnp.bfloat16):
    values = jax.random.normal(key, dims, jnp.float32) * width
    if len(shards) > 0:
        values = level_of(key, dims, shards, -0.22, 0.18) * values
    return jnp.clip(values, min=-bound, max=bound).astype(kind)


def setup_inputs(seed: int = 0) -> dict:
    key_of = jax.random.split(jax.random.key(seed), 9)
    hidden = gaussian(key_of[0], (PASSAGES, LEN, D), 1.0, 6.0, ((0, 32),))
    lengths = draw_lengths(jax.random.fold_in(key_of[8], 71), 0)
    list_ids = draw_list_ids(jax.random.fold_in(key_of[8], 71), 0)
    gain = jnp.clip(1.0 + 0.18 * jax.random.normal(key_of[3], (D,), jnp.float32), 0.099609375, 1.8984375).astype(jnp.bfloat16)
    head = gaussian(key_of[4], (D, EMB), D ** -0.5, 0.09375, ((0, 8), (1, 4)))
    list_slot = draw_list_slot(jax.random.fold_in(key_of[8], 71), 0)
    centroids = gaussian(key_of[6], (LISTS, EMB), 0.1, 0.59765625, ((0, 8),))
    rotation = gaussian(key_of[7], (EMB, EMB), EMB ** -0.5, 0.1875, ((0, 4),))
    return {"hidden": hidden, "lengths": lengths, "list_ids": list_ids, "gain": gain, "head": head, "list_slot": list_slot, "centroids": centroids, "rotation": rotation}


def encode(rows, cents, rotation):
    resid = (rows.astype(jnp.float32) - cents.astype(jnp.float32)).astype(jnp.bfloat16)
    rotated = jnp.dot(resid, rotation, preferred_element_type=jnp.float32)
    blocks = rotated.reshape(rotated.shape[0], EMB // BLOCK, BLOCK)
    scale = lax.optimization_barrier(jnp.max(jnp.abs(blocks), axis=-1)) + 1e-06
    codes = (blocks / scale[:, :, None]).reshape(rotated.shape).astype(jnp.bfloat16)
    return (codes, scale.astype(jnp.bfloat16))

def reference(hidden, lengths, list_ids, gain, head, list_slot, centroids, rotation):
    gain_f = gain.astype(jnp.float32)

    def pool_one(pair):
        states, length = pair
        states = states.astype(jnp.float32)
        mean_square = lax.optimization_barrier(jnp.mean(states * states, axis=-1, keepdims=True))
        normed = states * lax.rsqrt(mean_square + 1e-05) * gain_f
        valid = jnp.arange(LEN, dtype=jnp.int32) < length
        total = lax.optimization_barrier(jnp.sum(jnp.where(valid[:, None], normed, 0.0), axis=0))
        return total / length.astype(jnp.float32)
    pooled = lax.map(pool_one, (hidden, lengths)).astype(jnp.bfloat16)
    projected = jnp.dot(pooled, head, preferred_element_type=jnp.float32).astype(jnp.bfloat16)
    slot = list_slot[list_ids].astype(jnp.int32)
    cents = centroids[slot]
    codes, scales = encode(projected, cents, rotation)
    return (codes, scales)
```

```python
import functools

import jax
import jax.numpy as jnp
from jax import lax
from jax.experimental import pallas as pl
from jax.experimental.pallas import tpu as pltpu
from jax.sharding import Mesh
from jax.sharding import PartitionSpec as P

BLOCK = 64
LANES = 128
SUB = 8
DIGIT = 256
CORES = 2
STEP = 64

F32 = jnp.float32
BF16 = jnp.bfloat16


def pool_kernel(
    lens, ids, hidden, slots, gain, out, buf, weight, acc, slot_rows, items, counts, sems, slot_sem,
    *, owners, peers, lists_own, capacity, lead,
):
    passes, length, width = hidden.shape
    group = ids.shape[0]
    steps = length // STEP
    tiles = width // LANES
    rows = out.shape[1] * owners // tiles

    def slot_copy(g):
        return pltpu.make_async_copy(
            slots.at[pl.ds(ids[g] // LANES, 1)], slot_rows.at[pl.ds(g, 1)], slot_sem
        )

    def chunk_copy(p, c):
        return pltpu.make_async_copy(
            hidden.at[p, pl.ds(c * STEP, STEP)], buf.at[p * steps + c], sems.at[p * steps + c]
        )

    count = jnp.int32(0)
    for p in range(passes):
        for c in range(steps):
            needed = c * STEP < lens[p]

            @pl.when(needed)
            def _():
                chunk_copy(p, c).start()
                items[count] = p * steps + c

            count = count + needed.astype(jnp.int32)
    for g in range(group):
        slot_copy(g).start()
    for o in range(owners):
        counts[o] = 0

    def zero(p, _):
        acc[p] = jnp.zeros((SUB, width), F32)
        return 0

    lax.fori_loop(0, passes, zero, 0)
    sub = lax.broadcasted_iota(jnp.int32, (SUB, LANES), 0)

    def arrive(k):
        item = items[k]
        pltpu.make_async_copy(
            hidden.at[0, pl.ds(0, STEP)], buf.at[item], sems.at[item]
        ).wait()

    def weigh(k):
        item = items[k]
        p = item // steps
        start = (item % steps) * STEP
        size = lens[p]
        for s in range(0, STEP, 16):
            total = None
            for t in range(tiles):
                x = buf[item, s : s + 16, t * LANES : (t + 1) * LANES].astype(F32)
                total = x * x if total is None else total + x * x
            square = jnp.sum(total, axis=1, keepdims=True)
            token = lax.broadcasted_iota(jnp.int32, (16, 1), 0) + (start + s)
            value = jnp.where(token < size, lax.rsqrt(square / width + 1e-05), 0.0)
            weight[k % 2, s : s + 16, :] = jnp.broadcast_to(value, (16, LANES))

    def add(k):
        item = items[k]
        p = item // steps
        w = weight[k % 2]
        for t in range(tiles):
            x = buf[item, :, t * LANES : (t + 1) * LANES].astype(F32) * w
            part = x[0:SUB]
            for s in range(SUB, STEP, SUB):
                part = part + x[s : s + SUB]
            acc[p, :, t * LANES : (t + 1) * LANES] += part

    arrive(0)
    weigh(0)

    def body(k, _):
        later = jnp.minimum(k + 1, count - 1)

        @pl.when(k + 1 < count)
        def _():
            arrive(k + 1)

        add(k)
        weigh(later)
        return 0

    lax.fori_loop(0, count - 1, body, 0)
    add(count - 1)

    for g in range(group):
        slot_copy(g).wait()
    owner_row = lax.broadcasted_iota(jnp.int32, (lead, LANES), 0)
    lane = lax.broadcasted_iota(jnp.int32, (lead, LANES), 1)
    info = jnp.zeros((lead, LANES), F32)
    for g in range(group):
        slot = slot_rows[g, ids[g] % LANES]
        owner = slot // lists_own
        local = slot % lists_own
        rank = counts[owner]
        counts[owner] = rank + 1
        place = (g // passes) * rows + g % passes + 1
        for kind, value in enumerate((local // DIGIT, local % DIGIT, jnp.int32(place))):
            here = (owner_row == owner) & (lane == kind * capacity + rank)
            info = jnp.where(here, value.astype(F32), info)

    per = tiles // owners
    for o in range(owners):
        for q in range(per):
            t = o * per + q
            cols = slice(t * LANES, (t + 1) * LANES)
            scale = gain[0:1, cols].astype(F32)
            tile = jnp.zeros((rows, LANES), F32)
            row = lax.broadcasted_iota(jnp.int32, (rows, LANES), 0)
            for p in range(passes):
                line = jnp.sum(acc[p, :, cols], axis=0, keepdims=True) * scale
                line = line / lens[p].astype(F32)
                tile = jnp.where(row == p, jnp.broadcast_to(line, (rows, LANES)), tile)
            if q == 0:
                line = info[o : o + 1]
                tile = jnp.where(row == passes, jnp.broadcast_to(line, (rows, LANES)), tile)
            tile = tile.astype(BF16)
            for j in range(peers):
                out[o * peers + j, q * rows : (q + 1) * rows, :] = tile


def project_kernel(
    got, head, cents, own, other, info_v, info_s, acc, rows_in, spread, packed, info_sem, sem,
    *, owners, peers, passes, capacity, rows,
):
    width = head.shape[1]
    lists_own = cents.shape[0]
    col = pl.multiple_of(lax.axis_index("mp") * width, LANES)
    per = got.shape[1] // rows
    for o in range(owners):
        line = got[o * peers, 0:rows, :].astype(F32)[passes : passes + 1]
        info_v[o : o + 1, :] = line.astype(jnp.int32)
    info_copy = pltpu.make_async_copy(info_v, info_s, info_sem)
    info_copy.start()
    total = None
    for q in range(per):
        x = got[:, q * rows : (q + 1) * rows, :].reshape(owners * peers * rows, LANES)
        y = jnp.dot(x, head[q * LANES : (q + 1) * LANES, :], preferred_element_type=F32)
        total = y if total is None else total + y
    acc[...] = total.reshape(owners, peers * rows, width)
    spread[...] = jnp.zeros(spread.shape, F32)
    info_copy.wait()

    def local_row(o, k):
        value = info_s[o, k] * DIGIT + info_s[o, capacity + k]
        return jnp.clip(value, 0, lists_own - 1)

    def row_copy(o, k, first):
        return pltpu.make_async_copy(
            cents.at[pl.ds(pl.multiple_of(first, SUB), SUB), pl.ds(col, width)],
            rows_in.at[o * capacity + k],
            sem.at[o * capacity + k],
        )

    for o in range(owners):
        for k in range(capacity):
            row_copy(o, k, (local_row(o, k) // SUB) * SUB).start()
    sub = lax.broadcasted_iota(jnp.int32, (SUB, width), 0)
    for o in range(owners):
        for k in range(capacity):
            row_copy(o, k, 0).wait()
    for o in range(owners):
        for k in range(capacity):
            place = info_s[o, 2 * capacity + k]
            place = jnp.where(place > 0, place - 1, peers * rows)
            place = jnp.clip(place, 0, peers * rows)
            tile = rows_in[o * capacity + k].astype(F32)
            line = jnp.sum(jnp.where(sub == local_row(o, k) % SUB, tile, 0.0), axis=0, keepdims=True)
            spread[o, pl.ds(place, 1), :] = line
    core = lax.axis_index("core")
    group = peers * passes
    for side in range(CORES):
        for c in range(owners // CORES):
            o = c * CORES + (core if side == 0 else 1 - core)
            x = acc[o] - spread[o, 0 : peers * rows, :]
            for j in range(peers):
                at = c * group + j * passes
                packed[side, at : at + passes, :] = x[j * rows : j * rows + passes]
    own[...] = packed[0]
    other[...] = packed[1].astype(BF16)


def rotate_kernel(own, other, rotation, out, *, peers):
    group = out.shape[1]
    width = out.shape[2]
    resid = (own[...] + other[...].astype(F32)).astype(BF16)
    for j in range(peers):
        y = jnp.dot(
            resid, rotation[:, j * width : (j + 1) * width], preferred_element_type=F32
        ).astype(BF16)
        for c in range(resid.shape[0] // group):
            out[c * peers + j] = y[c * group : (c + 1) * group]


def quantize_kernel(parts, codes, scales):
    total = parts[0].astype(F32)
    for s in range(1, parts.shape[0]):
        total = total + parts[s].astype(F32)
    group, width = total.shape
    lane = lax.broadcasted_iota(jnp.int32, (group, LANES), 1)
    table = jnp.zeros((group, LANES), F32)
    for t in range(width // LANES):
        x = total[:, t * LANES : (t + 1) * LANES]
        size = jnp.abs(x)
        spread = jnp.zeros((group, LANES), F32)
        for b in range(LANES // BLOCK):
            inside = (lane >= b * BLOCK) & (lane < (b + 1) * BLOCK)
            top = jnp.max(jnp.where(inside, size, 0.0), axis=1, keepdims=True) + 1e-06
            spread = jnp.where(inside, top, spread)
            table = jnp.where(lane == t * (LANES // BLOCK) + b, top, table)
        codes[:, t * LANES : (t + 1) * LANES] = (x / spread).astype(BF16)
    scales[...] = table[:, : scales.shape[1]].astype(BF16)


def per_device(hidden, lengths, list_ids, gain, head, list_slot, centroids, rotation):
    passes, length, width = hidden.shape
    owners = lax.axis_size("chip") * lax.axis_size("core")
    peers = lax.axis_size("mp")
    group = list_ids.shape[0]
    lists_own = centroids.shape[0]
    capacity = max(2, 2 * group // owners)
    rows = -(-(passes + 1) // SUB) * SUB
    per = width // LANES // owners
    cols = head.shape[1]
    lead = -(-owners // SUB) * SUB
    steps = length // STEP
    vmem = pl.BlockSpec(memory_space=pltpu.VMEM)
    smem = pl.BlockSpec(memory_space=pltpu.SMEM)
    hbm = pl.BlockSpec(memory_space=pl.ANY)
    blocks = pl.pallas_call(
        functools.partial(
            pool_kernel, owners=owners, peers=peers, lists_own=lists_own, capacity=capacity, lead=lead
        ),
        out_shape=jax.ShapeDtypeStruct((owners * peers, per * rows, LANES), BF16),
        in_specs=[smem, smem, hbm, hbm, vmem],
        out_specs=vmem,
        scratch_shapes=[
            pltpu.VMEM((passes * steps, STEP, width), BF16),
            pltpu.VMEM((2, STEP, LANES), F32),
            pltpu.VMEM((passes, SUB, width), F32),
            pltpu.SMEM((group, LANES), jnp.int32),
            pltpu.SMEM((passes * steps,), jnp.int32),
            pltpu.SMEM((owners,), jnp.int32),
            pltpu.SemaphoreType.DMA((passes * steps,)),
            pltpu.SemaphoreType.DMA,
        ],
        name="pool",
    )(lengths, list_ids, hidden, list_slot.reshape(-1, LANES), gain.reshape(1, width))
    got = lax.all_to_all(blocks, ("chip", "core", "mp"), 0, 0, tiled=True)
    half = owners // CORES * group
    own, other = pl.pallas_call(
        functools.partial(
            project_kernel, owners=owners, peers=peers, passes=passes, capacity=capacity, rows=rows
        ),
        out_shape=(
            jax.ShapeDtypeStruct((half, cols), F32),
            jax.ShapeDtypeStruct((half, cols), BF16),
        ),
        in_specs=[vmem, vmem, hbm],
        out_specs=(vmem, vmem),
        scratch_shapes=[
            pltpu.VMEM((lead, LANES), jnp.int32),
            pltpu.SMEM((lead, LANES), jnp.int32),
            pltpu.VMEM((owners, peers * rows, cols), F32),
            pltpu.VMEM((owners * capacity, SUB, cols), BF16),
            pltpu.VMEM((owners, peers * rows + SUB, cols), F32),
            pltpu.VMEM((CORES, half, cols), F32),
            pltpu.SemaphoreType.DMA,
            pltpu.SemaphoreType.DMA((owners * capacity,)),
        ],
        name="project",
    )(got, head, centroids)
    other = lax.ppermute(other, "core", [(c, (c + 1) % CORES) for c in range(CORES)])
    parts = pl.pallas_call(
        functools.partial(rotate_kernel, peers=peers),
        out_shape=jax.ShapeDtypeStruct((owners // CORES * peers, group, cols), BF16),
        in_specs=[vmem, vmem, vmem],
        out_specs=vmem,
        name="rotate",
    )(own, other, rotation)
    parts = lax.all_to_all(parts, ("chip", "mp"), 0, 0, tiled=True)
    return pl.pallas_call(
        quantize_kernel,
        out_shape=(
            jax.ShapeDtypeStruct((group, cols), BF16),
            jax.ShapeDtypeStruct((group, cols // BLOCK), BF16),
        ),
        in_specs=[vmem],
        out_specs=(vmem, vmem),
        name="quantize",
    )(parts)


def solution(mesh):
    dp, mp = mesh.shape["dp"], mesh.shape["mp"]
    split = Mesh(mesh.devices.reshape(dp // CORES, CORES, mp), ("chip", "core", "mp"))
    rows = ("chip", "core")
    in_specs = (
        P(("chip", "core", "mp"), None, None),
        P(("chip", "core", "mp")),
        P(rows),
        P(),
        P(rows, "mp"),
        P(),
        P(rows, None),
        P("mp", None),
    )
    out_specs = (P(rows, "mp"), P(rows, "mp"))
    return jax.shard_map(
        per_device, mesh=split, in_specs=in_specs, out_specs=out_specs, check_vma=False
    )
```

```python
import functools

import jax
import jax.numpy as jnp
from jax import lax
from jax.experimental import pallas as pl
from jax.experimental.pallas import tpu as pltpu
from jax.sharding import Mesh
from jax.sharding import PartitionSpec as P

BLOCK = 64
LANES = 128
SUB = 8
DIGIT = 256
CORES = 2
STEP = 64

F32 = jnp.float32
BF16 = jnp.bfloat16


def near(x):
    return pltpu.with_memory_space_constraint(x, pltpu.VMEM)


def pool_kernel(
    lens, ids, hidden, slots, gain, out, buf, weight, acc, slot_rows, items, counts, sems, slot_sem,
    *, owners, peers, lists_own, capacity, lead,
):
    passes, length, width = hidden.shape
    group = ids.shape[0]
    steps = length // STEP
    tiles = width // LANES
    rows = out.shape[1] * owners // tiles

    def slot_copy(g):
        return pltpu.make_async_copy(
            slots.at[pl.ds(ids[g] // LANES, 1)], slot_rows.at[pl.ds(g, 1)], slot_sem
        )

    def chunk_copy(p, c):
        return pltpu.make_async_copy(
            hidden.at[p, pl.ds(c * STEP, STEP)], buf.at[p * steps + c], sems.at[p * steps + c]
        )

    count = jnp.int32(0)
    for p in range(passes):
        for c in range(steps):
            needed = c * STEP < lens[p]

            @pl.when(needed)
            def _():
                chunk_copy(p, c).start()
                items[count] = p * steps + c

            count = count + needed.astype(jnp.int32)
    for g in range(group):
        slot_copy(g).start()
    for o in range(owners):
        counts[o] = 0

    def zero(p, _):
        acc[p] = jnp.zeros((SUB, width), F32)
        return 0

    lax.fori_loop(0, passes, zero, 0)
    sub = lax.broadcasted_iota(jnp.int32, (SUB, LANES), 0)

    def arrive(k):
        item = items[k]
        pltpu.make_async_copy(
            hidden.at[0, pl.ds(0, STEP)], buf.at[item], sems.at[item]
        ).wait()

    def weigh(k):
        item = items[k]
        p = item // steps
        start = (item % steps) * STEP
        size = lens[p]
        for s in range(0, STEP, 16):
            total = None
            for t in range(tiles):
                x = buf[item, s : s + 16, t * LANES : (t + 1) * LANES].astype(F32)
                total = x * x if total is None else total + x * x
            square = jnp.sum(total, axis=1, keepdims=True)
            token = lax.broadcasted_iota(jnp.int32, (16, 1), 0) + (start + s)
            value = jnp.where(token < size, lax.rsqrt(square / width + 1e-05), 0.0)
            weight[k % 2, s : s + 16, :] = jnp.broadcast_to(value, (16, LANES))

    def add(k):
        item = items[k]
        p = item // steps
        w = weight[k % 2]
        for t in range(tiles):
            x = buf[item, :, t * LANES : (t + 1) * LANES].astype(F32) * w
            part = x[0:SUB]
            for s in range(SUB, STEP, SUB):
                part = part + x[s : s + SUB]
            acc[p, :, t * LANES : (t + 1) * LANES] += part

    arrive(0)
    weigh(0)

    def body(k, _):
        later = jnp.minimum(k + 1, count - 1)

        @pl.when(k + 1 < count)
        def _():
            arrive(k + 1)

        add(k)
        weigh(later)
        return 0

    lax.fori_loop(0, count - 1, body, 0)
    add(count - 1)

    for g in range(group):
        slot_copy(g).wait()
    owner_row = lax.broadcasted_iota(jnp.int32, (lead, LANES), 0)
    lane = lax.broadcasted_iota(jnp.int32, (lead, LANES), 1)
    info = jnp.zeros((lead, LANES), F32)
    for g in range(group):
        slot = slot_rows[g, ids[g] % LANES]
        owner = slot // lists_own
        local = slot % lists_own
        rank = counts[owner]
        counts[owner] = rank + 1
        place = (g // passes) * rows + g % passes + 1
        for kind, value in enumerate((local // DIGIT, local % DIGIT, jnp.int32(place))):
            here = (owner_row == owner) & (lane == kind * capacity + rank)
            info = jnp.where(here, value.astype(F32), info)

    per = tiles // owners
    for o in range(owners):
        for q in range(per):
            t = o * per + q
            cols = slice(t * LANES, (t + 1) * LANES)
            scale = gain[t : t + 1].astype(F32)
            tile = jnp.zeros((rows, LANES), F32)
            row = lax.broadcasted_iota(jnp.int32, (rows, LANES), 0)
            for p in range(passes):
                line = jnp.sum(acc[p, :, cols], axis=0, keepdims=True) * scale
                line = line / lens[p].astype(F32)
                tile = jnp.where(row == p, jnp.broadcast_to(line, (rows, LANES)), tile)
            if q == 0:
                line = info[o : o + 1]
                tile = jnp.where(row == passes, jnp.broadcast_to(line, (rows, LANES)), tile)
            tile = tile.astype(BF16)
            for j in range(peers):
                out[o * peers + j, q * rows : (q + 1) * rows, :] = tile


def project_kernel(
    got, head, cents, own, other, info_v, info_s, acc, rows_in, spread, packed, info_sem, sem,
    *, owners, peers, passes, capacity, rows,
):
    width = head.shape[1]
    lists_own = cents.shape[0]
    col = pl.multiple_of(lax.axis_index("mp") * width, LANES)
    per = got.shape[1] // rows
    for o in range(owners):
        line = got[o * peers, 0:rows, :].astype(F32)[passes : passes + 1]
        info_v[o : o + 1, :] = line.astype(jnp.int32)
    info_copy = pltpu.make_async_copy(info_v, info_s, info_sem)
    info_copy.start()
    total = None
    for q in range(per):
        x = got[:, q * rows : (q + 1) * rows, :].reshape(owners * peers * rows, LANES)
        y = jnp.dot(x, head[q * LANES : (q + 1) * LANES, :], preferred_element_type=F32)
        total = y if total is None else total + y
    acc[...] = total.reshape(owners, peers * rows, width)
    spread[...] = jnp.zeros(spread.shape, F32)
    info_copy.wait()

    def local_row(o, k):
        value = info_s[o, k] * DIGIT + info_s[o, capacity + k]
        return jnp.clip(value, 0, lists_own - 1)

    def row_copy(o, k, first):
        return pltpu.make_async_copy(
            cents.at[pl.ds(pl.multiple_of(first, SUB), SUB), pl.ds(col, width)],
            rows_in.at[o * capacity + k],
            sem.at[o * capacity + k],
        )

    for o in range(owners):
        for k in range(capacity):
            row_copy(o, k, (local_row(o, k) // SUB) * SUB).start()
    sub = lax.broadcasted_iota(jnp.int32, (SUB, width), 0)
    for o in range(owners):
        for k in range(capacity):
            row_copy(o, k, 0).wait()
    for o in range(owners):
        for k in range(capacity):
            place = info_s[o, 2 * capacity + k]
            place = jnp.where(place > 0, place - 1, peers * rows)
            place = jnp.clip(place, 0, peers * rows)
            tile = rows_in[o * capacity + k].astype(F32)
            line = jnp.sum(jnp.where(sub == local_row(o, k) % SUB, tile, 0.0), axis=0, keepdims=True)
            spread[o, pl.ds(place, 1), :] = line
    core = lax.axis_index("core")
    group = peers * passes
    for side in range(CORES):
        for c in range(owners // CORES):
            o = c * CORES + (core if side == 0 else 1 - core)
            x = acc[o] - spread[o, 0 : peers * rows, :]
            for j in range(peers):
                at = c * group + j * passes
                packed[side, at : at + passes, :] = x[j * rows : j * rows + passes]
    own[...] = packed[0]
    other[...] = packed[1].astype(BF16)


def rotate_kernel(own, other, rotation, out, *, peers):
    group = out.shape[1]
    width = out.shape[2]
    resid = (own[...] + other[...].astype(F32)).astype(BF16)
    for j in range(peers):
        y = jnp.dot(
            resid, rotation[:, j * width : (j + 1) * width], preferred_element_type=F32
        ).astype(BF16)
        for c in range(resid.shape[0] // group):
            out[c * peers + j] = y[c * group : (c + 1) * group]


def quantize_kernel(parts, codes, scales):
    total = parts[0].astype(F32)
    for s in range(1, parts.shape[0]):
        total = total + parts[s].astype(F32)
    group, width = total.shape
    lane = lax.broadcasted_iota(jnp.int32, (group, LANES), 1)
    table = jnp.zeros((group, LANES), F32)
    for t in range(width // LANES):
        x = total[:, t * LANES : (t + 1) * LANES]
        size = jnp.abs(x)
        spread = jnp.zeros((group, LANES), F32)
        for b in range(LANES // BLOCK):
            inside = (lane >= b * BLOCK) & (lane < (b + 1) * BLOCK)
            top = jnp.max(jnp.where(inside, size, 0.0), axis=1, keepdims=True) + 1e-06
            spread = jnp.where(inside, top, spread)
            table = jnp.where(lane == t * (LANES // BLOCK) + b, top, table)
        codes[:, t * LANES : (t + 1) * LANES] = (x / spread).astype(BF16)
    scales[...] = table.T[: scales.shape[0]].astype(BF16)


def per_device(hidden, lengths, list_ids, gain, head, list_slot, centroids, rotation):
    passes, length, width = hidden.shape
    owners = lax.axis_size("chip") * lax.axis_size("core")
    peers = lax.axis_size("mp")
    group = list_ids.shape[0]
    lists_own = centroids.shape[0]
    capacity = max(2, 2 * group // owners)
    rows = -(-(passes + 1) // SUB) * SUB
    per = width // LANES // owners
    cols = head.shape[1]
    lead = -(-owners // SUB) * SUB
    steps = length // STEP
    vmem = pl.BlockSpec(memory_space=pltpu.VMEM)
    smem = pl.BlockSpec(memory_space=pltpu.SMEM)
    hbm = pl.BlockSpec(memory_space=pl.ANY)
    blocks = pl.pallas_call(
        functools.partial(
            pool_kernel, owners=owners, peers=peers, lists_own=lists_own, capacity=capacity, lead=lead
        ),
        out_shape=pltpu.VMEM((owners * peers, per * rows, LANES), BF16),
        in_specs=[smem, smem, hbm, hbm, vmem],
        out_specs=vmem,
        scratch_shapes=[
            pltpu.VMEM((passes * steps, STEP, width), BF16),
            pltpu.VMEM((2, STEP, LANES), F32),
            pltpu.VMEM((passes, SUB, width), F32),
            pltpu.SMEM((group, LANES), jnp.int32),
            pltpu.SMEM((passes * steps,), jnp.int32),
            pltpu.SMEM((owners,), jnp.int32),
            pltpu.SemaphoreType.DMA((passes * steps,)),
            pltpu.SemaphoreType.DMA,
        ],
        compiler_params=pltpu.CompilerParams(vmem_limit_bytes=hidden.size * 2 + 6 * 2**20),
        name="pool",
    )(lengths, list_ids, hidden, list_slot.reshape(-1, LANES), gain.reshape(-1, LANES))
    got = lax.all_to_all(blocks, ("chip", "core", "mp"), 0, 0, tiled=True)
    half = owners // CORES * group
    own, other = pl.pallas_call(
        functools.partial(
            project_kernel, owners=owners, peers=peers, passes=passes, capacity=capacity, rows=rows
        ),
        out_shape=(
            pltpu.VMEM((half, cols), F32),
            pltpu.VMEM((half, cols), BF16),
        ),
        in_specs=[vmem, vmem, hbm],
        out_specs=(vmem, vmem),
        scratch_shapes=[
            pltpu.VMEM((lead, LANES), jnp.int32),
            pltpu.SMEM((lead, LANES), jnp.int32),
            pltpu.VMEM((owners, peers * rows, cols), F32),
            pltpu.VMEM((owners * capacity, SUB, cols), BF16),
            pltpu.VMEM((owners, peers * rows + SUB, cols), F32),
            pltpu.VMEM((CORES, half, cols), F32),
            pltpu.SemaphoreType.DMA,
            pltpu.SemaphoreType.DMA((owners * capacity,)),
        ],
        compiler_params=pltpu.CompilerParams(vmem_limit_bytes=8 * 2**20),
        name="project",
    )(near(got), near(head), centroids)
    other = lax.ppermute(other, "core", [(c, (c + 1) % CORES) for c in range(CORES)])
    parts = pl.pallas_call(
        functools.partial(rotate_kernel, peers=peers),
        out_shape=pltpu.VMEM((owners // CORES * peers, group, cols), BF16),
        in_specs=[vmem, vmem, vmem],
        out_specs=vmem,
        compiler_params=pltpu.CompilerParams(vmem_limit_bytes=8 * 2**20),
        name="rotate",
    )(near(own), near(other), near(rotation))
    parts = lax.all_to_all(parts, ("chip", "mp"), 0, 0, tiled=True)
    codes, scales = pl.pallas_call(
        quantize_kernel,
        out_shape=(
            jax.ShapeDtypeStruct((group, cols), BF16),
            jax.ShapeDtypeStruct((cols // BLOCK, group), BF16),
        ),
        in_specs=[vmem],
        out_specs=(vmem, vmem),
        compiler_params=pltpu.CompilerParams(vmem_limit_bytes=8 * 2**20),
        name="quantize",
    )(near(parts))
    return codes, scales.T


def solution(mesh):
    dp, mp = mesh.shape["dp"], mesh.shape["mp"]
    split = Mesh(mesh.devices.reshape(dp // CORES, CORES, mp), ("chip", "core", "mp"))
    rows = ("chip", "core")
    in_specs = (
        P(("chip", "core", "mp"), None, None),
        P(("chip", "core", "mp")),
        P(rows),
        P(),
        P(rows, "mp"),
        P(),
        P(rows, None),
        P("mp", None),
    )
    out_specs = (P(rows, "mp"), P(rows, "mp"))
    return jax.shard_map(
        per_device, mesh=split, in_specs=in_specs, out_specs=out_specs, check_vma=False
    )
```

```python
import functools

import jax
import jax.numpy as jnp
from jax import lax
from jax.experimental import pallas as pl
from jax.experimental.pallas import tpu as pltpu
from jax.sharding import Mesh
from jax.sharding import PartitionSpec as P

BLOCK = 64
LANES = 128
SUB = 8
DIGIT = 256
CORES = 2
STEP = 64

F32 = jnp.float32
BF16 = jnp.bfloat16


def near(x):
    return pltpu.with_memory_space_constraint(x, pltpu.VMEM)


def far(x):
    return pltpu.with_memory_space_constraint(x, pltpu.HBM)


def pool_kernel(
    lens, ids, hidden, slots, gain, head, out, head_out, buf, weight, acc, slot_rows, items, counts,
    sems, slot_sem, head_sem, *, owners, peers, lists_own, capacity, lead,
):
    passes, length, width = hidden.shape
    group = ids.shape[0]
    steps = length // STEP
    tiles = width // LANES
    rows = out.shape[1] * owners // tiles

    def slot_copy(g):
        return pltpu.make_async_copy(
            slots.at[pl.ds(ids[g] // LANES, 1)], slot_rows.at[pl.ds(g, 1)], slot_sem
        )

    def chunk_copy(p, c):
        return pltpu.make_async_copy(
            hidden.at[p, pl.ds(c * STEP, STEP)], buf.at[p * steps + c], sems.at[p * steps + c]
        )

    count = jnp.int32(0)
    for p in range(passes):
        for c in range(steps):
            needed = c * STEP < lens[p]

            @pl.when(needed)
            def _():
                chunk_copy(p, c).start()
                items[count] = p * steps + c

            count = count + needed.astype(jnp.int32)
    for g in range(group):
        slot_copy(g).start()
    head_copy = pltpu.make_async_copy(head, head_out, head_sem)
    head_copy.start()
    for o in range(owners):
        counts[o] = 0

    def zero(p, _):
        acc[p] = jnp.zeros((SUB, width), F32)
        return 0

    lax.fori_loop(0, passes, zero, 0)
    sub = lax.broadcasted_iota(jnp.int32, (SUB, LANES), 0)

    def arrive(k):
        item = items[k]
        pltpu.make_async_copy(
            hidden.at[0, pl.ds(0, STEP)], buf.at[item], sems.at[item]
        ).wait()

    def weigh(k):
        item = items[k]
        p = item // steps
        start = (item % steps) * STEP
        size = lens[p]
        for s in range(0, STEP, 16):
            total = None
            for t in range(tiles):
                x = buf[item, s : s + 16, t * LANES : (t + 1) * LANES].astype(F32)
                total = x * x if total is None else total + x * x
            square = jnp.sum(total, axis=1, keepdims=True)
            token = lax.broadcasted_iota(jnp.int32, (16, 1), 0) + (start + s)
            value = jnp.where(token < size, lax.rsqrt(square / width + 1e-05), 0.0)
            weight[k % 2, s : s + 16, :] = jnp.broadcast_to(value, (16, LANES))

    def add(k):
        item = items[k]
        p = item // steps
        w = weight[k % 2]
        for t in range(tiles):
            x = buf[item, :, t * LANES : (t + 1) * LANES].astype(F32) * w
            part = x[0:SUB]
            for s in range(SUB, STEP, SUB):
                part = part + x[s : s + SUB]
            acc[p, :, t * LANES : (t + 1) * LANES] += part

    arrive(0)
    weigh(0)

    def body(k, _):
        later = jnp.minimum(k + 1, count - 1)

        @pl.when(k + 1 < count)
        def _():
            arrive(k + 1)

        add(k)
        weigh(later)
        return 0

    lax.fori_loop(0, count - 1, body, 0)
    add(count - 1)

    head_copy.wait()
    for g in range(group):
        slot_copy(g).wait()
    owner_row = lax.broadcasted_iota(jnp.int32, (lead, LANES), 0)
    lane = lax.broadcasted_iota(jnp.int32, (lead, LANES), 1)
    info = jnp.zeros((lead, LANES), F32)
    for g in range(group):
        slot = slot_rows[g, ids[g] % LANES]
        owner = slot // lists_own
        local = slot % lists_own
        rank = counts[owner]
        counts[owner] = rank + 1
        place = (g // passes) * rows + g % passes + 1
        for kind, value in enumerate((local // DIGIT, local % DIGIT, jnp.int32(place))):
            here = (owner_row == owner) & (lane == kind * capacity + rank)
            info = jnp.where(here, value.astype(F32), info)

    per = tiles // owners
    for o in range(owners):
        for q in range(per):
            t = o * per + q
            cols = slice(t * LANES, (t + 1) * LANES)
            scale = gain[t : t + 1].astype(F32)
            tile = jnp.zeros((rows, LANES), F32)
            row = lax.broadcasted_iota(jnp.int32, (rows, LANES), 0)
            for p in range(passes):
                line = jnp.sum(acc[p, :, cols], axis=0, keepdims=True) * scale
                line = line / lens[p].astype(F32)
                tile = jnp.where(row == p, jnp.broadcast_to(line, (rows, LANES)), tile)
            if q == 0:
                line = info[o : o + 1]
                tile = jnp.where(row == passes, jnp.broadcast_to(line, (rows, LANES)), tile)
            tile = tile.astype(BF16)
            for j in range(peers):
                out[o * peers + j, q * rows : (q + 1) * rows, :] = tile


def project_kernel(
    got, head, cents, own, other, info_v, info_s, acc, rows_in, spread, packed, info_sem, sem,
    *, owners, peers, passes, capacity, rows,
):
    width = head.shape[1]
    lists_own = cents.shape[0]
    col = pl.multiple_of(lax.axis_index("mp") * width, LANES)
    per = got.shape[1] // rows
    for o in range(owners):
        line = got[o * peers, 0:rows, :].astype(F32)[passes : passes + 1]
        info_v[o : o + 1, :] = line.astype(jnp.int32)
    info_copy = pltpu.make_async_copy(info_v, info_s, info_sem)
    info_copy.start()
    total = None
    for q in range(per):
        x = got[:, q * rows : (q + 1) * rows, :].reshape(owners * peers * rows, LANES)
        y = jnp.dot(x, head[q * LANES : (q + 1) * LANES, :], preferred_element_type=F32)
        total = y if total is None else total + y
    acc[...] = total.reshape(owners, peers * rows, width)
    spread[...] = jnp.zeros(spread.shape, F32)
    info_copy.wait()

    def local_row(o, k):
        value = info_s[o, k] * DIGIT + info_s[o, capacity + k]
        return jnp.clip(value, 0, lists_own - 1)

    def row_copy(o, k, first):
        return pltpu.make_async_copy(
            cents.at[pl.ds(pl.multiple_of(first, SUB), SUB), pl.ds(col, width)],
            rows_in.at[o * capacity + k],
            sem.at[o * capacity + k],
        )

    for o in range(owners):
        for k in range(capacity):
            row_copy(o, k, (local_row(o, k) // SUB) * SUB).start()
    sub = lax.broadcasted_iota(jnp.int32, (SUB, width), 0)
    for o in range(owners):
        for k in range(capacity):
            row_copy(o, k, 0).wait()
    for o in range(owners):
        for k in range(capacity):
            place = info_s[o, 2 * capacity + k]
            place = jnp.where(place > 0, place - 1, peers * rows)
            place = jnp.clip(place, 0, peers * rows)
            tile = rows_in[o * capacity + k].astype(F32)
            line = jnp.sum(jnp.where(sub == local_row(o, k) % SUB, tile, 0.0), axis=0, keepdims=True)
            spread[o, pl.ds(place, 1), :] = line
    core = lax.axis_index("core")
    group = peers * passes
    for side in range(CORES):
        for c in range(owners // CORES):
            o = c * CORES + (core if side == 0 else 1 - core)
            x = acc[o] - spread[o, 0 : peers * rows, :]
            for j in range(peers):
                at = c * group + j * passes
                packed[side, at : at + passes, :] = x[j * rows : j * rows + passes]
    own[...] = packed[0]
    other[...] = packed[1].astype(BF16)


def rotate_kernel(own, other, rotation, out, *, peers):
    group = out.shape[1]
    width = out.shape[2]
    resid = (own[...] + other[...].astype(F32)).astype(BF16)
    for j in range(peers):
        y = jnp.dot(
            resid, rotation[:, j * width : (j + 1) * width], preferred_element_type=F32
        ).astype(BF16)
        for c in range(resid.shape[0] // group):
            out[c * peers + j] = y[c * group : (c + 1) * group]


def quantize_kernel(parts, codes, scales):
    total = parts[0].astype(F32)
    for s in range(1, parts.shape[0]):
        total = total + parts[s].astype(F32)
    group, width = total.shape
    lane = lax.broadcasted_iota(jnp.int32, (group, LANES), 1)
    table = jnp.zeros((group, LANES), F32)
    for t in range(width // LANES):
        x = total[:, t * LANES : (t + 1) * LANES]
        size = jnp.abs(x)
        spread = jnp.zeros((group, LANES), F32)
        for b in range(LANES // BLOCK):
            inside = (lane >= b * BLOCK) & (lane < (b + 1) * BLOCK)
            top = jnp.max(jnp.where(inside, size, 0.0), axis=1, keepdims=True) + 1e-06
            spread = jnp.where(inside, top, spread)
            table = jnp.where(lane == t * (LANES // BLOCK) + b, top, table)
        codes[:, t * LANES : (t + 1) * LANES] = (x / spread).astype(BF16)
    scales[...] = table.T[: scales.shape[0]].astype(BF16)


def per_device(hidden, lengths, list_ids, gain, head, list_slot, centroids, rotation):
    passes, length, width = hidden.shape
    owners = lax.axis_size("chip") * lax.axis_size("core")
    peers = lax.axis_size("mp")
    group = list_ids.shape[0]
    lists_own = centroids.shape[0]
    capacity = max(2, 2 * group // owners)
    rows = -(-(passes + 1) // SUB) * SUB
    per = width // LANES // owners
    cols = head.shape[1]
    lead = -(-owners // SUB) * SUB
    steps = length // STEP
    vmem = pl.BlockSpec(memory_space=pltpu.VMEM)
    smem = pl.BlockSpec(memory_space=pltpu.SMEM)
    hbm = pl.BlockSpec(memory_space=pl.ANY)
    blocks, head = pl.pallas_call(
        functools.partial(
            pool_kernel, owners=owners, peers=peers, lists_own=lists_own, capacity=capacity, lead=lead
        ),
        out_shape=(
            pltpu.VMEM((owners * peers, per * rows, LANES), BF16),
            pltpu.VMEM(head.shape, BF16),
        ),
        in_specs=[smem, smem, hbm, hbm, vmem, hbm],
        out_specs=(vmem, vmem),
        scratch_shapes=[
            pltpu.VMEM((passes * steps, STEP, width), BF16),
            pltpu.VMEM((2, STEP, LANES), F32),
            pltpu.VMEM((passes, SUB, width), F32),
            pltpu.SMEM((group, LANES), jnp.int32),
            pltpu.SMEM((passes * steps,), jnp.int32),
            pltpu.SMEM((owners,), jnp.int32),
            pltpu.SemaphoreType.DMA((passes * steps,)),
            pltpu.SemaphoreType.DMA,
            pltpu.SemaphoreType.DMA,
        ],
        compiler_params=pltpu.CompilerParams(vmem_limit_bytes=hidden.size * 2 + 6 * 2**20),
        name="pool",
    )(
        far(lengths), far(list_ids), far(hidden), far(list_slot.reshape(-1, LANES)),
        far(gain.reshape(-1, LANES)), far(head),
    )
    got = lax.all_to_all(blocks, ("chip", "core", "mp"), 0, 0, tiled=True)
    half = owners // CORES * group
    own, other = pl.pallas_call(
        functools.partial(
            project_kernel, owners=owners, peers=peers, passes=passes, capacity=capacity, rows=rows
        ),
        out_shape=(
            pltpu.VMEM((half, cols), F32),
            pltpu.VMEM((half, cols), BF16),
        ),
        in_specs=[vmem, vmem, hbm],
        out_specs=(vmem, vmem),
        scratch_shapes=[
            pltpu.VMEM((lead, LANES), jnp.int32),
            pltpu.SMEM((lead, LANES), jnp.int32),
            pltpu.VMEM((owners, peers * rows, cols), F32),
            pltpu.VMEM((owners * capacity, SUB, cols), BF16),
            pltpu.VMEM((owners, peers * rows + SUB, cols), F32),
            pltpu.VMEM((CORES, half, cols), F32),
            pltpu.SemaphoreType.DMA,
            pltpu.SemaphoreType.DMA((owners * capacity,)),
        ],
        compiler_params=pltpu.CompilerParams(vmem_limit_bytes=8 * 2**20),
        name="project",
    )(near(got), near(head), far(centroids))
    other = lax.ppermute(other, "core", [(c, (c + 1) % CORES) for c in range(CORES)])
    parts = pl.pallas_call(
        functools.partial(rotate_kernel, peers=peers),
        out_shape=pltpu.VMEM((owners // CORES * peers, group, cols), BF16),
        in_specs=[vmem, vmem, vmem],
        out_specs=vmem,
        compiler_params=pltpu.CompilerParams(vmem_limit_bytes=8 * 2**20),
        name="rotate",
    )(near(own), near(other), near(rotation))
    parts = lax.all_to_all(parts, ("chip", "mp"), 0, 0, tiled=True)
    codes, scales = pl.pallas_call(
        quantize_kernel,
        out_shape=(
            jax.ShapeDtypeStruct((group, cols), BF16),
            jax.ShapeDtypeStruct((cols // BLOCK, group), BF16),
        ),
        in_specs=[vmem],
        out_specs=(vmem, vmem),
        compiler_params=pltpu.CompilerParams(vmem_limit_bytes=8 * 2**20),
        name="quantize",
    )(near(parts))
    return codes, scales.T


def solution(mesh):
    dp, mp = mesh.shape["dp"], mesh.shape["mp"]
    split = Mesh(mesh.devices.reshape(dp // CORES, CORES, mp), ("chip", "core", "mp"))
    rows = ("chip", "core")
    in_specs = (
        P(("chip", "core", "mp"), None, None),
        P(("chip", "core", "mp")),
        P(rows),
        P(),
        P(rows, "mp"),
        P(),
        P(rows, None),
        P("mp", None),
    )
    out_specs = (P(rows, "mp"), P(rows, "mp"))
    return jax.shard_map(
        per_device, mesh=split, in_specs=in_specs, out_specs=out_specs, check_vma=False
    )
```

```python
import functools

import jax
import jax.numpy as jnp
from jax import lax
from jax.experimental import pallas as pl
from jax.experimental.pallas import tpu as pltpu
from jax.sharding import Mesh
from jax.sharding import PartitionSpec as P

BLOCK = 64
LANES = 128
SUB = 8
DIGIT = 256
CORES = 2
STEP = 64

F32 = jnp.float32
BF16 = jnp.bfloat16


def near(x):
    return pltpu.with_memory_space_constraint(x, pltpu.VMEM)


def far(x):
    return pltpu.with_memory_space_constraint(x, pltpu.HBM)


def pool_kernel(
    lens_hbm, ids_hbm, hidden, slots, gain_hbm, head, out, head_out, buf, weight, acc, slot_rows, gain,
    lens, ids, items, sems, slot_sem, side_sems, *, owners, peers, lists_own, capacity,
):
    passes, length, width = hidden.shape
    group = ids.shape[0]
    steps = length // STEP
    tiles = width // LANES
    per = tiles // owners
    rows = out.shape[1] // per

    def chunk_copy(p, c):
        return pltpu.make_async_copy(
            hidden.at[p, pl.ds(c * STEP, STEP)], buf.at[p * steps + c], sems.at[p * steps + c]
        )

    def slot_copy(g):
        return pltpu.make_async_copy(
            slots.at[pl.ds(lax.div(ids[g], LANES), 1)], slot_rows.at[pl.ds(g, 1)], slot_sem
        )

    side = [
        pltpu.make_async_copy(source, target, side_sems.at[n])
        for n, (source, target) in enumerate(
            ((lens_hbm, lens), (ids_hbm, ids), (gain_hbm, gain), (head, head_out))
        )
    ]
    side[0].start()
    side[1].start()
    for p in range(passes):
        chunk_copy(p, 0).start()
        items[p] = p * steps
    side[0].wait()
    count = jnp.int32(passes)
    for c in range(1, steps):
        for p in range(passes):
            needed = lens[p] > c * STEP

            @pl.when(needed)
            def _():
                chunk_copy(p, c).start()
                items[count] = p * steps + c

            count = count + needed.astype(jnp.int32)
    side[1].wait()
    for g in range(group):
        slot_copy(g).start()
    side[2].start()
    side[3].start()

    def zero(p, _):
        acc[p] = jnp.zeros((SUB, width), F32)
        return 0

    lax.fori_loop(0, passes, zero, 0)

    def arrive(k):
        item = items[k]
        pltpu.make_async_copy(
            hidden.at[0, pl.ds(0, STEP)], buf.at[item], sems.at[item]
        ).wait()

    def weigh(k):
        item = items[k]
        p = lax.div(item, steps)
        start = lax.rem(item, steps) * STEP
        size = lens[p]
        for s in range(0, STEP, SUB):
            x = buf[item, s : s + SUB, :]
            x = x * x
            x = (x[:, : width // 2] + x[:, width // 2 :]).astype(F32)
            total = x[:, :LANES]
            for t in range(LANES, width // 2, LANES):
                total = total + x[:, t : t + LANES]
            square = jnp.sum(total, axis=1, keepdims=True)
            token = lax.broadcasted_iota(jnp.int32, (SUB, 1), 0) + (start + s)
            value = jnp.where(token < size, lax.rsqrt(square * (1.0 / width) + 1e-05), 0.0)
            weight[lax.rem(k, 2), s : s + SUB, :] = jnp.broadcast_to(value, (SUB, LANES))

    def add(k):
        item = items[k]
        p = lax.div(item, steps)
        w = weight[lax.rem(k, 2)]
        for t in range(tiles):
            x = buf[item, :, t * LANES : (t + 1) * LANES].astype(F32) * w
            part = x[0:SUB]
            for s in range(SUB, STEP, SUB):
                part = part + x[s : s + SUB]
            acc[p, :, t * LANES : (t + 1) * LANES] += part

    arrive(0)
    weigh(jnp.int32(0))

    def body(k, _):
        arrive(k + 1)
        add(k)
        weigh(k + 1)
        return 0

    lax.fori_loop(0, count - 1, body, 0)
    for n in (2, 3):
        side[n].wait()
    for g in range(group):
        slot_copy(g).wait()
    add(count - 1)

    shape = (-(-group // SUB) * SUB, LANES)
    sub = lax.broadcasted_iota(jnp.int32, (SUB, LANES), 0)
    blocks = []
    for start in range(0, shape[0], SUB):
        block = jnp.zeros((SUB, LANES), jnp.int32)
        for g in range(start, min(start + SUB, group)):
            block = jnp.where(sub == g - start, lax.rem(ids[g], LANES), block)
        blocks.append(block)
    column = jnp.concatenate(blocks, axis=0)
    line = lax.broadcasted_iota(jnp.int32, shape, 0)
    lane = lax.broadcasted_iota(jnp.int32, shape, 1)
    picked = jnp.where((lane == column) & (line < group), slot_rows[...], 0).astype(F32)
    slot = jnp.sum(picked, axis=1, keepdims=True).astype(jnp.int32)
    slot = jnp.broadcast_to(slot, shape)
    owner = lax.div(slot, lists_own)
    local = slot - owner * lists_own
    high = lax.div(local, DIGIT)
    low = local - high * DIGIT
    owner_line = jnp.sum(jnp.where(line == lane, owner.astype(F32), 0.0), axis=0, keepdims=True)
    earlier = (jnp.broadcast_to(owner_line, shape) == owner.astype(F32)) & (lane < line)
    rank = jnp.sum(jnp.where(earlier, 1.0, 0.0), axis=1, keepdims=True).astype(jnp.int32)
    rank = jnp.broadcast_to(rank, shape)
    peer = jnp.zeros(shape, jnp.int32)
    for j in range(1, peers):
        peer = peer + (line >= j * passes).astype(jnp.int32)
    place = line + peer * (rows - passes) + 1
    entry = jnp.where(lane == rank, high, 0)
    entry = jnp.where(lane == rank + capacity, low, entry)
    entry = jnp.where(lane == rank + 2 * capacity, place, entry)
    entry = jnp.where((rank < capacity) & (line < group), entry, 0).astype(F32)

    inverse = jnp.zeros((SUB, LANES), F32)
    for p in range(passes):
        inverse = jnp.where(sub == p, lens[p].astype(F32), inverse)
    inverse = jnp.where(sub < passes, 1.0 / jnp.maximum(inverse, 1.0), 0.0)
    for o in range(owners):
        info = jnp.sum(jnp.where(owner == o, entry, 0.0), axis=0, keepdims=True)
        for q in range(per):
            t = o * per + q
            cols = slice(t * LANES, (t + 1) * LANES)
            parts = [acc[p, :, cols] if p < passes else None for p in range(SUB)]
            bit = SUB // 2
            while bit:
                merged = []
                for n in range(bit):
                    a, b = parts[n], parts[n + bit]
                    if a is None:
                        merged.append(None)
                    elif b is None:
                        merged.append(jnp.where((sub & bit) == 0, a + pltpu.roll(a, SUB - bit, 0), 0.0))
                    else:
                        first = jnp.where((sub & bit) == 0, a, b)
                        second = jnp.where((sub & bit) == 0, b, a)
                        if bit * 2 == SUB:
                            merged.append(first + pltpu.roll(second, bit, 0))
                        else:
                            up = pltpu.roll(second, SUB - bit, 0)
                            down = pltpu.roll(second, bit, 0)
                            merged.append(first + jnp.where((sub & bit) == 0, up, down))
                parts = merged
                bit //= 2
            tile = parts[0] * gain[t : t + 1].astype(F32) * inverse
            if q == 0:
                tile = jnp.where(sub == passes, jnp.broadcast_to(info, (SUB, LANES)), tile)
            tile = tile.astype(BF16)
            for j in range(peers):
                out[o * peers + j, q * rows : (q + 1) * rows, :] = tile


def project_kernel(
    got, head, cents, own, other, info_v, info_s, acc, rows_in, packed, info_sem, row_sems,
    *, owners, peers, passes, capacity,
):
    rows = SUB
    width = head.shape[1]
    lists_own = cents.shape[0]
    per = got.shape[1] // rows
    wide = peers * rows
    col = pl.multiple_of(lax.axis_index("mp") * width, LANES)
    for o in range(owners):
        line = got[o * peers, 0:rows, :].astype(F32)[passes : passes + 1]
        info_v[o : o + 1, :] = line.astype(jnp.int32)
    info_copy = pltpu.make_async_copy(info_v, info_s, info_sem)
    info_copy.start()
    info_copy.wait()
    entries = [(o, k) for o in range(owners) for k in range(capacity)]

    def row_copy(n, first):
        return pltpu.make_async_copy(
            cents.at[pl.ds(first, SUB), pl.ds(col, width)], rows_in.at[n], row_sems.at[n]
        )

    which = []
    for n, (o, k) in enumerate(entries):
        row = jnp.clip(info_s[o, k] * DIGIT + info_s[o, capacity + k], 0, lists_own - 1)
        first = lax.div(row, SUB) * SUB
        row_copy(n, pl.multiple_of(first, SUB)).start()
        which.append(row - first)
    total = None
    for q in range(per):
        x = got[:, q * rows : (q + 1) * rows, :].reshape(owners * peers * rows, LANES)
        y = jnp.dot(x, head[q * LANES : (q + 1) * LANES, :], preferred_element_type=F32)
        total = y if total is None else total + y
    lane = lax.broadcasted_iota(jnp.int32, (1, LANES), 1)
    share = LANES // SUB
    for n in range(len(entries)):
        row_copy(n, 0).wait()
    for start in range(0, len(entries), share):
        part = entries[start : start + share]
        target = jnp.full((1, LANES), -1, jnp.int32)
        for m, (o, k) in enumerate(part):
            place = info_s[o, 2 * capacity + k]
            at = jnp.where((place > 0) & (place <= wide), o * wide + place - 1, -1)
            target = jnp.where(lane == m * SUB + which[start + m], at, target)
        depth = len(part) * SUB
        spots = lax.broadcasted_iota(jnp.int32, (owners * wide, LANES), 0)
        chosen = jnp.where(spots == target, 1.0, 0.0).astype(BF16)[:, :depth]
        lines = rows_in[start : start + len(part)].reshape(depth, width)
        total = total - jnp.dot(chosen, lines, preferred_element_type=F32)
    acc[...] = total.reshape(owners, wide, width)
    core = lax.axis_index("core")
    group = peers * passes
    for side in range(CORES):
        for c in range(owners // CORES):
            x = acc[c * CORES + (core if side == 0 else 1 - core)]
            for j in range(peers):
                at = c * group + j * passes
                packed[side, at : at + passes, :] = x[j * rows : j * rows + passes]
    own[...] = packed[0]
    other[...] = packed[1].astype(BF16)


def rotate_kernel(own, other, rotation, out, *, peers):
    group = out.shape[1]
    width = out.shape[2]
    resid = (own[...] + other[...].astype(F32)).astype(BF16)
    for j in range(peers):
        y = jnp.dot(
            resid, rotation[:, j * width : (j + 1) * width], preferred_element_type=F32
        ).astype(BF16)
        for c in range(resid.shape[0] // group):
            out[c * peers + j] = y[c * group : (c + 1) * group]


def quantize_kernel(parts, codes, scales):
    total = parts[0].astype(F32)
    for s in range(1, parts.shape[0]):
        total = total + parts[s].astype(F32)
    group, width = total.shape
    lane = lax.broadcasted_iota(jnp.int32, (group, LANES), 1)
    table = jnp.zeros((group, LANES), F32)
    for t in range(width // LANES):
        x = total[:, t * LANES : (t + 1) * LANES]
        size = jnp.abs(x)
        spread = jnp.zeros((group, LANES), F32)
        for b in range(LANES // BLOCK):
            inside = (lane >= b * BLOCK) & (lane < (b + 1) * BLOCK)
            top = jnp.max(jnp.where(inside, size, 0.0), axis=1, keepdims=True) + 1e-06
            spread = jnp.where(inside, top, spread)
            table = jnp.where(lane == t * (LANES // BLOCK) + b, top, table)
        codes[:, t * LANES : (t + 1) * LANES] = (x / spread).astype(BF16)
    scales[...] = table.T[: scales.shape[0]].astype(BF16)


def pool_call(lengths, list_ids, hidden, list_slot, gain, head, *, owners, peers, lists_own):
    passes, length, width = hidden.shape
    assert passes < SUB and length % STEP == 0
    group = list_ids.shape[0]
    capacity = max(2, 2 * group // owners)
    per = width // LANES // owners
    steps = length // STEP
    padded = -(-group // SUB) * SUB
    vmem = pl.BlockSpec(memory_space=pltpu.VMEM)
    hbm = pl.BlockSpec(memory_space=pl.ANY)
    return pl.pallas_call(
        functools.partial(
            pool_kernel, owners=owners, peers=peers, lists_own=lists_own, capacity=capacity
        ),
        out_shape=(
            pltpu.VMEM((owners * peers, per * SUB, LANES), BF16),
            pltpu.VMEM(head.shape, BF16),
        ),
        in_specs=[hbm] * 6,
        out_specs=(vmem, vmem),
        scratch_shapes=[
            pltpu.VMEM((passes * steps, STEP, width), BF16),
            pltpu.VMEM((2, STEP, LANES), F32),
            pltpu.VMEM((passes, SUB, width), F32),
            pltpu.VMEM((padded, LANES), jnp.int32),
            pltpu.VMEM((width // LANES, LANES), BF16),
            pltpu.SMEM((passes,), jnp.int32),
            pltpu.SMEM((group,), jnp.int32),
            pltpu.SMEM((passes * steps,), jnp.int32),
            pltpu.SemaphoreType.DMA((passes * steps,)),
            pltpu.SemaphoreType.DMA,
            pltpu.SemaphoreType.DMA((4,)),
        ],
        compiler_params=pltpu.CompilerParams(vmem_limit_bytes=hidden.size * 2 + 6 * 2**20),
        name="pool",
    )(
        far(lengths), far(list_ids), far(hidden), far(list_slot.reshape(-1, LANES)),
        far(gain.reshape(-1, LANES)), far(head),
    )


def per_device(hidden, lengths, list_ids, gain, head, list_slot, centroids, rotation):
    passes, length, width = hidden.shape
    owners = lax.axis_size("chip") * lax.axis_size("core")
    peers = lax.axis_size("mp")
    group = list_ids.shape[0]
    lists_own = centroids.shape[0]
    capacity = max(2, 2 * group // owners)
    cols = head.shape[1]
    lead = -(-owners // SUB) * SUB
    vmem = pl.BlockSpec(memory_space=pltpu.VMEM)
    hbm = pl.BlockSpec(memory_space=pl.ANY)
    blocks, head = pool_call(
        lengths, list_ids, hidden, list_slot, gain, head,
        owners=owners, peers=peers, lists_own=lists_own,
    )
    got = lax.all_to_all(blocks, ("chip", "core", "mp"), 0, 0, tiled=True)
    half = owners // CORES * group
    own, other = pl.pallas_call(
        functools.partial(
            project_kernel, owners=owners, peers=peers, passes=passes, capacity=capacity
        ),
        out_shape=(
            pltpu.VMEM((half, cols), F32),
            pltpu.VMEM((half, cols), BF16),
        ),
        in_specs=[vmem, vmem, hbm],
        out_specs=(vmem, vmem),
        scratch_shapes=[
            pltpu.VMEM((lead, LANES), jnp.int32),
            pltpu.SMEM((lead, LANES), jnp.int32),
            pltpu.VMEM((owners, peers * SUB, cols), F32),
            pltpu.VMEM((owners * capacity, SUB, cols), BF16),
            pltpu.VMEM((CORES, half, cols), F32),
            pltpu.SemaphoreType.DMA,
            pltpu.SemaphoreType.DMA((owners * capacity,)),
        ],
        compiler_params=pltpu.CompilerParams(vmem_limit_bytes=8 * 2**20),
        name="project",
    )(near(got), near(head), far(centroids))
    other = lax.ppermute(other, "core", [(c, (c + 1) % CORES) for c in range(CORES)])
    parts = pl.pallas_call(
        functools.partial(rotate_kernel, peers=peers),
        out_shape=pltpu.VMEM((owners // CORES * peers, group, cols), BF16),
        in_specs=[vmem, vmem, vmem],
        out_specs=vmem,
        compiler_params=pltpu.CompilerParams(vmem_limit_bytes=8 * 2**20),
        name="rotate",
    )(near(own), near(other), near(rotation))
    parts = lax.all_to_all(parts, ("chip", "mp"), 0, 0, tiled=True)
    codes, scales = pl.pallas_call(
        quantize_kernel,
        out_shape=(
            jax.ShapeDtypeStruct((group, cols), BF16),
            jax.ShapeDtypeStruct((cols // BLOCK, group), BF16),
        ),
        in_specs=[vmem],
        out_specs=(vmem, vmem),
        compiler_params=pltpu.CompilerParams(vmem_limit_bytes=8 * 2**20),
        name="quantize",
    )(near(parts))
    return codes, scales.T


def solution(mesh):
    dp, mp = mesh.shape["dp"], mesh.shape["mp"]
    split = Mesh(mesh.devices.reshape(dp // CORES, CORES, mp), ("chip", "core", "mp"))
    rows = ("chip", "core")
    in_specs = (
        P(("chip", "core", "mp"), None, None),
        P(("chip", "core", "mp")),
        P(rows),
        P(),
        P(rows, "mp"),
        P(),
        P(rows, None),
        P("mp", None),
    )
    out_specs = (P(rows, "mp"), P(rows, "mp"))
    return jax.shard_map(
        per_device, mesh=split, in_specs=in_specs, out_specs=out_specs, check_vma=False
    )
```

```python
import functools

import jax
import jax.numpy as jnp
from jax import lax
from jax.experimental import pallas as pl
from jax.experimental.pallas import tpu as pltpu
from jax.sharding import Mesh
from jax.sharding import PartitionSpec as P

BLOCK = 64
LANES = 128
SUB = 8
DIGIT = 256
CORES = 2
STEP = 64

F32 = jnp.float32
BF16 = jnp.bfloat16


def near(x):
    return pltpu.with_memory_space_constraint(x, pltpu.VMEM)


def far(x):
    return pltpu.with_memory_space_constraint(x, pltpu.HBM)


def pool_kernel(
    lens_hbm, ids_hbm, hidden, slots, gain_hbm, head, out, head_out, buf, weight, acc, slot_rows, gain,
    lens, ids, items, sems, slot_sem, side_sems, *, owners, peers, lists_own, capacity,
):
    passes, length, width = hidden.shape
    group = ids.shape[0]
    steps = length // STEP
    tiles = width // LANES
    per = tiles // owners
    rows = out.shape[1] // per

    def chunk_copy(p, c):
        return pltpu.make_async_copy(
            hidden.at[p, pl.ds(c * STEP, STEP)], buf.at[p * steps + c], sems.at[p * steps + c]
        )

    def slot_copy(g):
        return pltpu.make_async_copy(
            slots.at[pl.ds(lax.div(ids[g], LANES), 1)], slot_rows.at[pl.ds(g, 1)], slot_sem
        )

    side = [
        pltpu.make_async_copy(source, target, side_sems.at[n])
        for n, (source, target) in enumerate(
            ((lens_hbm, lens), (ids_hbm, ids), (gain_hbm, gain), (head, head_out))
        )
    ]
    side[0].start()
    side[1].start()
    for p in range(passes):
        chunk_copy(p, 0).start()
        items[p] = p * steps
    side[0].wait()
    count = jnp.int32(passes)
    for c in range(1, steps):
        for p in range(passes):
            needed = lens[p] > c * STEP

            @pl.when(needed)
            def _():
                chunk_copy(p, c).start()
                items[count] = p * steps + c

            count = count + needed.astype(jnp.int32)
    side[1].wait()
    for g in range(group):
        slot_copy(g).start()
    side[2].start()
    side[3].start()

    def zero(p, _):
        acc[p] = jnp.zeros((SUB, width), F32)
        return 0

    lax.fori_loop(0, passes, zero, 0)

    def arrive(k):
        item = items[k]
        pltpu.make_async_copy(
            hidden.at[0, pl.ds(0, STEP)], buf.at[item], sems.at[item]
        ).wait()

    def weigh(k):
        item = items[k]
        p = lax.div(item, steps)
        start = lax.rem(item, steps) * STEP
        size = lens[p]
        for s in range(0, STEP, SUB):
            x = buf[item, s : s + SUB, :]
            x = x * x
            x = (x[:, : width // 2] + x[:, width // 2 :]).astype(F32)
            total = x[:, :LANES]
            for t in range(LANES, width // 2, LANES):
                total = total + x[:, t : t + LANES]
            square = jnp.sum(total, axis=1, keepdims=True)
            token = lax.broadcasted_iota(jnp.int32, (SUB, 1), 0) + (start + s)
            value = jnp.where(token < size, lax.rsqrt(square * (1.0 / width) + 1e-05), 0.0)
            weight[lax.rem(k, 2), s : s + SUB, :] = jnp.broadcast_to(value, (SUB, 2 * LANES)).astype(BF16)

    def add(k):
        item = items[k]
        p = lax.div(item, steps)
        slot = lax.rem(k, 2)
        pair = 2 * LANES
        for t in range(0, width, pair):
            total = None
            for s in range(0, STEP, 2 * SUB):
                x = buf[item, s : s + SUB, t : t + pair] * weight[slot, s : s + SUB, :]
                e = s + SUB
                x = x + buf[item, e : e + SUB, t : t + pair] * weight[slot, e : e + SUB, :]
                x = x.astype(F32)
                total = x if total is None else total + x
            acc[p, :, t : t + pair] += total

    arrive(0)
    weigh(jnp.int32(0))

    def body(k, _):
        arrive(k + 1)
        add(k)
        weigh(k + 1)
        return 0

    lax.fori_loop(0, count - 1, body, 0)
    for n in (2, 3):
        side[n].wait()
    pltpu.make_async_copy(
        slots.at[pl.ds(0, group)], slot_rows.at[pl.ds(0, group)], slot_sem
    ).wait()
    add(count - 1)

    shape = (-(-group // SUB) * SUB, LANES)
    sub = lax.broadcasted_iota(jnp.int32, (SUB, LANES), 0)
    blocks = []
    for start in range(0, shape[0], SUB):
        block = jnp.zeros((SUB, LANES), jnp.int32)
        for g in range(start, min(start + SUB, group)):
            block = jnp.where(sub == g - start, lax.rem(ids[g], LANES), block)
        blocks.append(block)
    column = jnp.concatenate(blocks, axis=0)
    line = lax.broadcasted_iota(jnp.int32, shape, 0)
    lane = lax.broadcasted_iota(jnp.int32, shape, 1)
    picked = jnp.where((lane == column) & (line < group), slot_rows[...], 0).astype(F32)
    slot = jnp.sum(picked, axis=1, keepdims=True).astype(jnp.int32)
    slot = jnp.broadcast_to(slot, shape)
    owner = lax.div(slot, lists_own)
    local = slot - owner * lists_own
    high = lax.div(local, DIGIT)
    low = local - high * DIGIT
    owner_line = jnp.sum(jnp.where(line == lane, owner.astype(F32), 0.0), axis=0, keepdims=True)
    earlier = (jnp.broadcast_to(owner_line, shape) == owner.astype(F32)) & (lane < line)
    rank = jnp.sum(jnp.where(earlier, 1.0, 0.0), axis=1, keepdims=True).astype(jnp.int32)
    rank = jnp.broadcast_to(rank, shape)
    peer = jnp.zeros(shape, jnp.int32)
    for j in range(1, peers):
        peer = peer + (line >= j * passes).astype(jnp.int32)
    place = line + peer * (rows - passes) + 1
    entry = jnp.where(lane == rank, high, 0)
    entry = jnp.where(lane == rank + capacity, low, entry)
    entry = jnp.where(lane == rank + 2 * capacity, place, entry)
    entry = jnp.where((rank < capacity) & (line < group), entry, 0).astype(F32)

    inverse = jnp.zeros((SUB, LANES), F32)
    for p in range(passes):
        inverse = jnp.where(sub == p, lens[p].astype(F32), inverse)
    inverse = jnp.where(sub < passes, 1.0 / jnp.maximum(inverse, 1.0), 0.0)
    for o in range(owners):
        info = jnp.sum(jnp.where(owner == o, entry, 0.0), axis=0, keepdims=True)
        for q in range(per):
            t = o * per + q
            cols = slice(t * LANES, (t + 1) * LANES)
            parts = [acc[p, :, cols] if p < passes else None for p in range(SUB)]
            bit = SUB // 2
            while bit:
                merged = []
                for n in range(bit):
                    a, b = parts[n], parts[n + bit]
                    if a is None:
                        merged.append(None)
                    elif b is None:
                        merged.append(jnp.where((sub & bit) == 0, a + pltpu.roll(a, SUB - bit, 0), 0.0))
                    else:
                        first = jnp.where((sub & bit) == 0, a, b)
                        second = jnp.where((sub & bit) == 0, b, a)
                        if bit * 2 == SUB:
                            merged.append(first + pltpu.roll(second, bit, 0))
                        else:
                            up = pltpu.roll(second, SUB - bit, 0)
                            down = pltpu.roll(second, bit, 0)
                            merged.append(first + jnp.where((sub & bit) == 0, up, down))
                parts = merged
                bit //= 2
            tile = parts[0] * gain[t : t + 1].astype(F32) * inverse
            if q == 0:
                tile = jnp.where(sub == passes, jnp.broadcast_to(info, (SUB, LANES)), tile)
            tile = tile.astype(BF16)
            for j in range(peers):
                out[o * peers + j, q * rows : (q + 1) * rows, :] = tile


def project_kernel(
    got, head, cents, own, other, info_v, info_s, acc, rows_in, packed, info_sem, row_sem,
    *, owners, peers, passes, capacity,
):
    rows = SUB
    width = head.shape[1]
    lists_own = cents.shape[0]
    per = got.shape[1] // rows
    wide = peers * rows
    col = pl.multiple_of(lax.axis_index("mp") * width, LANES)
    lines = [got[o * peers, 0:rows, :].astype(F32)[passes : passes + 1] for o in range(owners)]
    lines += [jnp.zeros((1, LANES), F32)] * (info_v.shape[1] - owners)
    info = jnp.concatenate(lines, axis=0).astype(jnp.int32)
    row = info * DIGIT + pltpu.roll(info, LANES - capacity, 1)
    row = jnp.clip(row, 0, lists_own - 1)
    place = pltpu.roll(info, LANES - 2 * capacity, 1)
    first = lax.div(row, SUB)
    base = lax.broadcasted_iota(jnp.int32, info.shape, 0) * wide - 1
    info_v[0] = first
    info_v[1] = row - first * SUB
    info_v[2] = jnp.where((place > 0) & (place <= wide), place + base, -1)
    info_copy = pltpu.make_async_copy(info_v, info_s, info_sem)
    info_copy.start()
    info_copy.wait()
    entries = [(o, k) for o in range(owners) for k in range(capacity)]
    for n, (o, k) in enumerate(entries):
        pltpu.make_async_copy(
            cents.at[pl.ds(pl.multiple_of(info_s[0, o, k] * SUB, SUB), SUB), pl.ds(col, width)],
            rows_in.at[n],
            row_sem,
        ).start()
    x = jnp.concatenate(
        [
            got[:, q * rows : (q + 1) * rows, :].reshape(owners * peers * rows, LANES)
            for q in range(per)
        ],
        axis=1,
    )
    total = jnp.dot(x, head[...], preferred_element_type=F32)
    lane = lax.broadcasted_iota(jnp.int32, (1, LANES), 1)
    spots = lax.broadcasted_iota(jnp.int32, (owners * wide, LANES), 0)
    share = LANES // SUB
    chosen = []
    for start in range(0, len(entries), share):
        target = jnp.full((1, LANES), -1, jnp.int32)
        for m, (o, k) in enumerate(entries[start : start + share]):
            target = jnp.where(lane == m * SUB + info_s[1, o, k], info_s[2, o, k], target)
        chosen.append(jnp.where(spots == target, 1.0, 0.0).astype(BF16))
    depth = len(entries) * SUB
    chosen = jnp.concatenate(chosen, axis=1)[:, :depth]
    pltpu.make_async_copy(rows_in, rows_in, row_sem).wait()
    total = total - jnp.dot(
        chosen, rows_in[...].reshape(depth, width), preferred_element_type=F32
    )
    acc[...] = total.reshape(owners, wide, width)
    core = lax.axis_index("core")
    group = peers * passes
    for side in range(CORES):
        for c in range(owners // CORES):
            x = acc[c * CORES + (core if side == 0 else 1 - core)]
            for j in range(peers):
                at = c * group + j * passes
                packed[side, at : at + passes, :] = x[j * rows : j * rows + passes]
    own[...] = packed[0]
    other[...] = packed[1].astype(BF16)


def rotate_kernel(own, other, rotation, out, *, peers):
    group = out.shape[1]
    width = out.shape[2]
    resid = (own[...] + other[...].astype(F32)).astype(BF16)
    for j in range(peers):
        y = jnp.dot(
            resid, rotation[:, j * width : (j + 1) * width], preferred_element_type=F32
        ).astype(BF16)
        for c in range(resid.shape[0] // group):
            out[c * peers + j] = y[c * group : (c + 1) * group]


def quantize_kernel(parts, codes, scales):
    total = parts[0].astype(F32)
    for s in range(1, parts.shape[0]):
        total = total + parts[s].astype(F32)
    group, width = total.shape
    lane = lax.broadcasted_iota(jnp.int32, (group, LANES), 1)
    table = jnp.zeros((group, LANES), F32)
    for t in range(width // LANES):
        x = total[:, t * LANES : (t + 1) * LANES]
        size = jnp.abs(x)
        spread = jnp.zeros((group, LANES), F32)
        for b in range(LANES // BLOCK):
            inside = (lane >= b * BLOCK) & (lane < (b + 1) * BLOCK)
            top = jnp.max(jnp.where(inside, size, 0.0), axis=1, keepdims=True) + 1e-06
            spread = jnp.where(inside, top, spread)
            table = jnp.where(lane == t * (LANES // BLOCK) + b, top, table)
        codes[:, t * LANES : (t + 1) * LANES] = (x / spread).astype(BF16)
    scales[...] = table.T[: scales.shape[0]].astype(BF16)


def pool_call(lengths, list_ids, hidden, list_slot, gain, head, *, owners, peers, lists_own):
    passes, length, width = hidden.shape
    assert passes < SUB and length % STEP == 0
    group = list_ids.shape[0]
    capacity = max(2, 2 * group // owners)
    per = width // LANES // owners
    steps = length // STEP
    padded = -(-group // SUB) * SUB
    vmem = pl.BlockSpec(memory_space=pltpu.VMEM)
    hbm = pl.BlockSpec(memory_space=pl.ANY)
    return pl.pallas_call(
        functools.partial(
            pool_kernel, owners=owners, peers=peers, lists_own=lists_own, capacity=capacity
        ),
        out_shape=(
            pltpu.VMEM((owners * peers, per * SUB, LANES), BF16),
            pltpu.VMEM(head.shape, BF16),
        ),
        in_specs=[hbm] * 6,
        out_specs=(vmem, vmem),
        scratch_shapes=[
            pltpu.VMEM((passes * steps, STEP, width), BF16),
            pltpu.VMEM((2, STEP, 2 * LANES), BF16),
            pltpu.VMEM((passes, SUB, width), F32),
            pltpu.VMEM((padded, LANES), jnp.int32),
            pltpu.VMEM((width // LANES, LANES), BF16),
            pltpu.SMEM((passes,), jnp.int32),
            pltpu.SMEM((group,), jnp.int32),
            pltpu.SMEM((passes * steps,), jnp.int32),
            pltpu.SemaphoreType.DMA((passes * steps,)),
            pltpu.SemaphoreType.DMA,
            pltpu.SemaphoreType.DMA((4,)),
        ],
        compiler_params=pltpu.CompilerParams(vmem_limit_bytes=hidden.size * 2 + 6 * 2**20),
        name="pool",
    )(
        far(lengths), far(list_ids), far(hidden), far(list_slot.reshape(-1, LANES)),
        far(gain.reshape(-1, LANES)), far(head),
    )


def per_device(hidden, lengths, list_ids, gain, head, list_slot, centroids, rotation):
    passes, length, width = hidden.shape
    owners = lax.axis_size("chip") * lax.axis_size("core")
    peers = lax.axis_size("mp")
    group = list_ids.shape[0]
    lists_own = centroids.shape[0]
    capacity = max(2, 2 * group // owners)
    cols = head.shape[1]
    lead = -(-owners // SUB) * SUB
    vmem = pl.BlockSpec(memory_space=pltpu.VMEM)
    hbm = pl.BlockSpec(memory_space=pl.ANY)
    blocks, head = pool_call(
        lengths, list_ids, hidden, list_slot, gain, head,
        owners=owners, peers=peers, lists_own=lists_own,
    )
    got = lax.all_to_all(blocks, ("chip", "core", "mp"), 0, 0, tiled=True)
    half = owners // CORES * group
    own, other = pl.pallas_call(
        functools.partial(
            project_kernel, owners=owners, peers=peers, passes=passes, capacity=capacity
        ),
        out_shape=(
            pltpu.VMEM((half, cols), F32),
            pltpu.VMEM((half, cols), BF16),
        ),
        in_specs=[vmem, vmem, hbm],
        out_specs=(vmem, vmem),
        scratch_shapes=[
            pltpu.VMEM((3, lead, LANES), jnp.int32),
            pltpu.SMEM((3, lead, LANES), jnp.int32),
            pltpu.VMEM((owners, peers * SUB, cols), F32),
            pltpu.VMEM((owners * capacity, SUB, cols), BF16),
            pltpu.VMEM((CORES, half, cols), F32),
            pltpu.SemaphoreType.DMA,
            pltpu.SemaphoreType.DMA,
        ],
        compiler_params=pltpu.CompilerParams(vmem_limit_bytes=8 * 2**20),
        name="project",
    )(near(got), near(head), far(centroids))
    other = lax.ppermute(other, "core", [(c, (c + 1) % CORES) for c in range(CORES)])
    parts = pl.pallas_call(
        functools.partial(rotate_kernel, peers=peers),
        out_shape=pltpu.VMEM((owners // CORES * peers, group, cols), BF16),
        in_specs=[vmem, vmem, vmem],
        out_specs=vmem,
        compiler_params=pltpu.CompilerParams(vmem_limit_bytes=8 * 2**20),
        name="rotate",
    )(near(own), near(other), near(rotation))
    parts = lax.all_to_all(parts, ("chip", "mp"), 0, 0, tiled=True)
    codes, scales = pl.pallas_call(
        quantize_kernel,
        out_shape=(
            jax.ShapeDtypeStruct((group, cols), BF16),
            jax.ShapeDtypeStruct((cols // BLOCK, group), BF16),
        ),
        in_specs=[vmem],
        out_specs=(vmem, vmem),
        compiler_params=pltpu.CompilerParams(vmem_limit_bytes=8 * 2**20),
        name="quantize",
    )(near(parts))
    return codes, scales.T


def solution(mesh):
    dp, mp = mesh.shape["dp"], mesh.shape["mp"]
    split = Mesh(mesh.devices.reshape(dp // CORES, CORES, mp), ("chip", "core", "mp"))
    rows = ("chip", "core")
    in_specs = (
        P(("chip", "core", "mp"), None, None),
        P(("chip", "core", "mp")),
        P(rows),
        P(),
        P(rows, "mp"),
        P(),
        P(rows, None),
        P("mp", None),
    )
    out_specs = (P(rows, "mp"), P(rows, "mp"))
    return jax.shard_map(
        per_device, mesh=split, in_specs=in_specs, out_specs=out_specs, check_vma=False
    )
```

```python
import functools

import jax
import jax.numpy as jnp
from jax import lax
from jax.experimental import pallas as pl
from jax.experimental.pallas import tpu as pltpu
from jax.sharding import Mesh
from jax.sharding import PartitionSpec as P

BLOCK = 64
LANES = 128
SUB = 8
DIGIT = 256
CORES = 2
STEP = 64

F32 = jnp.float32
BF16 = jnp.bfloat16


def near(x):
    return pltpu.with_memory_space_constraint(x, pltpu.VMEM)


def far(x):
    return pltpu.with_memory_space_constraint(x, pltpu.HBM)


def pool_kernel(
    lens_hbm, ids_hbm, hidden, slots, gain_hbm, head, out, head_out, buf, weight, acc, slot_rows, gain,
    lens, ids, items, sems, slot_sem, side_sems, *, owners, peers, lists_own, capacity,
):
    passes, length, width = hidden.shape
    group = ids.shape[0]
    steps = length // STEP
    tiles = width // LANES
    per = tiles // owners
    rows = out.shape[1] // per

    def chunk_copy(p, c):
        return pltpu.make_async_copy(
            hidden.at[p, pl.ds(c * STEP, STEP)], buf.at[p * steps + c], sems.at[p * steps + c]
        )

    def slot_copy(g):
        return pltpu.make_async_copy(
            slots.at[pl.ds(lax.div(ids[g], LANES), 1)], slot_rows.at[pl.ds(g, 1)], slot_sem
        )

    side = [
        pltpu.make_async_copy(source, target, side_sems.at[n])
        for n, (source, target) in enumerate(
            ((lens_hbm, lens), (ids_hbm, ids), (gain_hbm, gain), (head, head_out))
        )
    ]
    side[0].start()
    side[1].start()
    for p in range(passes):
        chunk_copy(p, 0).start()
        items[p] = p * steps
    side[0].wait()
    count = jnp.int32(passes)
    for c in range(1, steps):
        for p in range(passes):
            needed = lens[p] > c * STEP

            @pl.when(needed)
            def _():
                chunk_copy(p, c).start()
                items[count] = p * steps + c

            count = count + needed.astype(jnp.int32)
    side[1].wait()
    for g in range(group):
        slot_copy(g).start()
    side[2].start()
    side[3].start()

    def zero(p, _):
        acc[p] = jnp.zeros((SUB, width), F32)
        return 0

    lax.fori_loop(0, passes, zero, 0)

    def arrive(k):
        item = items[k]
        pltpu.make_async_copy(
            hidden.at[0, pl.ds(0, STEP)], buf.at[item], sems.at[item]
        ).wait()

    def weigh(k):
        item = items[k]
        p = lax.div(item, steps)
        start = lax.rem(item, steps) * STEP
        size = lens[p]
        for s in range(0, STEP, SUB):
            x = buf[item, s : s + SUB, :]
            x = x * x
            x = (x[:, : width // 2] + x[:, width // 2 :]).astype(F32)
            total = x[:, :LANES]
            for t in range(LANES, width // 2, LANES):
                total = total + x[:, t : t + LANES]
            square = jnp.sum(total, axis=1, keepdims=True)
            token = lax.broadcasted_iota(jnp.int32, (SUB, 1), 0) + (start + s)
            value = jnp.where(token < size, lax.rsqrt(square * (1.0 / width) + 1e-05), 0.0)
            weight[lax.rem(k, 2), s : s + SUB, :] = jnp.broadcast_to(value, (SUB, 2 * LANES)).astype(BF16)

    def add(k):
        item = items[k]
        p = lax.div(item, steps)
        slot = lax.rem(k, 2)
        pair = 2 * LANES
        for t in range(0, width, pair):
            total = None
            for s in range(0, STEP, 2 * SUB):
                x = buf[item, s : s + SUB, t : t + pair] * weight[slot, s : s + SUB, :]
                e = s + SUB
                x = x + buf[item, e : e + SUB, t : t + pair] * weight[slot, e : e + SUB, :]
                x = x.astype(F32)
                total = x if total is None else total + x
            acc[p, :, t : t + pair] += total

    arrive(0)
    weigh(jnp.int32(0))

    def body(k, _):
        arrive(k + 1)
        add(k)
        weigh(k + 1)
        return 0

    lax.fori_loop(0, count - 1, body, 0)
    for n in (2, 3):
        side[n].wait()
    pltpu.make_async_copy(
        slots.at[pl.ds(0, group)], slot_rows.at[pl.ds(0, group)], slot_sem
    ).wait()
    add(count - 1)

    shape = (-(-group // SUB) * SUB, LANES)
    sub = lax.broadcasted_iota(jnp.int32, (SUB, LANES), 0)
    blocks = []
    for start in range(0, shape[0], SUB):
        block = jnp.zeros((SUB, LANES), jnp.int32)
        for g in range(start, min(start + SUB, group)):
            block = jnp.where(sub == g - start, lax.rem(ids[g], LANES), block)
        blocks.append(block)
    column = jnp.concatenate(blocks, axis=0)
    line = lax.broadcasted_iota(jnp.int32, shape, 0)
    lane = lax.broadcasted_iota(jnp.int32, shape, 1)
    picked = jnp.where((lane == column) & (line < group), slot_rows[...], 0).astype(F32)
    slot = jnp.sum(picked, axis=1, keepdims=True).astype(jnp.int32)
    slot = jnp.broadcast_to(slot, shape)
    owner = lax.div(slot, lists_own)
    local = slot - owner * lists_own
    high = lax.div(local, DIGIT)
    low = local - high * DIGIT
    owner_line = jnp.sum(jnp.where(line == lane, owner.astype(F32), 0.0), axis=0, keepdims=True)
    earlier = (jnp.broadcast_to(owner_line, shape) == owner.astype(F32)) & (lane < line)
    rank = jnp.sum(jnp.where(earlier, 1.0, 0.0), axis=1, keepdims=True).astype(jnp.int32)
    rank = jnp.broadcast_to(rank, shape)
    peer = jnp.zeros(shape, jnp.int32)
    for j in range(1, peers):
        peer = peer + (line >= j * passes).astype(jnp.int32)
    place = line + peer * (rows - passes) + 1
    entry = jnp.where(lane == rank, high, 0)
    entry = jnp.where(lane == rank + capacity, low, entry)
    entry = jnp.where(lane == rank + 2 * capacity, place, entry)
    entry = jnp.where((rank < capacity) & (line < group), entry, 0).astype(F32)

    inverse = jnp.zeros((SUB, LANES), F32)
    for p in range(passes):
        inverse = jnp.where(sub == p, lens[p].astype(F32), inverse)
    inverse = jnp.where(sub < passes, 1.0 / jnp.maximum(inverse, 1.0), 0.0)
    for o in range(owners):
        info = jnp.sum(jnp.where(owner == o, entry, 0.0), axis=0, keepdims=True)
        for q in range(per):
            t = o * per + q
            cols = slice(t * LANES, (t + 1) * LANES)
            parts = [acc[p, :, cols] if p < passes else None for p in range(SUB)]
            bit = SUB // 2
            while bit:
                merged = []
                for n in range(bit):
                    a, b = parts[n], parts[n + bit]
                    if a is None:
                        merged.append(None)
                    elif b is None:
                        merged.append(jnp.where((sub & bit) == 0, a + pltpu.roll(a, SUB - bit, 0), 0.0))
                    else:
                        first = jnp.where((sub & bit) == 0, a, b)
                        second = jnp.where((sub & bit) == 0, b, a)
                        if bit * 2 == SUB:
                            merged.append(first + pltpu.roll(second, bit, 0))
                        else:
                            up = pltpu.roll(second, SUB - bit, 0)
                            down = pltpu.roll(second, bit, 0)
                            merged.append(first + jnp.where((sub & bit) == 0, up, down))
                parts = merged
                bit //= 2
            tile = parts[0] * gain[t : t + 1].astype(F32) * inverse
            if q == 0:
                tile = jnp.where(sub == passes, jnp.broadcast_to(info, (SUB, LANES)), tile)
            tile = tile.astype(BF16)
            for j in range(peers):
                out[o * peers + j, q * rows : (q + 1) * rows, :] = tile


def project_kernel(
    got, head, cents, own, other, info_v, info_s, rows_in, info_sem, row_sem,
    *, owners, peers, passes, capacity,
):
    width = head.shape[1]
    lists_own = cents.shape[0]
    per = got.shape[1] // SUB
    wide = peers * SUB
    group = peers * passes
    half = owners // CORES * group
    core = lax.axis_index("core")
    col = pl.multiple_of(lax.axis_index("mp") * width, LANES)

    def final_row(o, at):
        peer = lax.div(at, SUB)
        chip = lax.div(o, CORES)
        away = jnp.where(o - chip * CORES == core, 0, half)
        return away + chip * group + peer * passes + (at - peer * SUB)

    lines = [got[o * peers, 0:SUB, :].astype(F32)[passes : passes + 1] for o in range(owners)]
    lines += [jnp.zeros((1, LANES), F32)] * (info_v.shape[1] - owners)
    info = jnp.concatenate(lines, axis=0).astype(jnp.int32)
    row = info * DIGIT + pltpu.roll(info, LANES - capacity, 1)
    row = jnp.clip(row, 0, lists_own - 1)
    place = pltpu.roll(info, LANES - 2 * capacity, 1)
    first = lax.div(row, SUB)
    real = (place > 0) & (place <= wide)
    info_v[0] = first
    info_v[1] = row - first * SUB
    info_v[2] = jnp.where(
        real,
        final_row(lax.broadcasted_iota(jnp.int32, info.shape, 0), jnp.where(real, place - 1, 0)),
        -1,
    )
    info_copy = pltpu.make_async_copy(info_v, info_s, info_sem)
    info_copy.start()
    info_copy.wait()
    entries = [(o, k) for o in range(owners) for k in range(capacity)]
    for n, (o, k) in enumerate(entries):
        pltpu.make_async_copy(
            cents.at[pl.ds(pl.multiple_of(info_s[0, o, k] * SUB, SUB), SUB), pl.ds(col, width)],
            rows_in.at[n],
            row_sem,
        ).start()
    lane = lax.broadcasted_iota(jnp.int32, (1, LANES), 1)
    spots = lax.broadcasted_iota(jnp.int32, (CORES * half, LANES), 0)
    share = LANES // SUB
    chosen = []
    for start in range(0, len(entries), share):
        target = jnp.full((1, LANES), -1, jnp.int32)
        for m, (o, k) in enumerate(entries[start : start + share]):
            target = jnp.where(lane == m * SUB + info_s[1, o, k], info_s[2, o, k], target)
        chosen.append(jnp.where(spots == target, -1.0, 0.0).astype(BF16))
    depth = len(entries) * SUB
    chosen = jnp.concatenate(chosen, axis=1)[:, :depth]
    sources = owners * wide
    order = []
    for start in range(0, sources, LANES):
        at = lane + start
        o = lax.div(at, wide)
        at = at - o * wide
        target = jnp.where(at - lax.div(at, SUB) * SUB < passes, final_row(o, at), -1)
        order.append(jnp.where(spots == target, 1.0, 0.0).astype(BF16))
    x = jnp.concatenate(
        [
            got[:, q * SUB : (q + 1) * SUB, :].reshape(sources, LANES)
            for q in range(per)
        ],
        axis=1,
    )
    x = jnp.dot(jnp.concatenate(order, axis=1), x, preferred_element_type=F32).astype(BF16)
    total = jnp.dot(x, head[...], preferred_element_type=F32)
    pltpu.make_async_copy(rows_in, rows_in, row_sem).wait()
    total = total + jnp.dot(
        chosen, rows_in[...].reshape(depth, width), preferred_element_type=F32
    )
    own[...] = total[:half]
    other[...] = total[half:].astype(BF16)


def rotate_kernel(own, other, rotation, out, *, peers):
    group = out.shape[1]
    width = out.shape[2]
    resid = (own[...] + other[...].astype(F32)).astype(BF16)
    for j in range(peers):
        y = jnp.dot(
            resid, rotation[:, j * width : (j + 1) * width], preferred_element_type=F32
        ).astype(BF16)
        for c in range(resid.shape[0] // group):
            out[c * peers + j] = y[c * group : (c + 1) * group]


def quantize_kernel(parts, codes, scales):
    total = parts[0].astype(F32)
    for s in range(1, parts.shape[0]):
        total = total + parts[s].astype(F32)
    group, width = total.shape
    lane = lax.broadcasted_iota(jnp.int32, (group, LANES), 1)
    table = jnp.zeros((group, LANES), F32)
    for t in range(width // LANES):
        x = total[:, t * LANES : (t + 1) * LANES]
        size = jnp.abs(x)
        spread = jnp.zeros((group, LANES), F32)
        for b in range(LANES // BLOCK):
            inside = (lane >= b * BLOCK) & (lane < (b + 1) * BLOCK)
            top = jnp.max(jnp.where(inside, size, 0.0), axis=1, keepdims=True) + 1e-06
            spread = jnp.where(inside, top, spread)
            table = jnp.where(lane == t * (LANES // BLOCK) + b, top, table)
        codes[:, t * LANES : (t + 1) * LANES] = (x / spread).astype(BF16)
    scales[...] = table.T[: scales.shape[0]].astype(BF16)


def pool_call(lengths, list_ids, hidden, list_slot, gain, head, *, owners, peers, lists_own):
    passes, length, width = hidden.shape
    assert passes < SUB and length % STEP == 0
    group = list_ids.shape[0]
    capacity = max(2, 2 * group // owners)
    per = width // LANES // owners
    steps = length // STEP
    padded = -(-group // SUB) * SUB
    vmem = pl.BlockSpec(memory_space=pltpu.VMEM)
    hbm = pl.BlockSpec(memory_space=pl.ANY)
    return pl.pallas_call(
        functools.partial(
            pool_kernel, owners=owners, peers=peers, lists_own=lists_own, capacity=capacity
        ),
        out_shape=(
            pltpu.VMEM((owners * peers, per * SUB, LANES), BF16),
            pltpu.VMEM(head.shape, BF16),
        ),
        in_specs=[hbm] * 6,
        out_specs=(vmem, vmem),
        scratch_shapes=[
            pltpu.VMEM((passes * steps, STEP, width), BF16),
            pltpu.VMEM((2, STEP, 2 * LANES), BF16),
            pltpu.VMEM((passes, SUB, width), F32),
            pltpu.VMEM((padded, LANES), jnp.int32),
            pltpu.VMEM((width // LANES, LANES), BF16),
            pltpu.SMEM((passes,), jnp.int32),
            pltpu.SMEM((group,), jnp.int32),
            pltpu.SMEM((passes * steps,), jnp.int32),
            pltpu.SemaphoreType.DMA((passes * steps,)),
            pltpu.SemaphoreType.DMA,
            pltpu.SemaphoreType.DMA((4,)),
        ],
        compiler_params=pltpu.CompilerParams(vmem_limit_bytes=hidden.size * 2 + 6 * 2**20),
        name="pool",
    )(
        far(lengths), far(list_ids), far(hidden), far(list_slot.reshape(-1, LANES)),
        far(gain.reshape(-1, LANES)), far(head),
    )


def per_device(hidden, lengths, list_ids, gain, head, list_slot, centroids, rotation):
    passes, length, width = hidden.shape
    owners = lax.axis_size("chip") * lax.axis_size("core")
    peers = lax.axis_size("mp")
    group = list_ids.shape[0]
    lists_own = centroids.shape[0]
    capacity = max(2, 2 * group // owners)
    cols = head.shape[1]
    lead = -(-owners // SUB) * SUB
    vmem = pl.BlockSpec(memory_space=pltpu.VMEM)
    hbm = pl.BlockSpec(memory_space=pl.ANY)
    blocks, head = pool_call(
        lengths, list_ids, hidden, list_slot, gain, head,
        owners=owners, peers=peers, lists_own=lists_own,
    )
    got = lax.all_to_all(blocks, ("chip", "core", "mp"), 0, 0, tiled=True)
    half = owners // CORES * group
    own, other = pl.pallas_call(
        functools.partial(
            project_kernel, owners=owners, peers=peers, passes=passes, capacity=capacity
        ),
        out_shape=(
            pltpu.VMEM((half, cols), F32),
            pltpu.VMEM((half, cols), BF16),
        ),
        in_specs=[vmem, vmem, hbm],
        out_specs=(vmem, vmem),
        scratch_shapes=[
            pltpu.VMEM((3, lead, LANES), jnp.int32),
            pltpu.SMEM((3, lead, LANES), jnp.int32),
            pltpu.VMEM((owners * capacity, SUB, cols), BF16),
            pltpu.SemaphoreType.DMA,
            pltpu.SemaphoreType.DMA,
        ],
        compiler_params=pltpu.CompilerParams(vmem_limit_bytes=8 * 2**20),
        name="project",
    )(near(got), near(head), far(centroids))
    other = lax.ppermute(other, "core", [(c, (c + 1) % CORES) for c in range(CORES)])
    parts = pl.pallas_call(
        functools.partial(rotate_kernel, peers=peers),
        out_shape=pltpu.VMEM((owners // CORES * peers, group, cols), BF16),
        in_specs=[vmem, vmem, vmem],
        out_specs=vmem,
        compiler_params=pltpu.CompilerParams(vmem_limit_bytes=8 * 2**20),
        name="rotate",
    )(near(own), near(other), near(rotation))
    parts = lax.all_to_all(parts, ("chip", "mp"), 0, 0, tiled=True)
    codes, scales = pl.pallas_call(
        quantize_kernel,
        out_shape=(
            jax.ShapeDtypeStruct((group, cols), BF16),
            jax.ShapeDtypeStruct((cols // BLOCK, group), BF16),
        ),
        in_specs=[vmem],
        out_specs=(vmem, vmem),
        compiler_params=pltpu.CompilerParams(vmem_limit_bytes=8 * 2**20),
        name="quantize",
    )(near(parts))
    return codes, scales.T


def solution(mesh):
    dp, mp = mesh.shape["dp"], mesh.shape["mp"]
    split = Mesh(mesh.devices.reshape(dp // CORES, CORES, mp), ("chip", "core", "mp"))
    rows = ("chip", "core")
    in_specs = (
        P(("chip", "core", "mp"), None, None),
        P(("chip", "core", "mp")),
        P(rows),
        P(),
        P(rows, "mp"),
        P(),
        P(rows, None),
        P("mp", None),
    )
    out_specs = (P(rows, "mp"), P(rows, "mp"))
    return jax.shard_map(
        per_device, mesh=split, in_specs=in_specs, out_specs=out_specs, check_vma=False
    )
```

```python
import functools

import jax
import jax.numpy as jnp
from jax import lax
from jax.experimental import pallas as pl
from jax.experimental.pallas import tpu as pltpu
from jax.sharding import Mesh
from jax.sharding import PartitionSpec as P

BLOCK = 64
LANES = 128
SUB = 8
DIGIT = 256
CORES = 2
STEP = 64

F32 = jnp.float32
BF16 = jnp.bfloat16


def near(x):
    return pltpu.with_memory_space_constraint(x, pltpu.VMEM)


def far(x):
    return pltpu.with_memory_space_constraint(x, pltpu.HBM)


def pool_kernel(
    lens_hbm, ids_hbm, hidden, slots, gain_hbm, head, out, head_out, buf, weight, acc, slot_rows, gain,
    lens, ids, items, sems, slot_sem, side_sems, *, owners, peers, lists_own, capacity,
):
    passes, length, width = hidden.shape
    group = ids.shape[0]
    steps = length // STEP
    tiles = width // LANES
    per = tiles // owners
    pairs = -(-passes // 2)

    def chunk_copy(p, c):
        return pltpu.make_async_copy(
            hidden.at[p, pl.ds(c * STEP, STEP)], buf.at[p * steps + c], sems.at[p * steps + c]
        )

    def slot_copy(g):
        return pltpu.make_async_copy(
            slots.at[pl.ds(lax.div(ids[g], LANES), 1)], slot_rows.at[pl.ds(g, 1)], slot_sem
        )

    side = [
        pltpu.make_async_copy(source, target, side_sems.at[n])
        for n, (source, target) in enumerate(
            ((lens_hbm, lens), (ids_hbm, ids), (gain_hbm, gain), (head, head_out))
        )
    ]
    side[0].start()
    side[1].start()
    for p in range(passes):
        chunk_copy(p, 0).start()
        items[p] = p * steps
    side[0].wait()
    count = jnp.int32(passes)
    for c in range(1, steps):
        for p in range(passes):
            needed = lens[p] > c * STEP

            @pl.when(needed)
            def _():
                chunk_copy(p, c).start()
                items[count] = p * steps + c

            count = count + needed.astype(jnp.int32)
    side[1].wait()
    for g in range(group):
        slot_copy(g).start()
    side[2].start()
    side[3].start()

    def zero(p, _):
        acc[p] = jnp.zeros((SUB, width), F32)
        return 0

    lax.fori_loop(0, passes, zero, 0)

    def arrive(k):
        item = items[k]
        pltpu.make_async_copy(
            hidden.at[0, pl.ds(0, STEP)], buf.at[item], sems.at[item]
        ).wait()

    def weigh(k):
        item = items[k]
        p = lax.div(item, steps)
        start = lax.rem(item, steps) * STEP
        size = lens[p]
        for s in range(0, STEP, SUB):
            x = buf[item, s : s + SUB, :]
            x = x * x
            x = (x[:, : width // 2] + x[:, width // 2 :]).astype(F32)
            total = x[:, :LANES]
            for t in range(LANES, width // 2, LANES):
                total = total + x[:, t : t + LANES]
            square = jnp.sum(total, axis=1, keepdims=True)
            token = lax.broadcasted_iota(jnp.int32, (SUB, 1), 0) + (start + s)
            value = jnp.where(token < size, lax.rsqrt(square * (1.0 / width) + 1e-05), 0.0)
            weight[lax.rem(k, 2), s : s + SUB, :] = jnp.broadcast_to(value, (SUB, 2 * LANES)).astype(BF16)

    def add(k):
        item = items[k]
        p = lax.div(item, steps)
        slot = lax.rem(k, 2)
        pair = 2 * LANES
        for t in range(0, width, pair):
            total = None
            for s in range(0, STEP, 2 * SUB):
                x = buf[item, s : s + SUB, t : t + pair] * weight[slot, s : s + SUB, :]
                e = s + SUB
                x = x + buf[item, e : e + SUB, t : t + pair] * weight[slot, e : e + SUB, :]
                x = x.astype(F32)
                total = x if total is None else total + x
            acc[p, :, t : t + pair] += total

    arrive(0)
    weigh(jnp.int32(0))

    def body(k, _):
        arrive(k + 1)
        add(k)
        weigh(k + 1)
        return 0

    lax.fori_loop(0, count - 1, body, 0)
    for n in (2, 3):
        side[n].wait()
    pltpu.make_async_copy(
        slots.at[pl.ds(0, group)], slot_rows.at[pl.ds(0, group)], slot_sem
    ).wait()
    add(count - 1)

    shape = (-(-group // SUB) * SUB, LANES)
    sub = lax.broadcasted_iota(jnp.int32, (SUB, LANES), 0)
    blocks = []
    for start in range(0, shape[0], SUB):
        block = jnp.zeros((SUB, LANES), jnp.int32)
        for g in range(start, min(start + SUB, group)):
            block = jnp.where(sub == g - start, lax.rem(ids[g], LANES), block)
        blocks.append(block)
    column = jnp.concatenate(blocks, axis=0)
    line = lax.broadcasted_iota(jnp.int32, shape, 0)
    lane = lax.broadcasted_iota(jnp.int32, shape, 1)
    picked = jnp.where((lane == column) & (line < group), slot_rows[...], 0).astype(F32)
    slot = jnp.sum(picked, axis=1, keepdims=True).astype(jnp.int32)
    slot = jnp.broadcast_to(slot, shape)
    owner = lax.div(slot, lists_own)
    local = slot - owner * lists_own
    high = lax.div(local, DIGIT)
    low = local - high * DIGIT
    owner_line = jnp.sum(jnp.where(line == lane, owner.astype(F32), 0.0), axis=0, keepdims=True)
    earlier = (jnp.broadcast_to(owner_line, shape) == owner.astype(F32)) & (lane < line)
    rank = jnp.sum(jnp.where(earlier, 1.0, 0.0), axis=1, keepdims=True).astype(jnp.int32)
    rank = jnp.broadcast_to(rank, shape)
    peer = jnp.zeros(shape, jnp.int32)
    for j in range(1, peers):
        peer = peer + (line >= j * passes).astype(jnp.int32)
    place = line + peer * (SUB - passes) + 1
    entry = jnp.where(lane == rank, high, 0)
    entry = jnp.where(lane == rank + capacity, low, entry)
    entry = jnp.where(lane == rank + 2 * capacity, place, entry)
    entry = jnp.where((rank < capacity) & (line < group), entry, 0).astype(F32)

    inverse = jnp.zeros((SUB, LANES), F32)
    for p in range(passes):
        inverse = jnp.where(sub == p, lens[p].astype(F32), inverse)
    inverse = jnp.where(sub < passes, 1.0 / jnp.maximum(inverse, 1.0), 0.0)
    for o in range(owners):
        info = jnp.sum(jnp.where(owner == o, entry, 0.0), axis=0, keepdims=True)
        for q in range(per):
            t = o * per + q
            cols = slice(t * LANES, (t + 1) * LANES)
            parts = [acc[p, :, cols] if p < passes else None for p in range(SUB)]
            bit = SUB // 2
            while bit:
                merged = []
                for n in range(bit):
                    a, b = parts[n], parts[n + bit]
                    if a is None:
                        merged.append(None)
                    elif b is None:
                        merged.append(jnp.where((sub & bit) == 0, a + pltpu.roll(a, SUB - bit, 0), 0.0))
                    else:
                        first = jnp.where((sub & bit) == 0, a, b)
                        second = jnp.where((sub & bit) == 0, b, a)
                        if bit * 2 == SUB:
                            merged.append(first + pltpu.roll(second, bit, 0))
                        else:
                            up = pltpu.roll(second, SUB - bit, 0)
                            down = pltpu.roll(second, bit, 0)
                            merged.append(first + jnp.where((sub & bit) == 0, up, down))
                parts = merged
                bit //= 2
            tile = parts[0] * gain[t : t + 1].astype(F32) * inverse
            for n in range(pairs):
                piece = tile[2 * n : 2 * n + 2].astype(BF16)
                at = (q * pairs + n) * LANES
                for j in range(peers):
                    out[o * peers + j, :, at : at + LANES] = piece
        info = jnp.broadcast_to(info, (2, LANES)).astype(BF16)
        for j in range(peers):
            out[o * peers + j, :, per * pairs * LANES :] = info


def project_kernel(
    got, head, cents, own, other, info_v, info_s, rows_in, info_sem, row_sem,
    *, owners, peers, passes, capacity,
):
    width = head.shape[1]
    lists_own = cents.shape[0]
    pairs = -(-passes // 2)
    per = (got.shape[2] // LANES - 1) // pairs
    wide = peers * SUB
    group = peers * passes
    half = owners // CORES * group
    core = lax.axis_index("core")
    col = pl.multiple_of(lax.axis_index("mp") * width, LANES)

    def final_row(o, at):
        peer = lax.div(at, SUB)
        chip = lax.div(o, CORES)
        away = jnp.where(o - chip * CORES == core, 0, half)
        return away + chip * group + peer * passes + (at - peer * SUB)

    tail = per * pairs * LANES
    lines = [got[o * peers, :, tail:].astype(F32)[0:1] for o in range(owners)]
    lines += [jnp.zeros((1, LANES), F32)] * (info_v.shape[1] - owners)
    info = jnp.concatenate(lines, axis=0).astype(jnp.int32)
    row = info * DIGIT + pltpu.roll(info, LANES - capacity, 1)
    row = jnp.clip(row, 0, lists_own - 1)
    place = pltpu.roll(info, LANES - 2 * capacity, 1)
    first = lax.div(row, SUB)
    real = (place > 0) & (place <= wide)
    info_v[0] = first
    info_v[1] = row - first * SUB
    info_v[2] = jnp.where(
        real,
        final_row(lax.broadcasted_iota(jnp.int32, info.shape, 0), jnp.where(real, place - 1, 0)),
        -1,
    )
    info_copy = pltpu.make_async_copy(info_v, info_s, info_sem)
    info_copy.start()
    info_copy.wait()
    entries = [(o, k) for o in range(owners) for k in range(capacity)]
    for n, (o, k) in enumerate(entries):
        pltpu.make_async_copy(
            cents.at[pl.ds(pl.multiple_of(info_s[0, o, k] * SUB, SUB), SUB), pl.ds(col, width)],
            rows_in.at[n],
            row_sem,
        ).start()
    lane = lax.broadcasted_iota(jnp.int32, (1, LANES), 1)
    spots = lax.broadcasted_iota(jnp.int32, (CORES * half, LANES), 0)
    share = LANES // SUB
    chosen = []
    for start in range(0, len(entries), share):
        target = jnp.full((1, LANES), -1, jnp.int32)
        for m, (o, k) in enumerate(entries[start : start + share]):
            target = jnp.where(lane == m * SUB + info_s[1, o, k], info_s[2, o, k], target)
        chosen.append(jnp.where(spots == target, -1.0, 0.0).astype(BF16))
    depth = len(entries) * SUB
    chosen = jnp.concatenate(chosen, axis=1)[:, :depth]
    sources = owners * peers
    depth_in = pairs * sources * 2
    order = []
    for start in range(0, depth_in, LANES):
        at = lane + start
        pair = lax.div(at, sources * 2)
        at = at - pair * sources * 2
        source = lax.div(at, 2)
        p = pair * 2 + at - source * 2
        o = lax.div(source, peers)
        target = jnp.where(p < passes, final_row(o, (source - o * peers) * SUB + p), -1)
        order.append(jnp.where(spots == target, 1.0, 0.0).astype(BF16))
    order = jnp.concatenate(order, axis=1)[:, :depth_in]
    x = jnp.concatenate(
        [
            jnp.concatenate(
                [
                    got[:, :, (q * pairs + n) * LANES : (q * pairs + n + 1) * LANES].reshape(
                        sources * 2, LANES
                    )
                    for q in range(per)
                ],
                axis=1,
            )
            for n in range(pairs)
        ],
        axis=0,
    )
    x = jnp.dot(order, x, preferred_element_type=F32).astype(BF16)
    total = jnp.dot(x, head[...], preferred_element_type=F32)
    pltpu.make_async_copy(rows_in, rows_in, row_sem).wait()
    total = total + jnp.dot(
        chosen, rows_in[...].reshape(depth, width), preferred_element_type=F32
    )
    own[...] = total[:half]
    other[...] = total[half:].astype(BF16)


def rotate_kernel(own, other, rotation, out, *, peers):
    group = out.shape[1]
    width = out.shape[2]
    resid = (own[...] + other[...].astype(F32)).astype(BF16)
    for j in range(peers):
        y = jnp.dot(
            resid, rotation[:, j * width : (j + 1) * width], preferred_element_type=F32
        ).astype(BF16)
        for c in range(resid.shape[0] // group):
            out[c * peers + j] = y[c * group : (c + 1) * group]


def quantize_kernel(parts, codes, scales):
    total = parts[0].astype(F32)
    for s in range(1, parts.shape[0]):
        total = total + parts[s].astype(F32)
    group, width = total.shape
    lane = lax.broadcasted_iota(jnp.int32, (group, LANES), 1)
    table = jnp.zeros((group, LANES), F32)
    for t in range(width // LANES):
        x = total[:, t * LANES : (t + 1) * LANES]
        size = jnp.abs(x)
        spread = jnp.zeros((group, LANES), F32)
        for b in range(LANES // BLOCK):
            inside = (lane >= b * BLOCK) & (lane < (b + 1) * BLOCK)
            top = jnp.max(jnp.where(inside, size, 0.0), axis=1, keepdims=True) + 1e-06
            spread = jnp.where(inside, top, spread)
            table = jnp.where(lane == t * (LANES // BLOCK) + b, top, table)
        codes[:, t * LANES : (t + 1) * LANES] = (x / spread).astype(BF16)
    scales[...] = table.T[: scales.shape[0]].astype(BF16)


def pool_call(lengths, list_ids, hidden, list_slot, gain, head, *, owners, peers, lists_own):
    passes, length, width = hidden.shape
    assert passes < SUB and length % STEP == 0
    group = list_ids.shape[0]
    capacity = max(2, 2 * group // owners)
    per = width // LANES // owners
    steps = length // STEP
    padded = -(-group // SUB) * SUB
    vmem = pl.BlockSpec(memory_space=pltpu.VMEM)
    hbm = pl.BlockSpec(memory_space=pl.ANY)
    return pl.pallas_call(
        functools.partial(
            pool_kernel, owners=owners, peers=peers, lists_own=lists_own, capacity=capacity
        ),
        out_shape=(
            pltpu.VMEM((owners * peers, 2, (per * -(-passes // 2) + 1) * LANES), BF16),
            pltpu.VMEM(head.shape, BF16),
        ),
        in_specs=[hbm] * 6,
        out_specs=(vmem, vmem),
        scratch_shapes=[
            pltpu.VMEM((passes * steps, STEP, width), BF16),
            pltpu.VMEM((2, STEP, 2 * LANES), BF16),
            pltpu.VMEM((passes, SUB, width), F32),
            pltpu.VMEM((padded, LANES), jnp.int32),
            pltpu.VMEM((width // LANES, LANES), BF16),
            pltpu.SMEM((passes,), jnp.int32),
            pltpu.SMEM((group,), jnp.int32),
            pltpu.SMEM((passes * steps,), jnp.int32),
            pltpu.SemaphoreType.DMA((passes * steps,)),
            pltpu.SemaphoreType.DMA,
            pltpu.SemaphoreType.DMA((4,)),
        ],
        compiler_params=pltpu.CompilerParams(vmem_limit_bytes=hidden.size * 2 + 6 * 2**20),
        name="pool",
    )(
        far(lengths), far(list_ids), far(hidden), far(list_slot.reshape(-1, LANES)),
        far(gain.reshape(-1, LANES)), far(head),
    )


def per_device(hidden, lengths, list_ids, gain, head, list_slot, centroids, rotation):
    passes, length, width = hidden.shape
    owners = lax.axis_size("chip") * lax.axis_size("core")
    peers = lax.axis_size("mp")
    group = list_ids.shape[0]
    lists_own = centroids.shape[0]
    capacity = max(2, 2 * group // owners)
    cols = head.shape[1]
    lead = -(-owners // SUB) * SUB
    vmem = pl.BlockSpec(memory_space=pltpu.VMEM)
    hbm = pl.BlockSpec(memory_space=pl.ANY)
    blocks, head = pool_call(
        lengths, list_ids, hidden, list_slot, gain, head,
        owners=owners, peers=peers, lists_own=lists_own,
    )
    got = lax.all_to_all(blocks, ("chip", "core", "mp"), 0, 0, tiled=True)
    half = owners // CORES * group
    own, other = pl.pallas_call(
        functools.partial(
            project_kernel, owners=owners, peers=peers, passes=passes, capacity=capacity
        ),
        out_shape=(
            pltpu.VMEM((half, cols), F32),
            pltpu.VMEM((half, cols), BF16),
        ),
        in_specs=[vmem, vmem, hbm],
        out_specs=(vmem, vmem),
        scratch_shapes=[
            pltpu.VMEM((3, lead, LANES), jnp.int32),
            pltpu.SMEM((3, lead, LANES), jnp.int32),
            pltpu.VMEM((owners * capacity, SUB, cols), BF16),
            pltpu.SemaphoreType.DMA,
            pltpu.SemaphoreType.DMA,
        ],
        compiler_params=pltpu.CompilerParams(vmem_limit_bytes=8 * 2**20),
        name="project",
    )(near(got), near(head), far(centroids))
    other = lax.ppermute(other, "core", [(c, (c + 1) % CORES) for c in range(CORES)])
    parts = pl.pallas_call(
        functools.partial(rotate_kernel, peers=peers),
        out_shape=pltpu.VMEM((owners // CORES * peers, group, cols), BF16),
        in_specs=[vmem, vmem, vmem],
        out_specs=vmem,
        compiler_params=pltpu.CompilerParams(vmem_limit_bytes=8 * 2**20),
        name="rotate",
    )(near(own), near(other), near(rotation))
    parts = lax.all_to_all(parts, ("chip", "mp"), 0, 0, tiled=True)
    codes, scales = pl.pallas_call(
        quantize_kernel,
        out_shape=(
            jax.ShapeDtypeStruct((group, cols), BF16),
            jax.ShapeDtypeStruct((cols // BLOCK, group), BF16),
        ),
        in_specs=[vmem],
        out_specs=(vmem, vmem),
        compiler_params=pltpu.CompilerParams(vmem_limit_bytes=8 * 2**20),
        name="quantize",
    )(near(parts))
    return codes, scales.T


def solution(mesh):
    dp, mp = mesh.shape["dp"], mesh.shape["mp"]
    split = Mesh(mesh.devices.reshape(dp // CORES, CORES, mp), ("chip", "core", "mp"))
    rows = ("chip", "core")
    in_specs = (
        P(("chip", "core", "mp"), None, None),
        P(("chip", "core", "mp")),
        P(rows),
        P(),
        P(rows, "mp"),
        P(),
        P(rows, None),
        P("mp", None),
    )
    out_specs = (P(rows, "mp"), P(rows, "mp"))
    return jax.shard_map(
        per_device, mesh=split, in_specs=in_specs, out_specs=out_specs, check_vma=False
    )
```

```python
import functools

import jax
import jax.numpy as jnp
from jax import lax
from jax.experimental import pallas as pl
from jax.experimental.pallas import tpu as pltpu
from jax.sharding import Mesh
from jax.sharding import PartitionSpec as P

BLOCK = 64
LANES = 128
SUB = 8
DIGIT = 256
CORES = 2
STEP = 64

F32 = jnp.float32
BF16 = jnp.bfloat16


def near(x):
    return pltpu.with_memory_space_constraint(x, pltpu.VMEM)


def far(x):
    return pltpu.with_memory_space_constraint(x, pltpu.HBM)


def pool_kernel(
    lens_hbm, ids_hbm, hidden, slots, gain_hbm, head, out, head_out, buf, weight, acc, slot_rows, gain,
    lens, ids, items, sems, slot_sem, side_sems, *, owners, peers, lists_own, capacity,
):
    passes, length, width = hidden.shape
    group = ids.shape[0]
    steps = length // STEP
    tiles = width // LANES
    per = tiles // owners
    pairs = -(-passes // 2)

    def chunk_copy(p, c):
        return pltpu.make_async_copy(
            hidden.at[p, pl.ds(c * STEP, STEP)], buf.at[p * steps + c], sems.at[p * steps + c]
        )

    def slot_copy(g):
        return pltpu.make_async_copy(
            slots.at[pl.ds(lax.div(ids[g], LANES), 1)], slot_rows.at[pl.ds(g, 1)], slot_sem
        )

    side = [
        pltpu.make_async_copy(source, target, side_sems.at[n])
        for n, (source, target) in enumerate(
            ((lens_hbm, lens), (ids_hbm, ids), (gain_hbm, gain), (head, head_out))
        )
    ]
    side[0].start()
    side[1].start()
    for p in range(passes):
        chunk_copy(p, 0).start()
        items[p] = p * steps
    side[0].wait()
    count = jnp.int32(passes)
    for c in range(1, steps):
        for p in range(passes):
            needed = lens[p] > c * STEP

            @pl.when(needed)
            def _():
                chunk_copy(p, c).start()
                items[count] = p * steps + c

            count = count + needed.astype(jnp.int32)
    side[1].wait()
    for g in range(group):
        slot_copy(g).start()
    side[2].start()
    side[3].start()

    def zero(p, _):
        acc[p] = jnp.zeros((SUB, width), F32)
        return 0

    lax.fori_loop(0, passes, zero, 0)

    def arrive(k):
        item = items[k]
        pltpu.make_async_copy(
            hidden.at[0, pl.ds(0, STEP)], buf.at[item], sems.at[item]
        ).wait()

    def weigh(k):
        item = items[k]
        p = lax.div(item, steps)
        start = lax.rem(item, steps) * STEP
        size = lens[p]
        for s in range(0, STEP, SUB):
            x = buf[item, s : s + SUB, :]
            x = x * x
            x = (x[:, : width // 2] + x[:, width // 2 :]).astype(F32)
            total = x[:, :LANES]
            for t in range(LANES, width // 2, LANES):
                total = total + x[:, t : t + LANES]
            square = jnp.sum(total, axis=1, keepdims=True)
            token = lax.broadcasted_iota(jnp.int32, (SUB, 1), 0) + (start + s)
            value = jnp.where(token < size, lax.rsqrt(square * (1.0 / width) + 1e-05), 0.0)
            weight[lax.rem(k, 2), s : s + SUB, :] = jnp.broadcast_to(value, (SUB, 2 * LANES)).astype(BF16)

    def add(k):
        item = items[k]
        p = lax.div(item, steps)
        slot = lax.rem(k, 2)
        pair = 2 * LANES
        for t in range(0, width, pair):
            total = None
            for s in range(0, STEP, 2 * SUB):
                x = buf[item, s : s + SUB, t : t + pair] * weight[slot, s : s + SUB, :]
                e = s + SUB
                x = x + buf[item, e : e + SUB, t : t + pair] * weight[slot, e : e + SUB, :]
                x = x.astype(F32)
                total = x if total is None else total + x
            acc[p, :, t : t + pair] += total

    arrive(0)
    weigh(jnp.int32(0))

    def body(k, _):
        arrive(k + 1)
        add(k)
        weigh(k + 1)
        return 0

    lax.fori_loop(0, count - 1, body, 0)
    for n in (2, 3):
        side[n].wait()
    pltpu.make_async_copy(
        slots.at[pl.ds(0, group)], slot_rows.at[pl.ds(0, group)], slot_sem
    ).wait()
    add(count - 1)

    shape = (-(-group // SUB) * SUB, LANES)
    sub = lax.broadcasted_iota(jnp.int32, (SUB, LANES), 0)
    blocks = []
    for start in range(0, shape[0], SUB):
        block = jnp.zeros((SUB, LANES), jnp.int32)
        for g in range(start, min(start + SUB, group)):
            block = jnp.where(sub == g - start, lax.rem(ids[g], LANES), block)
        blocks.append(block)
    column = jnp.concatenate(blocks, axis=0)
    line = lax.broadcasted_iota(jnp.int32, shape, 0)
    lane = lax.broadcasted_iota(jnp.int32, shape, 1)
    picked = jnp.where((lane == column) & (line < group), slot_rows[...], 0).astype(F32)
    slot = jnp.sum(picked, axis=1, keepdims=True).astype(jnp.int32)
    slot = jnp.broadcast_to(slot, shape)
    owner = lax.div(slot, lists_own)
    local = slot - owner * lists_own
    high = lax.div(local, DIGIT)
    low = local - high * DIGIT
    owner_line = jnp.sum(jnp.where(line == lane, owner.astype(F32), 0.0), axis=0, keepdims=True)
    earlier = (jnp.broadcast_to(owner_line, shape) == owner.astype(F32)) & (lane < line)
    rank = jnp.sum(jnp.where(earlier, 1.0, 0.0), axis=1, keepdims=True).astype(jnp.int32)
    rank = jnp.broadcast_to(rank, shape)
    peer = jnp.zeros(shape, jnp.int32)
    for j in range(1, peers):
        peer = peer + (line >= j * passes).astype(jnp.int32)
    place = line + peer * (SUB - passes) + 1
    entry = jnp.where(lane == rank, high, 0)
    entry = jnp.where(lane == rank + capacity, low, entry)
    entry = jnp.where(lane == rank + 2 * capacity, place, entry)
    entry = jnp.where((rank < capacity) & (line < group), entry, 0).astype(F32)

    inverse = jnp.zeros((SUB, LANES), F32)
    for p in range(passes):
        inverse = jnp.where(sub == p, lens[p].astype(F32), inverse)
    inverse = jnp.where(sub < passes, 1.0 / jnp.maximum(inverse, 1.0), 0.0)
    for o in range(owners):
        info = jnp.sum(jnp.where(owner == o, entry, 0.0), axis=0, keepdims=True)
        for q in range(per):
            t = o * per + q
            cols = slice(t * LANES, (t + 1) * LANES)
            parts = [acc[p, :, cols] if p < passes else None for p in range(SUB)]
            bit = SUB // 2
            while bit:
                merged = []
                for n in range(bit):
                    a, b = parts[n], parts[n + bit]
                    if a is None:
                        merged.append(None)
                    elif b is None:
                        merged.append(jnp.where((sub & bit) == 0, a + pltpu.roll(a, SUB - bit, 0), 0.0))
                    else:
                        first = jnp.where((sub & bit) == 0, a, b)
                        second = jnp.where((sub & bit) == 0, b, a)
                        if bit * 2 == SUB:
                            merged.append(first + pltpu.roll(second, bit, 0))
                        else:
                            up = pltpu.roll(second, SUB - bit, 0)
                            down = pltpu.roll(second, bit, 0)
                            merged.append(first + jnp.where((sub & bit) == 0, up, down))
                parts = merged
                bit //= 2
            tile = parts[0] * gain[t : t + 1].astype(F32) * inverse
            for n in range(pairs):
                piece = tile[2 * n : 2 * n + 2].astype(BF16)
                at = (q * pairs + n) * LANES
                for j in range(peers):
                    out[o * peers + j, :, at : at + LANES] = piece
        info = jnp.broadcast_to(info, (2, LANES)).astype(BF16)
        for j in range(peers):
            out[o * peers + j, :, per * pairs * LANES :] = info


def project_kernel(
    got, head, cents, own, other, info_v, info_s, rows_in, info_sem, row_sem,
    *, owners, peers, passes, capacity,
):
    width = head.shape[1]
    lists_own = cents.shape[0]
    pairs = -(-passes // 2)
    per = (got.shape[2] // LANES - 1) // pairs
    wide = peers * SUB
    group = peers * passes
    half = owners // CORES * group
    core = lax.axis_index("core")
    col = pl.multiple_of(lax.axis_index("mp") * width, LANES)

    def final_row(o, at):
        peer = lax.div(at, SUB)
        chip = lax.div(o, CORES)
        away = jnp.where(o - chip * CORES == core, 0, half)
        return away + chip * group + peer * passes + (at - peer * SUB)

    tail = per * pairs * LANES
    lines = [got[o * peers, :, tail:].astype(F32)[0:1] for o in range(owners)]
    lines += [jnp.zeros((1, LANES), F32)] * (info_v.shape[1] - owners)
    info = jnp.concatenate(lines, axis=0).astype(jnp.int32)
    row = info * DIGIT + pltpu.roll(info, LANES - capacity, 1)
    row = jnp.clip(row, 0, lists_own - 1)
    place = pltpu.roll(info, LANES - 2 * capacity, 1)
    first = lax.div(row, SUB)
    real = (place > 0) & (place <= wide)
    info_v[0] = first
    info_v[1] = row - first * SUB
    info_v[2] = jnp.where(
        real,
        final_row(lax.broadcasted_iota(jnp.int32, info.shape, 0), jnp.where(real, place - 1, 0)),
        -1,
    )
    info_copy = pltpu.make_async_copy(info_v, info_s, info_sem)
    info_copy.start()
    entries = [(o, k) for o in range(owners) for k in range(capacity)]
    for n, (o, k) in enumerate(entries):
        pltpu.make_async_copy(
            cents.at[pl.ds(pl.multiple_of(first[o, k] * SUB, SUB), SUB), pl.ds(col, width)],
            rows_in.at[n],
            row_sem,
        ).start()
    info_copy.wait()
    lane = lax.broadcasted_iota(jnp.int32, (1, LANES), 1)
    spots = lax.broadcasted_iota(jnp.int32, (CORES * half, LANES), 0)
    share = LANES // SUB
    chosen = []
    for start in range(0, len(entries), share):
        target = jnp.full((1, LANES), -1, jnp.int32)
        for m, (o, k) in enumerate(entries[start : start + share]):
            target = jnp.where(lane == m * SUB + info_s[1, o, k], info_s[2, o, k], target)
        chosen.append(jnp.where(spots == target, -1.0, 0.0).astype(BF16))
    depth = len(entries) * SUB
    chosen = jnp.concatenate(chosen, axis=1)[:, :depth]
    sources = owners * peers
    depth_in = pairs * sources * 2
    order = []
    for start in range(0, depth_in, LANES):
        at = lane + start
        pair = lax.div(at, sources * 2)
        at = at - pair * sources * 2
        source = lax.div(at, 2)
        p = pair * 2 + at - source * 2
        o = lax.div(source, peers)
        target = jnp.where(p < passes, final_row(o, (source - o * peers) * SUB + p), -1)
        order.append(jnp.where(spots == target, 1.0, 0.0).astype(BF16))
    order = jnp.concatenate(order, axis=1)[:, :depth_in]
    x = jnp.concatenate(
        [
            jnp.concatenate(
                [
                    got[:, :, (q * pairs + n) * LANES : (q * pairs + n + 1) * LANES].reshape(
                        sources * 2, LANES
                    )
                    for q in range(per)
                ],
                axis=1,
            )
            for n in range(pairs)
        ],
        axis=0,
    )
    x = jnp.dot(order, x, preferred_element_type=F32).astype(BF16)
    total = jnp.dot(x, head[...], preferred_element_type=F32)
    pltpu.make_async_copy(rows_in, rows_in, row_sem).wait()
    total = total + jnp.dot(
        chosen, rows_in[...].reshape(depth, width), preferred_element_type=F32
    )
    own[...] = total[:half]
    other[...] = total[half:].astype(BF16)


def rotate_kernel(own, other, rotation, out, *, peers):
    group = out.shape[1]
    width = out.shape[2]
    resid = (own[...] + other[...].astype(F32)).astype(BF16)
    for j in range(peers):
        y = jnp.dot(
            resid, rotation[:, j * width : (j + 1) * width], preferred_element_type=F32
        ).astype(BF16)
        for c in range(resid.shape[0] // group):
            out[c * peers + j] = y[c * group : (c + 1) * group]


def quantize_kernel(parts, codes, scales):
    total = parts[0].astype(F32)
    for s in range(1, parts.shape[0]):
        total = total + parts[s].astype(F32)
    group, width = total.shape
    lane = lax.broadcasted_iota(jnp.int32, (group, LANES), 1)
    table = jnp.zeros((group, LANES), F32)
    for t in range(width // LANES):
        x = total[:, t * LANES : (t + 1) * LANES]
        size = jnp.abs(x)
        spread = jnp.zeros((group, LANES), F32)
        for b in range(LANES // BLOCK):
            inside = (lane >= b * BLOCK) & (lane < (b + 1) * BLOCK)
            top = jnp.max(jnp.where(inside, size, 0.0), axis=1, keepdims=True) + 1e-06
            spread = jnp.where(inside, top, spread)
            table = jnp.where(lane == t * (LANES // BLOCK) + b, top, table)
        codes[:, t * LANES : (t + 1) * LANES] = (x / spread).astype(BF16)
    scales[...] = table.T[: scales.shape[0]].astype(BF16)


def pool_call(lengths, list_ids, hidden, list_slot, gain, head, *, owners, peers, lists_own):
    passes, length, width = hidden.shape
    assert passes < SUB and length % STEP == 0
    group = list_ids.shape[0]
    capacity = max(2, 2 * group // owners)
    per = width // LANES // owners
    steps = length // STEP
    padded = -(-group // SUB) * SUB
    vmem = pl.BlockSpec(memory_space=pltpu.VMEM)
    hbm = pl.BlockSpec(memory_space=pl.ANY)
    return pl.pallas_call(
        functools.partial(
            pool_kernel, owners=owners, peers=peers, lists_own=lists_own, capacity=capacity
        ),
        out_shape=(
            pltpu.VMEM((owners * peers, 2, (per * -(-passes // 2) + 1) * LANES), BF16),
            pltpu.VMEM(head.shape, BF16),
        ),
        in_specs=[hbm] * 6,
        out_specs=(vmem, vmem),
        scratch_shapes=[
            pltpu.VMEM((passes * steps, STEP, width), BF16),
            pltpu.VMEM((2, STEP, 2 * LANES), BF16),
            pltpu.VMEM((passes, SUB, width), F32),
            pltpu.VMEM((padded, LANES), jnp.int32),
            pltpu.VMEM((width // LANES, LANES), BF16),
            pltpu.SMEM((passes,), jnp.int32),
            pltpu.SMEM((group,), jnp.int32),
            pltpu.SMEM((passes * steps,), jnp.int32),
            pltpu.SemaphoreType.DMA((passes * steps,)),
            pltpu.SemaphoreType.DMA,
            pltpu.SemaphoreType.DMA((4,)),
        ],
        compiler_params=pltpu.CompilerParams(vmem_limit_bytes=hidden.size * 2 + 6 * 2**20),
        name="pool",
    )(
        far(lengths), far(list_ids), far(hidden), far(list_slot.reshape(-1, LANES)),
        far(gain.reshape(-1, LANES)), far(head),
    )


def per_device(hidden, lengths, list_ids, gain, head, list_slot, centroids, rotation):
    passes, length, width = hidden.shape
    owners = lax.axis_size("chip") * lax.axis_size("core")
    peers = lax.axis_size("mp")
    group = list_ids.shape[0]
    lists_own = centroids.shape[0]
    capacity = max(2, 2 * group // owners)
    cols = head.shape[1]
    lead = -(-owners // SUB) * SUB
    vmem = pl.BlockSpec(memory_space=pltpu.VMEM)
    hbm = pl.BlockSpec(memory_space=pl.ANY)
    blocks, head = pool_call(
        lengths, list_ids, hidden, list_slot, gain, head,
        owners=owners, peers=peers, lists_own=lists_own,
    )
    got = lax.all_to_all(blocks, ("chip", "core", "mp"), 0, 0, tiled=True)
    half = owners // CORES * group
    own, other = pl.pallas_call(
        functools.partial(
            project_kernel, owners=owners, peers=peers, passes=passes, capacity=capacity
        ),
        out_shape=(
            pltpu.VMEM((half, cols), F32),
            pltpu.VMEM((half, cols), BF16),
        ),
        in_specs=[vmem, vmem, hbm],
        out_specs=(vmem, vmem),
        scratch_shapes=[
            pltpu.VMEM((3, lead, LANES), jnp.int32),
            pltpu.SMEM((3, lead, LANES), jnp.int32),
            pltpu.VMEM((owners * capacity, SUB, cols), BF16),
            pltpu.SemaphoreType.DMA,
            pltpu.SemaphoreType.DMA,
        ],
        compiler_params=pltpu.CompilerParams(vmem_limit_bytes=8 * 2**20),
        name="project",
    )(near(got), near(head), far(centroids))
    other = lax.ppermute(other, "core", [(c, (c + 1) % CORES) for c in range(CORES)])
    parts = pl.pallas_call(
        functools.partial(rotate_kernel, peers=peers),
        out_shape=pltpu.VMEM((owners // CORES * peers, group, cols), BF16),
        in_specs=[vmem, vmem, vmem],
        out_specs=vmem,
        compiler_params=pltpu.CompilerParams(vmem_limit_bytes=8 * 2**20),
        name="rotate",
    )(near(own), near(other), near(rotation))
    parts = lax.all_to_all(parts, ("chip", "mp"), 0, 0, tiled=True)
    codes, scales = pl.pallas_call(
        quantize_kernel,
        out_shape=(
            jax.ShapeDtypeStruct((group, cols), BF16),
            jax.ShapeDtypeStruct((cols // BLOCK, group), BF16),
        ),
        in_specs=[vmem],
        out_specs=(vmem, vmem),
        compiler_params=pltpu.CompilerParams(vmem_limit_bytes=8 * 2**20),
        name="quantize",
    )(near(parts))
    return codes, scales.T


def solution(mesh):
    dp, mp = mesh.shape["dp"], mesh.shape["mp"]
    split = Mesh(mesh.devices.reshape(dp // CORES, CORES, mp), ("chip", "core", "mp"))
    rows = ("chip", "core")
    in_specs = (
        P(("chip", "core", "mp"), None, None),
        P(("chip", "core", "mp")),
        P(rows),
        P(),
        P(rows, "mp"),
        P(),
        P(rows, None),
        P("mp", None),
    )
    out_specs = (P(rows, "mp"), P(rows, "mp"))
    return jax.shard_map(
        per_device, mesh=split, in_specs=in_specs, out_specs=out_specs, check_vma=False
    )
```

```python
import functools

import jax
import jax.numpy as jnp
from jax import lax
from jax.experimental import pallas as pl
from jax.experimental.pallas import tpu as pltpu
from jax.sharding import Mesh
from jax.sharding import PartitionSpec as P

BLOCK = 64
LANES = 128
SUB = 8
DIGIT = 256
CORES = 2
STEP = 64

F32 = jnp.float32
BF16 = jnp.bfloat16


def near(x):
    return pltpu.with_memory_space_constraint(x, pltpu.VMEM)


def far(x):
    return pltpu.with_memory_space_constraint(x, pltpu.HBM)


def pool_kernel(
    lens_hbm, ids_hbm, hidden, slots, gain_hbm, head, out, head_out, buf, weight, acc, slot_rows, gain,
    lens, ids, items, sems, slot_sem, side_sems, *, owners, peers, lists_own, capacity,
):
    passes, length, width = hidden.shape
    group = ids.shape[0]
    steps = length // STEP
    tiles = width // LANES
    per = tiles // owners
    pairs = -(-passes // 2)

    def chunk_copy(p, c):
        return pltpu.make_async_copy(
            hidden.at[p, pl.ds(c * STEP, STEP)], buf.at[p * steps + c], sems.at[p * steps + c]
        )

    def slot_copy(g):
        return pltpu.make_async_copy(
            slots.at[pl.ds(lax.div(ids[g], LANES), 1)], slot_rows.at[pl.ds(g, 1)], slot_sem
        )

    side = [
        pltpu.make_async_copy(source, target, side_sems.at[n])
        for n, (source, target) in enumerate(
            ((lens_hbm, lens), (ids_hbm, ids), (gain_hbm, gain), (head, head_out))
        )
    ]
    side[0].start()
    side[1].start()
    for p in range(passes):
        chunk_copy(p, 0).start()
        items[p] = p * steps
    side[0].wait()
    count = jnp.int32(passes)
    for c in range(1, steps):
        for p in range(passes):
            needed = lens[p] > c * STEP

            @pl.when(needed)
            def _():
                chunk_copy(p, c).start()
                items[count] = p * steps + c

            count = count + needed.astype(jnp.int32)
    side[1].wait()
    for g in range(group):
        slot_copy(g).start()
    side[2].start()
    side[3].start()

    def zero(p, _):
        acc[p] = jnp.zeros((SUB, width), F32)
        return 0

    lax.fori_loop(0, passes, zero, 0)

    def arrive(k):
        item = items[k]
        pltpu.make_async_copy(
            hidden.at[0, pl.ds(0, STEP)], buf.at[item], sems.at[item]
        ).wait()

    def weigh(k):
        item = items[k]
        p = lax.div(item, steps)
        start = lax.rem(item, steps) * STEP
        size = lens[p]
        for s in range(0, STEP, SUB):
            x = buf[item, s : s + SUB, :]
            x = x * x
            x = (x[:, : width // 2] + x[:, width // 2 :]).astype(F32)
            total = x[:, :LANES]
            for t in range(LANES, width // 2, LANES):
                total = total + x[:, t : t + LANES]
            square = jnp.sum(total, axis=1, keepdims=True)
            token = lax.broadcasted_iota(jnp.int32, (SUB, 1), 0) + (start + s)
            value = jnp.where(token < size, lax.rsqrt(square * (1.0 / width) + 1e-05), 0.0)
            weight[lax.rem(k, 2), s : s + SUB, :] = jnp.broadcast_to(value, (SUB, 2 * LANES)).astype(BF16)

    def add(k):
        item = items[k]
        p = lax.div(item, steps)
        slot = lax.rem(k, 2)
        pair = 2 * LANES
        for t in range(0, width, pair):
            total = None
            for s in range(0, STEP, 2 * SUB):
                x = buf[item, s : s + SUB, t : t + pair] * weight[slot, s : s + SUB, :]
                e = s + SUB
                x = x + buf[item, e : e + SUB, t : t + pair] * weight[slot, e : e + SUB, :]
                x = x.astype(F32)
                total = x if total is None else total + x
            acc[p, :, t : t + pair] += total

    arrive(0)
    weigh(jnp.int32(0))

    def body(k, _):
        arrive(k + 1)
        add(k)
        weigh(k + 1)
        return 0

    lax.fori_loop(0, count - 1, body, 0)
    for n in (2, 3):
        side[n].wait()
    pltpu.make_async_copy(
        slots.at[pl.ds(0, group)], slot_rows.at[pl.ds(0, group)], slot_sem
    ).wait()
    add(count - 1)

    shape = (-(-group // SUB) * SUB, LANES)
    sub = lax.broadcasted_iota(jnp.int32, (SUB, LANES), 0)
    blocks = []
    for start in range(0, shape[0], SUB):
        block = jnp.zeros((SUB, LANES), jnp.int32)
        for g in range(start, min(start + SUB, group)):
            block = jnp.where(sub == g - start, lax.rem(ids[g], LANES), block)
        blocks.append(block)
    column = jnp.concatenate(blocks, axis=0)
    line = lax.broadcasted_iota(jnp.int32, shape, 0)
    lane = lax.broadcasted_iota(jnp.int32, shape, 1)
    picked = jnp.where((lane == column) & (line < group), slot_rows[...], 0).astype(F32)
    slot = jnp.sum(picked, axis=1, keepdims=True).astype(jnp.int32)
    slot = jnp.broadcast_to(slot, shape)
    owner = lax.div(slot, lists_own)
    local = slot - owner * lists_own
    high = lax.div(local, DIGIT)
    low = local - high * DIGIT
    owner_line = jnp.sum(jnp.where(line == lane, owner.astype(F32), 0.0), axis=0, keepdims=True)
    earlier = (jnp.broadcast_to(owner_line, shape) == owner.astype(F32)) & (lane < line)
    rank = jnp.sum(jnp.where(earlier, 1.0, 0.0), axis=1, keepdims=True).astype(jnp.int32)
    rank = jnp.broadcast_to(rank, shape)
    peer = jnp.zeros(shape, jnp.int32)
    for j in range(1, peers):
        peer = peer + (line >= j * passes).astype(jnp.int32)
    place = line + peer * (SUB - passes) + 1
    entry = jnp.where(lane == rank, high, 0)
    entry = jnp.where(lane == rank + capacity, low, entry)
    entry = jnp.where(lane == rank + 2 * capacity, place, entry)
    entry = jnp.where((rank < capacity) & (line < group), entry, 0).astype(F32)

    inverse = jnp.zeros((SUB, LANES), F32)
    for p in range(passes):
        inverse = jnp.where(sub == p, lens[p].astype(F32), inverse)
    inverse = jnp.where(sub < passes, 1.0 / jnp.maximum(inverse, 1.0), 0.0)
    for o in range(owners):
        info = jnp.sum(jnp.where(owner == o, entry, 0.0), axis=0, keepdims=True)
        for q in range(per):
            t = o * per + q
            cols = slice(t * LANES, (t + 1) * LANES)
            parts = [acc[p, :, cols] if p < passes else None for p in range(SUB)]
            bit = SUB // 2
            while bit:
                merged = []
                for n in range(bit):
                    a, b = parts[n], parts[n + bit]
                    if a is None:
                        merged.append(None)
                    elif b is None:
                        merged.append(jnp.where((sub & bit) == 0, a + pltpu.roll(a, SUB - bit, 0), 0.0))
                    else:
                        first = jnp.where((sub & bit) == 0, a, b)
                        second = jnp.where((sub & bit) == 0, b, a)
                        if bit * 2 == SUB:
                            merged.append(first + pltpu.roll(second, bit, 0))
                        else:
                            up = pltpu.roll(second, SUB - bit, 0)
                            down = pltpu.roll(second, bit, 0)
                            merged.append(first + jnp.where((sub & bit) == 0, up, down))
                parts = merged
                bit //= 2
            tile = parts[0] * gain[t : t + 1].astype(F32) * inverse
            for n in range(pairs):
                piece = tile[2 * n : 2 * n + 2].astype(BF16)
                at = (q * pairs + n) * LANES
                for j in range(peers):
                    out[o * peers + j, :, at : at + LANES] = piece
        info = jnp.broadcast_to(info, (2, LANES)).astype(BF16)
        for j in range(peers):
            out[o * peers + j, :, per * pairs * LANES :] = info


def project_kernel(
    got, head, cents, rotation, own, other, rotation_out, info_v, info_s, rows_in, info_sem, row_sem,
    turn_sem,
    *, owners, peers, passes, capacity,
):
    width = head.shape[1]
    lists_own = cents.shape[0]
    pairs = -(-passes // 2)
    per = (got.shape[2] // LANES - 1) // pairs
    wide = peers * SUB
    group = peers * passes
    half = owners // CORES * group
    core = lax.axis_index("core")
    col = pl.multiple_of(lax.axis_index("mp") * width, LANES)

    def final_row(o, at):
        peer = lax.div(at, SUB)
        chip = lax.div(o, CORES)
        away = jnp.where(o - chip * CORES == core, 0, half)
        return away + chip * group + peer * passes + (at - peer * SUB)

    tail = per * pairs * LANES
    lines = [got[o * peers, :, tail:].astype(F32)[0:1] for o in range(owners)]
    lines += [jnp.zeros((1, LANES), F32)] * (info_v.shape[1] - owners)
    info = jnp.concatenate(lines, axis=0).astype(jnp.int32)
    row = info * DIGIT + pltpu.roll(info, LANES - capacity, 1)
    row = jnp.clip(row, 0, lists_own - 1)
    place = pltpu.roll(info, LANES - 2 * capacity, 1)
    first = lax.div(row, SUB)
    real = (place > 0) & (place <= wide)
    info_v[0] = first
    info_v[1] = row - first * SUB
    info_v[2] = jnp.where(
        real,
        final_row(lax.broadcasted_iota(jnp.int32, info.shape, 0), jnp.where(real, place - 1, 0)),
        -1,
    )
    info_copy = pltpu.make_async_copy(info_v, info_s, info_sem)
    info_copy.start()
    entries = [(o, k) for o in range(owners) for k in range(capacity)]
    for n, (o, k) in enumerate(entries):
        pltpu.make_async_copy(
            cents.at[pl.ds(pl.multiple_of(first[o, k] * SUB, SUB), SUB), pl.ds(col, width)],
            rows_in.at[n],
            row_sem,
        ).start()
    turn_copy = pltpu.make_async_copy(rotation, rotation_out, turn_sem)
    turn_copy.start()
    info_copy.wait()
    lane = lax.broadcasted_iota(jnp.int32, (1, LANES), 1)
    spots = lax.broadcasted_iota(jnp.int32, (CORES * half, LANES), 0)
    share = LANES // SUB
    chosen = []
    for start in range(0, len(entries), share):
        target = jnp.full((1, LANES), -1, jnp.int32)
        for m, (o, k) in enumerate(entries[start : start + share]):
            target = jnp.where(lane == m * SUB + info_s[1, o, k], info_s[2, o, k], target)
        chosen.append(jnp.where(spots == target, -1.0, 0.0).astype(BF16))
    depth = len(entries) * SUB
    chosen = jnp.concatenate(chosen, axis=1)[:, :depth]
    sources = owners * peers
    depth_in = pairs * sources * 2
    order = []
    for start in range(0, depth_in, LANES):
        at = lane + start
        pair = lax.div(at, sources * 2)
        at = at - pair * sources * 2
        source = lax.div(at, 2)
        p = pair * 2 + at - source * 2
        o = lax.div(source, peers)
        target = jnp.where(p < passes, final_row(o, (source - o * peers) * SUB + p), -1)
        order.append(jnp.where(spots == target, 1.0, 0.0).astype(BF16))
    order = jnp.concatenate(order, axis=1)[:, :depth_in]
    x = jnp.concatenate(
        [
            jnp.concatenate(
                [
                    got[:, :, (q * pairs + n) * LANES : (q * pairs + n + 1) * LANES].reshape(
                        sources * 2, LANES
                    )
                    for q in range(per)
                ],
                axis=1,
            )
            for n in range(pairs)
        ],
        axis=0,
    )
    x = jnp.dot(order, x, preferred_element_type=F32).astype(BF16)
    total = jnp.dot(x, head[...], preferred_element_type=F32)
    pltpu.make_async_copy(rows_in, rows_in, row_sem).wait()
    total = total + jnp.dot(
        chosen, rows_in[...].reshape(depth, width), preferred_element_type=F32
    )
    own[...] = total[:half]
    other[...] = total[half:].astype(BF16)
    turn_copy.wait()


def rotate_kernel(own, other, rotation, out, *, peers):
    group = out.shape[1]
    width = out.shape[2]
    resid = (own[...] + other[...].astype(F32)).astype(BF16)
    for j in range(peers):
        y = jnp.dot(
            resid, rotation[:, j * width : (j + 1) * width], preferred_element_type=F32
        ).astype(BF16)
        for c in range(resid.shape[0] // group):
            out[c * peers + j] = y[c * group : (c + 1) * group]


def quantize_kernel(parts, codes, scales):
    total = parts[0].astype(F32)
    for s in range(1, parts.shape[0]):
        total = total + parts[s].astype(F32)
    group, width = total.shape
    lane = lax.broadcasted_iota(jnp.int32, (group, LANES), 1)
    table = jnp.zeros((group, LANES), F32)
    for t in range(width // LANES):
        x = total[:, t * LANES : (t + 1) * LANES]
        size = jnp.abs(x)
        spread = jnp.zeros((group, LANES), F32)
        for b in range(LANES // BLOCK):
            inside = (lane >= b * BLOCK) & (lane < (b + 1) * BLOCK)
            top = jnp.max(jnp.where(inside, size, 0.0), axis=1, keepdims=True) + 1e-06
            spread = jnp.where(inside, top, spread)
            table = jnp.where(lane == t * (LANES // BLOCK) + b, top, table)
        codes[:, t * LANES : (t + 1) * LANES] = (x / spread).astype(BF16)
    scales[...] = table.T[: scales.shape[0]].astype(BF16)


def pool_call(lengths, list_ids, hidden, list_slot, gain, head, *, owners, peers, lists_own):
    passes, length, width = hidden.shape
    assert passes < SUB and length % STEP == 0
    group = list_ids.shape[0]
    capacity = max(2, 2 * group // owners)
    per = width // LANES // owners
    steps = length // STEP
    padded = -(-group // SUB) * SUB
    vmem = pl.BlockSpec(memory_space=pltpu.VMEM)
    hbm = pl.BlockSpec(memory_space=pl.ANY)
    return pl.pallas_call(
        functools.partial(
            pool_kernel, owners=owners, peers=peers, lists_own=lists_own, capacity=capacity
        ),
        out_shape=(
            pltpu.VMEM((owners * peers, 2, (per * -(-passes // 2) + 1) * LANES), BF16),
            pltpu.VMEM(head.shape, BF16),
        ),
        in_specs=[hbm] * 6,
        out_specs=(vmem, vmem),
        scratch_shapes=[
            pltpu.VMEM((passes * steps, STEP, width), BF16),
            pltpu.VMEM((2, STEP, 2 * LANES), BF16),
            pltpu.VMEM((passes, SUB, width), F32),
            pltpu.VMEM((padded, LANES), jnp.int32),
            pltpu.VMEM((width // LANES, LANES), BF16),
            pltpu.SMEM((passes,), jnp.int32),
            pltpu.SMEM((group,), jnp.int32),
            pltpu.SMEM((passes * steps,), jnp.int32),
            pltpu.SemaphoreType.DMA((passes * steps,)),
            pltpu.SemaphoreType.DMA,
            pltpu.SemaphoreType.DMA((4,)),
        ],
        compiler_params=pltpu.CompilerParams(vmem_limit_bytes=hidden.size * 2 + 6 * 2**20),
        name="pool",
    )(
        far(lengths), far(list_ids), far(hidden), far(list_slot.reshape(-1, LANES)),
        far(gain.reshape(-1, LANES)), far(head),
    )


def per_device(hidden, lengths, list_ids, gain, head, list_slot, centroids, rotation):
    passes, length, width = hidden.shape
    owners = lax.axis_size("chip") * lax.axis_size("core")
    peers = lax.axis_size("mp")
    group = list_ids.shape[0]
    lists_own = centroids.shape[0]
    capacity = max(2, 2 * group // owners)
    cols = head.shape[1]
    lead = -(-owners // SUB) * SUB
    vmem = pl.BlockSpec(memory_space=pltpu.VMEM)
    hbm = pl.BlockSpec(memory_space=pl.ANY)
    blocks, head = pool_call(
        lengths, list_ids, hidden, list_slot, gain, head,
        owners=owners, peers=peers, lists_own=lists_own,
    )
    got = lax.all_to_all(blocks, ("chip", "core", "mp"), 0, 0, tiled=True)
    half = owners // CORES * group
    own, other, rotation = pl.pallas_call(
        functools.partial(
            project_kernel, owners=owners, peers=peers, passes=passes, capacity=capacity
        ),
        out_shape=(
            pltpu.VMEM((half, cols), F32),
            pltpu.VMEM((half, cols), BF16),
            pltpu.VMEM(rotation.shape, BF16),
        ),
        in_specs=[vmem, vmem, hbm, hbm],
        out_specs=(vmem, vmem, vmem),
        scratch_shapes=[
            pltpu.VMEM((3, lead, LANES), jnp.int32),
            pltpu.SMEM((3, lead, LANES), jnp.int32),
            pltpu.VMEM((owners * capacity, SUB, cols), BF16),
            pltpu.SemaphoreType.DMA,
            pltpu.SemaphoreType.DMA,
            pltpu.SemaphoreType.DMA,
        ],
        compiler_params=pltpu.CompilerParams(vmem_limit_bytes=8 * 2**20),
        name="project",
    )(near(got), near(head), far(centroids), far(rotation))
    other = lax.ppermute(other, "core", [(c, (c + 1) % CORES) for c in range(CORES)])
    parts = pl.pallas_call(
        functools.partial(rotate_kernel, peers=peers),
        out_shape=pltpu.VMEM((owners // CORES * peers, group, cols), BF16),
        in_specs=[vmem, vmem, vmem],
        out_specs=vmem,
        compiler_params=pltpu.CompilerParams(vmem_limit_bytes=8 * 2**20),
        name="rotate",
    )(near(own), near(other), near(rotation))
    parts = lax.all_to_all(parts, ("chip", "mp"), 0, 0, tiled=True)
    codes, scales = pl.pallas_call(
        quantize_kernel,
        out_shape=(
            jax.ShapeDtypeStruct((group, cols), BF16),
            jax.ShapeDtypeStruct((cols // BLOCK, group), BF16),
        ),
        in_specs=[vmem],
        out_specs=(vmem, vmem),
        compiler_params=pltpu.CompilerParams(vmem_limit_bytes=8 * 2**20),
        name="quantize",
    )(near(parts))
    return codes, scales.T


def solution(mesh):
    dp, mp = mesh.shape["dp"], mesh.shape["mp"]
    split = Mesh(mesh.devices.reshape(dp // CORES, CORES, mp), ("chip", "core", "mp"))
    rows = ("chip", "core")
    in_specs = (
        P(("chip", "core", "mp"), None, None),
        P(("chip", "core", "mp")),
        P(rows),
        P(),
        P(rows, "mp"),
        P(),
        P(rows, None),
        P("mp", None),
    )
    out_specs = (P(rows, "mp"), P(rows, "mp"))
    return jax.shard_map(
        per_device, mesh=split, in_specs=in_specs, out_specs=out_specs, check_vma=False
    )
```

```python
import functools

import jax
import jax.numpy as jnp
from jax import lax
from jax.experimental import pallas as pl
from jax.experimental.pallas import tpu as pltpu
from jax.sharding import Mesh
from jax.sharding import PartitionSpec as P

BLOCK = 64
LANES = 128
SUB = 8
DIGIT = 256
CORES = 2
STEP = 64

F32 = jnp.float32
BF16 = jnp.bfloat16


def near(x):
    return pltpu.with_memory_space_constraint(x, pltpu.VMEM)


def far(x):
    return pltpu.with_memory_space_constraint(x, pltpu.HBM)


def pool_kernel(
    lens_hbm, ids_hbm, hidden, slots, gain_hbm, head, out, head_out, buf, weight, acc, slot_rows, gain,
    lens, ids, items, sems, slot_sem, side_sems, *, owners, peers, lists_own, capacity,
):
    passes, length, width = hidden.shape
    group = ids.shape[0]
    steps = length // STEP
    tiles = width // LANES
    per = tiles // owners
    pairs = -(-passes // 2)

    def chunk_copy(p, c):
        return pltpu.make_async_copy(
            hidden.at[p, pl.ds(c * STEP, STEP)], buf.at[p * steps + c], sems.at[p * steps + c]
        )

    def slot_copy(g):
        return pltpu.make_async_copy(
            slots.at[pl.ds(lax.div(ids[g], LANES), 1)], slot_rows.at[pl.ds(g, 1)], slot_sem
        )

    side = [
        pltpu.make_async_copy(source, target, side_sems.at[n])
        for n, (source, target) in enumerate(
            ((lens_hbm, lens), (ids_hbm, ids), (gain_hbm, gain), (head, head_out))
        )
    ]
    side[0].start()
    side[1].start()
    for p in range(passes):
        chunk_copy(p, 0).start()
        items[p] = p * steps
    side[0].wait()
    count = jnp.int32(passes)
    for c in range(1, steps):
        for p in range(passes):
            needed = lens[p] > c * STEP

            @pl.when(needed)
            def _():
                chunk_copy(p, c).start()
                items[count] = p * steps + c

            count = count + needed.astype(jnp.int32)
    side[1].wait()
    for g in range(group):
        slot_copy(g).start()
    side[2].start()
    side[3].start()

    def zero(p, _):
        acc[p] = jnp.zeros((SUB, width), F32)
        return 0

    lax.fori_loop(0, passes, zero, 0)

    def arrive(k):
        item = items[k]
        pltpu.make_async_copy(
            hidden.at[0, pl.ds(0, STEP)], buf.at[item], sems.at[item]
        ).wait()

    def weigh(k):
        item = items[k]
        p = lax.div(item, steps)
        start = lax.rem(item, steps) * STEP
        size = lens[p]
        for s in range(0, STEP, SUB):
            x = buf[item, s : s + SUB, :]
            x = x * x
            x = (x[:, : width // 2] + x[:, width // 2 :]).astype(F32)
            total = x[:, :LANES]
            for t in range(LANES, width // 2, LANES):
                total = total + x[:, t : t + LANES]
            square = jnp.sum(total, axis=1, keepdims=True)
            token = lax.broadcasted_iota(jnp.int32, (SUB, 1), 0) + (start + s)
            value = jnp.where(token < size, lax.rsqrt(square * (1.0 / width) + 1e-05), 0.0)
            weight[lax.rem(k, 2), s : s + SUB, :] = jnp.broadcast_to(value, (SUB, 2 * LANES)).astype(BF16)

    def add(k):
        item = items[k]
        p = lax.div(item, steps)
        slot = lax.rem(k, 2)
        pair = 2 * LANES
        for t in range(0, width, pair):
            total = None
            for s in range(0, STEP, 2 * SUB):
                x = buf[item, s : s + SUB, t : t + pair] * weight[slot, s : s + SUB, :]
                e = s + SUB
                x = x + buf[item, e : e + SUB, t : t + pair] * weight[slot, e : e + SUB, :]
                x = x.astype(F32)
                total = x if total is None else total + x
            acc[p, :, t : t + pair] += total

    arrive(0)
    weigh(jnp.int32(0))

    def body(k, _):
        arrive(k + 1)
        add(k)
        weigh(k + 1)
        return 0

    lax.fori_loop(0, count - 1, body, 0)
    for n in (2, 3):
        side[n].wait()
    pltpu.make_async_copy(
        slots.at[pl.ds(0, group)], slot_rows.at[pl.ds(0, group)], slot_sem
    ).wait()
    add(count - 1)

    shape = (-(-group // SUB) * SUB, LANES)
    sub = lax.broadcasted_iota(jnp.int32, (SUB, LANES), 0)
    blocks = []
    for start in range(0, shape[0], SUB):
        block = jnp.zeros((SUB, LANES), jnp.int32)
        for g in range(start, min(start + SUB, group)):
            block = jnp.where(sub == g - start, lax.rem(ids[g], LANES), block)
        blocks.append(block)
    column = jnp.concatenate(blocks, axis=0)
    line = lax.broadcasted_iota(jnp.int32, shape, 0)
    lane = lax.broadcasted_iota(jnp.int32, shape, 1)
    picked = jnp.where((lane == column) & (line < group), slot_rows[...], 0).astype(F32)
    slot = jnp.sum(picked, axis=1, keepdims=True).astype(jnp.int32)
    slot = jnp.broadcast_to(slot, shape)
    owner = lax.div(slot, lists_own)
    local = slot - owner * lists_own
    high = lax.div(local, DIGIT)
    low = local - high * DIGIT
    owner_line = jnp.sum(jnp.where(line == lane, owner.astype(F32), 0.0), axis=0, keepdims=True)
    earlier = (jnp.broadcast_to(owner_line, shape) == owner.astype(F32)) & (lane < line)
    rank = jnp.sum(jnp.where(earlier, 1.0, 0.0), axis=1, keepdims=True).astype(jnp.int32)
    rank = jnp.broadcast_to(rank, shape)
    peer = jnp.zeros(shape, jnp.int32)
    for j in range(1, peers):
        peer = peer + (line >= j * passes).astype(jnp.int32)
    place = line + peer * (SUB - passes) + 1
    entry = jnp.where(lane == rank, high, 0)
    entry = jnp.where(lane == rank + capacity, low, entry)
    entry = jnp.where(lane == rank + 2 * capacity, place, entry)
    entry = jnp.where((rank < capacity) & (line < group), entry, 0).astype(F32)

    inverse = jnp.zeros((SUB, LANES), F32)
    for p in range(passes):
        inverse = jnp.where(sub == p, lens[p].astype(F32), inverse)
    inverse = jnp.where(sub < passes, 1.0 / jnp.maximum(inverse, 1.0), 0.0)
    for o in range(owners):
        info = jnp.sum(jnp.where(owner == o, entry, 0.0), axis=0, keepdims=True)
        for q in range(per):
            t = o * per + q
            cols = slice(t * LANES, (t + 1) * LANES)
            parts = [acc[p, :, cols] if p < passes else None for p in range(SUB)]
            bit = SUB // 2
            while bit:
                merged = []
                for n in range(bit):
                    a, b = parts[n], parts[n + bit]
                    if a is None:
                        merged.append(None)
                    elif b is None:
                        merged.append(jnp.where((sub & bit) == 0, a + pltpu.roll(a, SUB - bit, 0), 0.0))
                    else:
                        first = jnp.where((sub & bit) == 0, a, b)
                        second = jnp.where((sub & bit) == 0, b, a)
                        if bit * 2 == SUB:
                            merged.append(first + pltpu.roll(second, bit, 0))
                        else:
                            up = pltpu.roll(second, SUB - bit, 0)
                            down = pltpu.roll(second, bit, 0)
                            merged.append(first + jnp.where((sub & bit) == 0, up, down))
                parts = merged
                bit //= 2
            tile = parts[0] * gain[t : t + 1].astype(F32) * inverse
            for n in range(pairs):
                piece = tile[2 * n : 2 * n + 2].astype(BF16)
                at = (q * pairs + n) * LANES
                for j in range(peers):
                    out[o * peers + j, :, at : at + LANES] = piece
        info = jnp.broadcast_to(info, (2, LANES)).astype(BF16)
        for j in range(peers):
            out[o * peers + j, :, per * pairs * LANES :] = info


def project_kernel(
    got, head, cents, rotation, own, other, rotation_out, info_v, info_s, rows_in, info_sem, row_sem,
    turn_sem,
    *, owners, peers, passes, capacity,
):
    width = head.shape[1]
    lists_own = cents.shape[0]
    pairs = -(-passes // 2)
    per = (got.shape[2] // LANES - 1) // pairs
    wide = peers * SUB
    group = peers * passes
    half = owners // CORES * group
    core = lax.axis_index("core")
    col = pl.multiple_of(lax.axis_index("mp") * width, LANES)

    def final_row(o, at):
        peer = lax.div(at, SUB)
        chip = lax.div(o, CORES)
        away = jnp.where(o - chip * CORES == core, 0, half)
        return away + chip * group + peer * passes + (at - peer * SUB)

    tail = per * pairs * LANES
    lines = [got[o * peers, :, tail:].astype(F32)[0:1] for o in range(owners)]
    lines += [jnp.zeros((1, LANES), F32)] * (info_v.shape[1] - owners)
    info = jnp.concatenate(lines, axis=0).astype(jnp.int32)
    row = info * DIGIT + pltpu.roll(info, LANES - capacity, 1)
    row = jnp.clip(row, 0, lists_own - 1)
    place = pltpu.roll(info, LANES - 2 * capacity, 1)
    first = lax.div(row, SUB)
    real = (place > 0) & (place <= wide)
    info_v[0] = first
    info_v[1] = row - first * SUB
    info_v[2] = jnp.where(
        real,
        final_row(lax.broadcasted_iota(jnp.int32, info.shape, 0), jnp.where(real, place - 1, 0)),
        -1,
    )
    info_copy = pltpu.make_async_copy(info_v, info_s, info_sem)
    info_copy.start()
    entries = [(o, k) for o in range(owners) for k in range(capacity)]
    for n, (o, k) in enumerate(entries):
        pltpu.make_async_copy(
            cents.at[pl.ds(pl.multiple_of(first[o, k] * SUB, SUB), SUB), pl.ds(col, width)],
            rows_in.at[n],
            row_sem,
        ).start()
    turn_copy = pltpu.make_async_copy(rotation, rotation_out, turn_sem)
    turn_copy.start()
    info_copy.wait()
    lane = lax.broadcasted_iota(jnp.int32, (1, LANES), 1)
    spots = lax.broadcasted_iota(jnp.int32, (CORES * half, LANES), 0)
    share = LANES // SUB
    chosen = []
    for start in range(0, len(entries), share):
        target = jnp.full((1, LANES), -1, jnp.int32)
        for m, (o, k) in enumerate(entries[start : start + share]):
            target = jnp.where(lane == m * SUB + info_s[1, o, k], info_s[2, o, k], target)
        chosen.append(jnp.where(spots == target, -1.0, 0.0).astype(BF16))
    depth = len(entries) * SUB
    chosen = jnp.concatenate(chosen, axis=1)[:, :depth]
    sources = owners * peers
    depth_in = pairs * sources * 2
    order = []
    for start in range(0, depth_in, LANES):
        at = lane + start
        pair = lax.div(at, sources * 2)
        at = at - pair * sources * 2
        source = lax.div(at, 2)
        p = pair * 2 + at - source * 2
        o = lax.div(source, peers)
        target = jnp.where(p < passes, final_row(o, (source - o * peers) * SUB + p), -1)
        order.append(jnp.where(spots == target, 1.0, 0.0).astype(BF16))
    order = jnp.concatenate(order, axis=1)[:, :depth_in]
    x = jnp.concatenate(
        [
            jnp.concatenate(
                [
                    got[:, :, (q * pairs + n) * LANES : (q * pairs + n + 1) * LANES].reshape(
                        sources * 2, LANES
                    )
                    for q in range(per)
                ],
                axis=1,
            )
            for n in range(pairs)
        ],
        axis=0,
    )
    x = jnp.dot(order, x, preferred_element_type=F32).astype(BF16)
    total = jnp.dot(x, head[...], preferred_element_type=F32)
    pltpu.make_async_copy(rows_in, rows_in, row_sem).wait()
    total = total + jnp.dot(
        chosen, rows_in[...].reshape(depth, width), preferred_element_type=F32
    )
    own[...] = total[:half]
    other[...] = total[half:].astype(BF16)
    turn_copy.wait()


def rotate_kernel(own, other, rotation, out, *, peers):
    group = out.shape[1]
    width = out.shape[2]
    resid = (own[...] + other[...].astype(F32)).astype(BF16)
    for j in range(peers):
        y = jnp.dot(
            resid, rotation[:, j * width : (j + 1) * width], preferred_element_type=F32
        ).astype(BF16)
        for c in range(resid.shape[0] // group):
            out[c * peers + j] = y[c * group : (c + 1) * group]


def quantize_kernel(parts, codes_hbm, scales_hbm, codes, scales, sems):
    total = parts[0].astype(F32)
    for s in range(1, parts.shape[0]):
        total = total + parts[s].astype(F32)
    group, width = total.shape
    lane = lax.broadcasted_iota(jnp.int32, (group, LANES), 1)
    table = jnp.zeros((group, LANES), F32)
    for t in range(width // LANES):
        x = total[:, t * LANES : (t + 1) * LANES]
        size = jnp.abs(x)
        spread = jnp.zeros((group, LANES), F32)
        for b in range(LANES // BLOCK):
            inside = (lane >= b * BLOCK) & (lane < (b + 1) * BLOCK)
            top = jnp.max(jnp.where(inside, size, 0.0), axis=1, keepdims=True) + 1e-06
            spread = jnp.where(inside, top, spread)
            table = jnp.where(lane == t * (LANES // BLOCK) + b, top, table)
        codes[:, t * LANES : (t + 1) * LANES] = (x / spread).astype(BF16)
    copies = [
        pltpu.make_async_copy(codes, codes_hbm, sems.at[0]),
        pltpu.make_async_copy(scales, scales_hbm, sems.at[1]),
    ]
    copies[0].start()
    scales[...] = table.T[: scales.shape[0]].astype(BF16)
    copies[1].start()
    for copy in copies:
        copy.wait()


def pool_call(lengths, list_ids, hidden, list_slot, gain, head, *, owners, peers, lists_own):
    passes, length, width = hidden.shape
    assert passes < SUB and length % STEP == 0
    group = list_ids.shape[0]
    capacity = max(2, 2 * group // owners)
    per = width // LANES // owners
    steps = length // STEP
    padded = -(-group // SUB) * SUB
    vmem = pl.BlockSpec(memory_space=pltpu.VMEM)
    hbm = pl.BlockSpec(memory_space=pl.ANY)
    return pl.pallas_call(
        functools.partial(
            pool_kernel, owners=owners, peers=peers, lists_own=lists_own, capacity=capacity
        ),
        out_shape=(
            pltpu.VMEM((owners * peers, 2, (per * -(-passes // 2) + 1) * LANES), BF16),
            pltpu.VMEM(head.shape, BF16),
        ),
        in_specs=[hbm] * 6,
        out_specs=(vmem, vmem),
        scratch_shapes=[
            pltpu.VMEM((passes * steps, STEP, width), BF16),
            pltpu.VMEM((2, STEP, 2 * LANES), BF16),
            pltpu.VMEM((passes, SUB, width), F32),
            pltpu.VMEM((padded, LANES), jnp.int32),
            pltpu.VMEM((width // LANES, LANES), BF16),
            pltpu.SMEM((passes,), jnp.int32),
            pltpu.SMEM((group,), jnp.int32),
            pltpu.SMEM((passes * steps,), jnp.int32),
            pltpu.SemaphoreType.DMA((passes * steps,)),
            pltpu.SemaphoreType.DMA,
            pltpu.SemaphoreType.DMA((4,)),
        ],
        compiler_params=pltpu.CompilerParams(vmem_limit_bytes=hidden.size * 2 + 6 * 2**20),
        name="pool",
    )(
        far(lengths), far(list_ids), far(hidden), far(list_slot.reshape(-1, LANES)),
        far(gain.reshape(-1, LANES)), far(head),
    )


def per_device(hidden, lengths, list_ids, gain, head, list_slot, centroids, rotation):
    passes, length, width = hidden.shape
    owners = lax.axis_size("chip") * lax.axis_size("core")
    peers = lax.axis_size("mp")
    group = list_ids.shape[0]
    lists_own = centroids.shape[0]
    capacity = max(2, 2 * group // owners)
    cols = head.shape[1]
    lead = -(-owners // SUB) * SUB
    vmem = pl.BlockSpec(memory_space=pltpu.VMEM)
    hbm = pl.BlockSpec(memory_space=pl.ANY)
    blocks, head = pool_call(
        lengths, list_ids, hidden, list_slot, gain, head,
        owners=owners, peers=peers, lists_own=lists_own,
    )
    got = lax.all_to_all(blocks, ("chip", "core", "mp"), 0, 0, tiled=True)
    half = owners // CORES * group
    own, other, rotation = pl.pallas_call(
        functools.partial(
            project_kernel, owners=owners, peers=peers, passes=passes, capacity=capacity
        ),
        out_shape=(
            pltpu.VMEM((half, cols), F32),
            pltpu.VMEM((half, cols), BF16),
            pltpu.VMEM(rotation.shape, BF16),
        ),
        in_specs=[vmem, vmem, hbm, hbm],
        out_specs=(vmem, vmem, vmem),
        scratch_shapes=[
            pltpu.VMEM((3, lead, LANES), jnp.int32),
            pltpu.SMEM((3, lead, LANES), jnp.int32),
            pltpu.VMEM((owners * capacity, SUB, cols), BF16),
            pltpu.SemaphoreType.DMA,
            pltpu.SemaphoreType.DMA,
            pltpu.SemaphoreType.DMA,
        ],
        compiler_params=pltpu.CompilerParams(vmem_limit_bytes=8 * 2**20),
        name="project",
    )(near(got), near(head), far(centroids), far(rotation))
    other = lax.ppermute(other, "core", [(c, (c + 1) % CORES) for c in range(CORES)])
    parts = pl.pallas_call(
        functools.partial(rotate_kernel, peers=peers),
        out_shape=pltpu.VMEM((owners // CORES * peers, group, cols), BF16),
        in_specs=[vmem, vmem, vmem],
        out_specs=vmem,
        compiler_params=pltpu.CompilerParams(vmem_limit_bytes=8 * 2**20),
        name="rotate",
    )(near(own), near(other), near(rotation))
    parts = lax.all_to_all(parts, ("chip", "mp"), 0, 0, tiled=True)
    codes, scales = pl.pallas_call(
        quantize_kernel,
        out_shape=(
            jax.ShapeDtypeStruct((group, cols), BF16),
            jax.ShapeDtypeStruct((cols // BLOCK, group), BF16),
        ),
        in_specs=[vmem],
        out_specs=(hbm, hbm),
        scratch_shapes=[
            pltpu.VMEM((group, cols), BF16),
            pltpu.VMEM((cols // BLOCK, group), BF16),
            pltpu.SemaphoreType.DMA((2,)),
        ],
        compiler_params=pltpu.CompilerParams(vmem_limit_bytes=8 * 2**20),
        name="quantize",
    )(near(parts))
    return codes, scales.T


def solution(mesh):
    dp, mp = mesh.shape["dp"], mesh.shape["mp"]
    split = Mesh(mesh.devices.reshape(dp // CORES, CORES, mp), ("chip", "core", "mp"))
    rows = ("chip", "core")
    in_specs = (
        P(("chip", "core", "mp"), None, None),
        P(("chip", "core", "mp")),
        P(rows),
        P(),
        P(rows, "mp"),
        P(),
        P(rows, None),
        P("mp", None),
    )
    out_specs = (P(rows, "mp"), P(rows, "mp"))
    return jax.shard_map(
        per_device, mesh=split, in_specs=in_specs, out_specs=out_specs, check_vma=False
    )
```

```python
import functools

import jax
import jax.numpy as jnp
from jax import lax
from jax.experimental import pallas as pl
from jax.experimental.pallas import tpu as pltpu
from jax.sharding import Mesh
from jax.sharding import PartitionSpec as P

BLOCK = 64
LANES = 128
SUB = 8
DIGIT = 256
CORES = 2
STEP = 64

F32 = jnp.float32
BF16 = jnp.bfloat16


def near(x):
    return pltpu.with_memory_space_constraint(x, pltpu.VMEM)


def far(x):
    return pltpu.with_memory_space_constraint(x, pltpu.HBM)


def pool_kernel(
    lens_hbm, ids_hbm, hidden, slots, gain_hbm, head, out, head_out, buf, weight, acc, slot_rows, gain,
    lens, ids, items, sems, slot_sem, side_sems, *, owners, peers, lists_own, capacity,
):
    passes, length, width = hidden.shape
    group = ids.shape[0]
    steps = length // STEP
    tiles = width // LANES
    per = tiles // owners
    pairs = -(-passes // 2)

    def chunk_copy(p, c):
        return pltpu.make_async_copy(
            hidden.at[p, pl.ds(c * STEP, STEP)], buf.at[p * steps + c], sems.at[p * steps + c]
        )

    def slot_copy(g):
        return pltpu.make_async_copy(
            slots.at[pl.ds(lax.div(ids[g], LANES), 1)], slot_rows.at[pl.ds(g, 1)], slot_sem
        )

    side = [
        pltpu.make_async_copy(source, target, side_sems.at[n])
        for n, (source, target) in enumerate(
            ((lens_hbm, lens), (ids_hbm, ids), (gain_hbm, gain), (head, head_out))
        )
    ]
    side[0].start()
    side[1].start()
    for p in range(passes):
        chunk_copy(p, 0).start()
        items[p] = p * steps
    side[1].wait()
    for g in range(group):
        slot_copy(g).start()
    side[0].wait()
    count = jnp.int32(passes)
    for c in range(1, steps):
        for p in range(passes):
            needed = lens[p] > c * STEP

            @pl.when(needed)
            def _():
                chunk_copy(p, c).start()
                items[count] = p * steps + c

            count = count + needed.astype(jnp.int32)
    side[2].start()
    side[3].start()

    def zero(p, _):
        acc[p] = jnp.zeros((SUB, width), F32)
        return 0

    lax.fori_loop(0, passes, zero, 0)

    def arrive(k):
        item = items[k]
        pltpu.make_async_copy(
            hidden.at[0, pl.ds(0, STEP)], buf.at[item], sems.at[item]
        ).wait()

    def weigh(k):
        item = items[k]
        p = lax.div(item, steps)
        start = lax.rem(item, steps) * STEP
        size = lens[p]
        for s in range(0, STEP, SUB):
            x = buf[item, s : s + SUB, :]
            x = x * x
            x = (x[:, : width // 2] + x[:, width // 2 :]).astype(F32)
            total = x[:, :LANES]
            for t in range(LANES, width // 2, LANES):
                total = total + x[:, t : t + LANES]
            square = jnp.sum(total, axis=1, keepdims=True)
            token = lax.broadcasted_iota(jnp.int32, (SUB, 1), 0) + (start + s)
            value = jnp.where(token < size, lax.rsqrt(square * (1.0 / width) + 1e-05), 0.0)
            weight[lax.rem(k, 2), s : s + SUB, :] = jnp.broadcast_to(value, (SUB, 2 * LANES)).astype(BF16)

    def add(k):
        item = items[k]
        p = lax.div(item, steps)
        slot = lax.rem(k, 2)
        pair = 2 * LANES
        for t in range(0, width, pair):
            total = None
            for s in range(0, STEP, 2 * SUB):
                x = buf[item, s : s + SUB, t : t + pair] * weight[slot, s : s + SUB, :]
                e = s + SUB
                x = x + buf[item, e : e + SUB, t : t + pair] * weight[slot, e : e + SUB, :]
                x = x.astype(F32)
                total = x if total is None else total + x
            acc[p, :, t : t + pair] += total

    arrive(0)
    weigh(jnp.int32(0))

    def body(k, _):
        arrive(k + 1)
        add(k)
        weigh(k + 1)
        return 0

    lax.fori_loop(0, count - 1, body, 0)
    for n in (2, 3):
        side[n].wait()
    pltpu.make_async_copy(
        slots.at[pl.ds(0, group)], slot_rows.at[pl.ds(0, group)], slot_sem
    ).wait()
    add(count - 1)

    shape = (-(-group // SUB) * SUB, LANES)
    sub = lax.broadcasted_iota(jnp.int32, (SUB, LANES), 0)
    blocks = []
    for start in range(0, shape[0], SUB):
        block = jnp.zeros((SUB, LANES), jnp.int32)
        for g in range(start, min(start + SUB, group)):
            block = jnp.where(sub == g - start, lax.rem(ids[g], LANES), block)
        blocks.append(block)
    column = jnp.concatenate(blocks, axis=0)
    line = lax.broadcasted_iota(jnp.int32, shape, 0)
    lane = lax.broadcasted_iota(jnp.int32, shape, 1)
    picked = jnp.where((lane == column) & (line < group), slot_rows[...], 0).astype(F32)
    slot = jnp.sum(picked, axis=1, keepdims=True).astype(jnp.int32)
    slot = jnp.broadcast_to(slot, shape)
    owner = lax.div(slot, lists_own)
    local = slot - owner * lists_own
    high = lax.div(local, DIGIT)
    low = local - high * DIGIT
    owner_line = jnp.sum(jnp.where(line == lane, owner.astype(F32), 0.0), axis=0, keepdims=True)
    earlier = (jnp.broadcast_to(owner_line, shape) == owner.astype(F32)) & (lane < line)
    rank = jnp.sum(jnp.where(earlier, 1.0, 0.0), axis=1, keepdims=True).astype(jnp.int32)
    rank = jnp.broadcast_to(rank, shape)
    peer = jnp.zeros(shape, jnp.int32)
    for j in range(1, peers):
        peer = peer + (line >= j * passes).astype(jnp.int32)
    place = line + peer * (SUB - passes) + 1
    entry = jnp.where(lane == rank, high, 0)
    entry = jnp.where(lane == rank + capacity, low, entry)
    entry = jnp.where(lane == rank + 2 * capacity, place, entry)
    entry = jnp.where((rank < capacity) & (line < group), entry, 0).astype(F32)

    inverse = jnp.zeros((SUB, LANES), F32)
    for p in range(passes):
        inverse = jnp.where(sub == p, lens[p].astype(F32), inverse)
    inverse = jnp.where(sub < passes, 1.0 / jnp.maximum(inverse, 1.0), 0.0)
    for o in range(owners):
        info = jnp.sum(jnp.where(owner == o, entry, 0.0), axis=0, keepdims=True)
        for q in range(per):
            t = o * per + q
            cols = slice(t * LANES, (t + 1) * LANES)
            parts = [acc[p, :, cols] if p < passes else None for p in range(SUB)]
            bit = SUB // 2
            while bit:
                merged = []
                for n in range(bit):
                    a, b = parts[n], parts[n + bit]
                    if a is None:
                        merged.append(None)
                    elif b is None:
                        merged.append(jnp.where((sub & bit) == 0, a + pltpu.roll(a, SUB - bit, 0), 0.0))
                    else:
                        first = jnp.where((sub & bit) == 0, a, b)
                        second = jnp.where((sub & bit) == 0, b, a)
                        if bit * 2 == SUB:
                            merged.append(first + pltpu.roll(second, bit, 0))
                        else:
                            up = pltpu.roll(second, SUB - bit, 0)
                            down = pltpu.roll(second, bit, 0)
                            merged.append(first + jnp.where((sub & bit) == 0, up, down))
                parts = merged
                bit //= 2
            tile = parts[0] * gain[t : t + 1].astype(F32) * inverse
            for n in range(pairs):
                piece = tile[2 * n : 2 * n + 2].astype(BF16)
                at = (q * pairs + n) * LANES
                for j in range(peers):
                    out[o * peers + j, :, at : at + LANES] = piece
        info = jnp.broadcast_to(info, (2, LANES)).astype(BF16)
        for j in range(peers):
            out[o * peers + j, :, per * pairs * LANES :] = info


def project_kernel(
    got, head, cents, rotation, own, other, rotation_out, info_v, info_s, rows_in, info_sem, row_sem,
    turn_sem,
    *, owners, peers, passes, capacity,
):
    width = head.shape[1]
    lists_own = cents.shape[0]
    pairs = -(-passes // 2)
    per = (got.shape[2] // LANES - 1) // pairs
    wide = peers * SUB
    group = peers * passes
    half = owners // CORES * group
    core = lax.axis_index("core")
    col = pl.multiple_of(lax.axis_index("mp") * width, LANES)

    def final_row(o, at):
        peer = lax.div(at, SUB)
        chip = lax.div(o, CORES)
        away = jnp.where(o - chip * CORES == core, 0, half)
        return away + chip * group + peer * passes + (at - peer * SUB)

    tail = per * pairs * LANES
    lines = [got[o * peers, :, tail:].astype(F32)[0:1] for o in range(owners)]
    lines += [jnp.zeros((1, LANES), F32)] * (info_v.shape[1] - owners)
    info = jnp.concatenate(lines, axis=0).astype(jnp.int32)
    row = info * DIGIT + pltpu.roll(info, LANES - capacity, 1)
    row = jnp.clip(row, 0, lists_own - 1)
    place = pltpu.roll(info, LANES - 2 * capacity, 1)
    first = lax.div(row, SUB)
    real = (place > 0) & (place <= wide)
    info_v[0] = first
    info_v[1] = row - first * SUB
    info_v[2] = jnp.where(
        real,
        final_row(lax.broadcasted_iota(jnp.int32, info.shape, 0), jnp.where(real, place - 1, 0)),
        -1,
    )
    info_copy = pltpu.make_async_copy(info_v, info_s, info_sem)
    info_copy.start()
    entries = [(o, k) for o in range(owners) for k in range(capacity)]
    for n, (o, k) in enumerate(entries):
        pltpu.make_async_copy(
            cents.at[pl.ds(pl.multiple_of(first[o, k] * SUB, SUB), SUB), pl.ds(col, width)],
            rows_in.at[n],
            row_sem,
        ).start()
    turn_copy = pltpu.make_async_copy(rotation, rotation_out, turn_sem)
    turn_copy.start()
    info_copy.wait()
    lane = lax.broadcasted_iota(jnp.int32, (1, LANES), 1)
    spots = lax.broadcasted_iota(jnp.int32, (CORES * half, LANES), 0)
    share = LANES // SUB
    chosen = []
    for start in range(0, len(entries), share):
        target = jnp.full((1, LANES), -1, jnp.int32)
        for m, (o, k) in enumerate(entries[start : start + share]):
            target = jnp.where(lane == m * SUB + info_s[1, o, k], info_s[2, o, k], target)
        chosen.append(jnp.where(spots == target, -1.0, 0.0).astype(BF16))
    depth = len(entries) * SUB
    chosen = jnp.concatenate(chosen, axis=1)[:, :depth]
    sources = owners * peers
    depth_in = pairs * sources * 2
    order = []
    for start in range(0, depth_in, LANES):
        at = lane + start
        pair = lax.div(at, sources * 2)
        at = at - pair * sources * 2
        source = lax.div(at, 2)
        p = pair * 2 + at - source * 2
        o = lax.div(source, peers)
        target = jnp.where(p < passes, final_row(o, (source - o * peers) * SUB + p), -1)
        order.append(jnp.where(spots == target, 1.0, 0.0).astype(BF16))
    order = jnp.concatenate(order, axis=1)[:, :depth_in]
    x = jnp.concatenate(
        [
            jnp.concatenate(
                [
                    got[:, :, (q * pairs + n) * LANES : (q * pairs + n + 1) * LANES].reshape(
                        sources * 2, LANES
                    )
                    for q in range(per)
                ],
                axis=1,
            )
            for n in range(pairs)
        ],
        axis=0,
    )
    x = jnp.dot(order, x, preferred_element_type=F32).astype(BF16)
    total = jnp.dot(x, head[...], preferred_element_type=F32)
    pltpu.make_async_copy(rows_in, rows_in, row_sem).wait()
    total = total + jnp.dot(
        chosen, rows_in[...].reshape(depth, width), preferred_element_type=F32
    )
    own[...] = total[:half]
    other[...] = total[half:].astype(BF16)
    turn_copy.wait()


def rotate_kernel(own, other, rotation, out, *, peers):
    group = out.shape[1]
    width = out.shape[2]
    resid = (own[...] + other[...].astype(F32)).astype(BF16)
    for j in range(peers):
        y = jnp.dot(
            resid, rotation[:, j * width : (j + 1) * width], preferred_element_type=F32
        ).astype(BF16)
        for c in range(resid.shape[0] // group):
            out[c * peers + j] = y[c * group : (c + 1) * group]


def quantize_kernel(parts, codes_hbm, scales_hbm, codes, scales, sems):
    total = parts[0].astype(F32)
    for s in range(1, parts.shape[0]):
        total = total + parts[s].astype(F32)
    group, width = total.shape
    lane = lax.broadcasted_iota(jnp.int32, (group, LANES), 1)
    table = jnp.zeros((group, LANES), F32)
    for t in range(width // LANES):
        x = total[:, t * LANES : (t + 1) * LANES]
        size = jnp.abs(x)
        spread = jnp.zeros((group, LANES), F32)
        for b in range(LANES // BLOCK):
            inside = (lane >= b * BLOCK) & (lane < (b + 1) * BLOCK)
            top = jnp.max(jnp.where(inside, size, 0.0), axis=1, keepdims=True) + 1e-06
            spread = jnp.where(inside, top, spread)
            table = jnp.where(lane == t * (LANES // BLOCK) + b, top, table)
        codes[:, t * LANES : (t + 1) * LANES] = (x / spread).astype(BF16)
    copies = [
        pltpu.make_async_copy(codes, codes_hbm, sems.at[0]),
        pltpu.make_async_copy(scales, scales_hbm, sems.at[1]),
    ]
    copies[0].start()
    scales[...] = table.T[: scales.shape[0]].astype(BF16)
    copies[1].start()
    for copy in copies:
        copy.wait()


def pool_call(lengths, list_ids, hidden, list_slot, gain, head, *, owners, peers, lists_own):
    passes, length, width = hidden.shape
    assert passes < SUB and length % STEP == 0
    group = list_ids.shape[0]
    capacity = max(2, 2 * group // owners)
    per = width // LANES // owners
    steps = length // STEP
    padded = -(-group // SUB) * SUB
    vmem = pl.BlockSpec(memory_space=pltpu.VMEM)
    hbm = pl.BlockSpec(memory_space=pl.ANY)
    return pl.pallas_call(
        functools.partial(
            pool_kernel, owners=owners, peers=peers, lists_own=lists_own, capacity=capacity
        ),
        out_shape=(
            pltpu.VMEM((owners * peers, 2, (per * -(-passes // 2) + 1) * LANES), BF16),
            pltpu.VMEM(head.shape, BF16),
        ),
        in_specs=[hbm] * 6,
        out_specs=(vmem, vmem),
        scratch_shapes=[
            pltpu.VMEM((passes * steps, STEP, width), BF16),
            pltpu.VMEM((2, STEP, 2 * LANES), BF16),
            pltpu.VMEM((passes, SUB, width), F32),
            pltpu.VMEM((padded, LANES), jnp.int32),
            pltpu.VMEM((width // LANES, LANES), BF16),
            pltpu.SMEM((passes,), jnp.int32),
            pltpu.SMEM((group,), jnp.int32),
            pltpu.SMEM((passes * steps,), jnp.int32),
            pltpu.SemaphoreType.DMA((passes * steps,)),
            pltpu.SemaphoreType.DMA,
            pltpu.SemaphoreType.DMA((4,)),
        ],
        compiler_params=pltpu.CompilerParams(vmem_limit_bytes=hidden.size * 2 + 6 * 2**20),
        name="pool",
    )(
        far(lengths), far(list_ids), far(hidden), far(list_slot.reshape(-1, LANES)),
        far(gain.reshape(-1, LANES)), far(head),
    )


def per_device(hidden, lengths, list_ids, gain, head, list_slot, centroids, rotation):
    passes, length, width = hidden.shape
    owners = lax.axis_size("chip") * lax.axis_size("core")
    peers = lax.axis_size("mp")
    group = list_ids.shape[0]
    lists_own = centroids.shape[0]
    capacity = max(2, 2 * group // owners)
    cols = head.shape[1]
    lead = -(-owners // SUB) * SUB
    vmem = pl.BlockSpec(memory_space=pltpu.VMEM)
    hbm = pl.BlockSpec(memory_space=pl.ANY)
    blocks, head = pool_call(
        lengths, list_ids, hidden, list_slot, gain, head,
        owners=owners, peers=peers, lists_own=lists_own,
    )
    got = lax.all_to_all(blocks, ("chip", "core", "mp"), 0, 0, tiled=True)
    half = owners // CORES * group
    own, other, rotation = pl.pallas_call(
        functools.partial(
            project_kernel, owners=owners, peers=peers, passes=passes, capacity=capacity
        ),
        out_shape=(
            pltpu.VMEM((half, cols), F32),
            pltpu.VMEM((half, cols), BF16),
            pltpu.VMEM(rotation.shape, BF16),
        ),
        in_specs=[vmem, vmem, hbm, hbm],
        out_specs=(vmem, vmem, vmem),
        scratch_shapes=[
            pltpu.VMEM((3, lead, LANES), jnp.int32),
            pltpu.SMEM((3, lead, LANES), jnp.int32),
            pltpu.VMEM((owners * capacity, SUB, cols), BF16),
            pltpu.SemaphoreType.DMA,
            pltpu.SemaphoreType.DMA,
            pltpu.SemaphoreType.DMA,
        ],
        compiler_params=pltpu.CompilerParams(vmem_limit_bytes=8 * 2**20),
        name="project",
    )(near(got), near(head), far(centroids), far(rotation))
    other = lax.ppermute(other, "core", [(c, (c + 1) % CORES) for c in range(CORES)])
    parts = pl.pallas_call(
        functools.partial(rotate_kernel, peers=peers),
        out_shape=pltpu.VMEM((owners // CORES * peers, group, cols), BF16),
        in_specs=[vmem, vmem, vmem],
        out_specs=vmem,
        compiler_params=pltpu.CompilerParams(vmem_limit_bytes=8 * 2**20),
        name="rotate",
    )(near(own), near(other), near(rotation))
    parts = lax.all_to_all(parts, ("chip", "mp"), 0, 0, tiled=True)
    codes, scales = pl.pallas_call(
        quantize_kernel,
        out_shape=(
            jax.ShapeDtypeStruct((group, cols), BF16),
            jax.ShapeDtypeStruct((cols // BLOCK, group), BF16),
        ),
        in_specs=[vmem],
        out_specs=(hbm, hbm),
        scratch_shapes=[
            pltpu.VMEM((group, cols), BF16),
            pltpu.VMEM((cols // BLOCK, group), BF16),
            pltpu.SemaphoreType.DMA((2,)),
        ],
        compiler_params=pltpu.CompilerParams(vmem_limit_bytes=8 * 2**20),
        name="quantize",
    )(near(parts))
    return codes, scales.T


def solution(mesh):
    dp, mp = mesh.shape["dp"], mesh.shape["mp"]
    split = Mesh(mesh.devices.reshape(dp // CORES, CORES, mp), ("chip", "core", "mp"))
    rows = ("chip", "core")
    in_specs = (
        P(("chip", "core", "mp"), None, None),
        P(("chip", "core", "mp")),
        P(rows),
        P(),
        P(rows, "mp"),
        P(),
        P(rows, None),
        P("mp", None),
    )
    out_specs = (P(rows, "mp"), P(rows, "mp"))
    return jax.shard_map(
        per_device, mesh=split, in_specs=in_specs, out_specs=out_specs, check_vma=False
    )
```

```python
import functools

import jax
import jax.numpy as jnp
from jax import lax
from jax.experimental import pallas as pl
from jax.experimental.pallas import tpu as pltpu
from jax.sharding import Mesh
from jax.sharding import PartitionSpec as P

BLOCK = 64
LANES = 128
SUB = 8
DIGIT = 256
CORES = 2
STEP = 64

F32 = jnp.float32
BF16 = jnp.bfloat16


def near(x):
    return pltpu.with_memory_space_constraint(x, pltpu.VMEM)


def far(x):
    return pltpu.with_memory_space_constraint(x, pltpu.HBM)


def pool_kernel(
    lens_hbm, ids_hbm, hidden, slots, gain_hbm, head, out, head_out, buf, weight, acc, slot_rows, gain,
    lens, ids, items, sems, slot_sem, side_sems, *, owners, peers, lists_own, capacity,
):
    passes, length, width = hidden.shape
    group = ids.shape[0]
    steps = length // STEP
    tiles = width // LANES
    per = tiles // owners
    pairs = -(-passes // 2)

    def chunk_copy(p, c):
        return pltpu.make_async_copy(
            hidden.at[p, pl.ds(c * STEP, STEP)], buf.at[p * steps + c], sems.at[p * steps + c]
        )

    def slot_copy(g):
        return pltpu.make_async_copy(
            slots.at[pl.ds(lax.div(ids[g], LANES), 1)], slot_rows.at[pl.ds(g, 1)], slot_sem
        )

    side = [
        pltpu.make_async_copy(source, target, side_sems.at[n])
        for n, (source, target) in enumerate(
            ((lens_hbm, lens), (ids_hbm, ids), (gain_hbm, gain), (head, head_out))
        )
    ]
    side[0].start()
    side[1].start()
    for p in range(passes):
        chunk_copy(p, 0).start()
        items[p] = p * steps
    side[0].wait()
    count = jnp.int32(passes)
    for c in range(1, steps):
        for p in range(passes):
            needed = lens[p] > c * STEP

            @pl.when(needed)
            def _():
                chunk_copy(p, c).start()
                items[count] = p * steps + c

            count = count + needed.astype(jnp.int32)
    side[1].wait()
    for g in range(group):
        slot_copy(g).start()
    side[2].start()
    side[3].start()

    def zero(p, _):
        acc[p] = jnp.zeros((SUB, width), F32)
        return 0

    lax.fori_loop(0, passes, zero, 0)

    def arrive(k):
        item = items[k]
        pltpu.make_async_copy(
            hidden.at[0, pl.ds(0, STEP)], buf.at[item], sems.at[item]
        ).wait()

    def weigh(k):
        item = items[k]
        p = lax.div(item, steps)
        start = lax.rem(item, steps) * STEP
        size = lens[p]
        for s in range(0, STEP, SUB):
            x = buf[item, s : s + SUB, :]
            x = x * x
            x = (x[:, : width // 2] + x[:, width // 2 :]).astype(F32)
            total = x[:, :LANES]
            for t in range(LANES, width // 2, LANES):
                total = total + x[:, t : t + LANES]
            square = jnp.sum(total, axis=1, keepdims=True)
            token = lax.broadcasted_iota(jnp.int32, (SUB, 1), 0) + (start + s)
            value = jnp.where(token < size, lax.rsqrt(square * (1.0 / width) + 1e-05), 0.0)
            weight[lax.rem(k, 2), s : s + SUB, :] = jnp.broadcast_to(value, (SUB, 2 * LANES)).astype(BF16)

    def add(k):
        item = items[k]
        p = lax.div(item, steps)
        slot = lax.rem(k, 2)
        pair = 2 * LANES
        for t in range(0, width, pair):
            total = None
            for s in range(0, STEP, 2 * SUB):
                x = buf[item, s : s + SUB, t : t + pair] * weight[slot, s : s + SUB, :]
                e = s + SUB
                x = x + buf[item, e : e + SUB, t : t + pair] * weight[slot, e : e + SUB, :]
                x = x.astype(F32)
                total = x if total is None else total + x
            acc[p, :, t : t + pair] += total

    arrive(0)
    weigh(jnp.int32(0))

    def body(k, _):
        add(k)
        arrive(k + 1)
        weigh(k + 1)
        return 0

    lax.fori_loop(0, count - 1, body, 0)
    for n in (2, 3):
        side[n].wait()
    pltpu.make_async_copy(
        slots.at[pl.ds(0, group)], slot_rows.at[pl.ds(0, group)], slot_sem
    ).wait()
    add(count - 1)

    shape = (-(-group // SUB) * SUB, LANES)
    sub = lax.broadcasted_iota(jnp.int32, (SUB, LANES), 0)
    blocks = []
    for start in range(0, shape[0], SUB):
        block = jnp.zeros((SUB, LANES), jnp.int32)
        for g in range(start, min(start + SUB, group)):
            block = jnp.where(sub == g - start, lax.rem(ids[g], LANES), block)
        blocks.append(block)
    column = jnp.concatenate(blocks, axis=0)
    line = lax.broadcasted_iota(jnp.int32, shape, 0)
    lane = lax.broadcasted_iota(jnp.int32, shape, 1)
    picked = jnp.where((lane == column) & (line < group), slot_rows[...], 0).astype(F32)
    slot = jnp.sum(picked, axis=1, keepdims=True).astype(jnp.int32)
    slot = jnp.broadcast_to(slot, shape)
    owner = lax.div(slot, lists_own)
    local = slot - owner * lists_own
    high = lax.div(local, DIGIT)
    low = local - high * DIGIT
    owner_line = jnp.sum(jnp.where(line == lane, owner.astype(F32), 0.0), axis=0, keepdims=True)
    earlier = (jnp.broadcast_to(owner_line, shape) == owner.astype(F32)) & (lane < line)
    rank = jnp.sum(jnp.where(earlier, 1.0, 0.0), axis=1, keepdims=True).astype(jnp.int32)
    rank = jnp.broadcast_to(rank, shape)
    peer = jnp.zeros(shape, jnp.int32)
    for j in range(1, peers):
        peer = peer + (line >= j * passes).astype(jnp.int32)
    place = line + peer * (SUB - passes) + 1
    entry = jnp.where(lane == rank, high, 0)
    entry = jnp.where(lane == rank + capacity, low, entry)
    entry = jnp.where(lane == rank + 2 * capacity, place, entry)
    entry = jnp.where((rank < capacity) & (line < group), entry, 0).astype(F32)

    inverse = jnp.zeros((SUB, LANES), F32)
    for p in range(passes):
        inverse = jnp.where(sub == p, lens[p].astype(F32), inverse)
    inverse = jnp.where(sub < passes, 1.0 / jnp.maximum(inverse, 1.0), 0.0)
    for o in range(owners):
        info = jnp.sum(jnp.where(owner == o, entry, 0.0), axis=0, keepdims=True)
        for q in range(per):
            t = o * per + q
            cols = slice(t * LANES, (t + 1) * LANES)
            parts = [acc[p, :, cols] if p < passes else None for p in range(SUB)]
            bit = SUB // 2
            while bit:
                merged = []
                for n in range(bit):
                    a, b = parts[n], parts[n + bit]
                    if a is None:
                        merged.append(None)
                    elif b is None:
                        merged.append(jnp.where((sub & bit) == 0, a + pltpu.roll(a, SUB - bit, 0), 0.0))
                    else:
                        first = jnp.where((sub & bit) == 0, a, b)
                        second = jnp.where((sub & bit) == 0, b, a)
                        if bit * 2 == SUB:
                            merged.append(first + pltpu.roll(second, bit, 0))
                        else:
                            up = pltpu.roll(second, SUB - bit, 0)
                            down = pltpu.roll(second, bit, 0)
                            merged.append(first + jnp.where((sub & bit) == 0, up, down))
                parts = merged
                bit //= 2
            tile = parts[0] * gain[t : t + 1].astype(F32) * inverse
            for n in range(pairs):
                piece = tile[2 * n : 2 * n + 2].astype(BF16)
                at = (q * pairs + n) * LANES
                for j in range(peers):
                    out[o * peers + j, :, at : at + LANES] = piece
        info = jnp.broadcast_to(info, (2, LANES)).astype(BF16)
        for j in range(peers):
            out[o * peers + j, :, per * pairs * LANES :] = info


def project_kernel(
    got, head, cents, rotation, own, other, rotation_out, info_v, info_s, rows_in, info_sem, row_sem,
    turn_sem,
    *, owners, peers, passes, capacity,
):
    width = head.shape[1]
    lists_own = cents.shape[0]
    pairs = -(-passes // 2)
    per = (got.shape[2] // LANES - 1) // pairs
    wide = peers * SUB
    group = peers * passes
    half = owners // CORES * group
    core = lax.axis_index("core")
    col = pl.multiple_of(lax.axis_index("mp") * width, LANES)

    def final_row(o, at):
        peer = lax.div(at, SUB)
        chip = lax.div(o, CORES)
        away = jnp.where(o - chip * CORES == core, 0, half)
        return away + chip * group + peer * passes + (at - peer * SUB)

    tail = per * pairs * LANES
    lines = [got[o * peers, :, tail:].astype(F32)[0:1] for o in range(owners)]
    lines += [jnp.zeros((1, LANES), F32)] * (info_v.shape[1] - owners)
    info = jnp.concatenate(lines, axis=0).astype(jnp.int32)
    row = info * DIGIT + pltpu.roll(info, LANES - capacity, 1)
    row = jnp.clip(row, 0, lists_own - 1)
    place = pltpu.roll(info, LANES - 2 * capacity, 1)
    first = lax.div(row, SUB)
    real = (place > 0) & (place <= wide)
    info_v[0] = first
    info_v[1] = row - first * SUB
    info_v[2] = jnp.where(
        real,
        final_row(lax.broadcasted_iota(jnp.int32, info.shape, 0), jnp.where(real, place - 1, 0)),
        -1,
    )
    info_copy = pltpu.make_async_copy(info_v, info_s, info_sem)
    info_copy.start()
    entries = [(o, k) for o in range(owners) for k in range(capacity)]
    for n, (o, k) in enumerate(entries):
        pltpu.make_async_copy(
            cents.at[pl.ds(pl.multiple_of(first[o, k] * SUB, SUB), SUB), pl.ds(col, width)],
            rows_in.at[n],
            row_sem,
        ).start()
    turn_copy = pltpu.make_async_copy(rotation, rotation_out, turn_sem)
    turn_copy.start()
    info_copy.wait()
    lane = lax.broadcasted_iota(jnp.int32, (1, LANES), 1)
    spots = lax.broadcasted_iota(jnp.int32, (CORES * half, LANES), 0)
    share = LANES // SUB
    chosen = []
    for start in range(0, len(entries), share):
        target = jnp.full((1, LANES), -1, jnp.int32)
        for m, (o, k) in enumerate(entries[start : start + share]):
            target = jnp.where(lane == m * SUB + info_s[1, o, k], info_s[2, o, k], target)
        chosen.append(jnp.where(spots == target, -1.0, 0.0).astype(BF16))
    depth = len(entries) * SUB
    chosen = jnp.concatenate(chosen, axis=1)[:, :depth]
    sources = owners * peers
    depth_in = pairs * sources * 2
    order = []
    for start in range(0, depth_in, LANES):
        at = lane + start
        pair = lax.div(at, sources * 2)
        at = at - pair * sources * 2
        source = lax.div(at, 2)
        p = pair * 2 + at - source * 2
        o = lax.div(source, peers)
        target = jnp.where(p < passes, final_row(o, (source - o * peers) * SUB + p), -1)
        order.append(jnp.where(spots == target, 1.0, 0.0).astype(BF16))
    order = jnp.concatenate(order, axis=1)[:, :depth_in]
    x = jnp.concatenate(
        [
            jnp.concatenate(
                [
                    got[:, :, (q * pairs + n) * LANES : (q * pairs + n + 1) * LANES].reshape(
                        sources * 2, LANES
                    )
                    for q in range(per)
                ],
                axis=1,
            )
            for n in range(pairs)
        ],
        axis=0,
    )
    x = jnp.dot(order, x, preferred_element_type=F32).astype(BF16)
    total = jnp.dot(x, head[...], preferred_element_type=F32)
    pltpu.make_async_copy(rows_in, rows_in, row_sem).wait()
    total = total + jnp.dot(
        chosen, rows_in[...].reshape(depth, width), preferred_element_type=F32
    )
    own[...] = total[:half]
    other[...] = total[half:].astype(BF16)
    turn_copy.wait()


def rotate_kernel(own, other, rotation, out, *, peers):
    group = out.shape[1]
    width = out.shape[2]
    resid = (own[...] + other[...].astype(F32)).astype(BF16)
    for j in range(peers):
        y = jnp.dot(
            resid, rotation[:, j * width : (j + 1) * width], preferred_element_type=F32
        ).astype(BF16)
        for c in range(resid.shape[0] // group):
            out[c * peers + j] = y[c * group : (c + 1) * group]


def quantize_kernel(parts, codes_hbm, scales_hbm, codes, scales, sems):
    total = parts[0].astype(F32)
    for s in range(1, parts.shape[0]):
        total = total + parts[s].astype(F32)
    group, width = total.shape
    lane = lax.broadcasted_iota(jnp.int32, (group, LANES), 1)
    table = jnp.zeros((group, LANES), F32)
    for t in range(width // LANES):
        x = total[:, t * LANES : (t + 1) * LANES]
        size = jnp.abs(x)
        spread = jnp.zeros((group, LANES), F32)
        for b in range(LANES // BLOCK):
            inside = (lane >= b * BLOCK) & (lane < (b + 1) * BLOCK)
            top = jnp.max(jnp.where(inside, size, 0.0), axis=1, keepdims=True) + 1e-06
            spread = jnp.where(inside, top, spread)
            table = jnp.where(lane == t * (LANES // BLOCK) + b, top, table)
        codes[:, t * LANES : (t + 1) * LANES] = (x / spread).astype(BF16)
    copies = [
        pltpu.make_async_copy(codes, codes_hbm, sems.at[0]),
        pltpu.make_async_copy(scales, scales_hbm, sems.at[1]),
    ]
    copies[0].start()
    scales[...] = table.T[: scales.shape[0]].astype(BF16)
    copies[1].start()
    for copy in copies:
        copy.wait()


def pool_call(lengths, list_ids, hidden, list_slot, gain, head, *, owners, peers, lists_own):
    passes, length, width = hidden.shape
    assert passes < SUB and length % STEP == 0
    group = list_ids.shape[0]
    capacity = max(2, 2 * group // owners)
    per = width // LANES // owners
    steps = length // STEP
    padded = -(-group // SUB) * SUB
    vmem = pl.BlockSpec(memory_space=pltpu.VMEM)
    hbm = pl.BlockSpec(memory_space=pl.ANY)
    return pl.pallas_call(
        functools.partial(
            pool_kernel, owners=owners, peers=peers, lists_own=lists_own, capacity=capacity
        ),
        out_shape=(
            pltpu.VMEM((owners * peers, 2, (per * -(-passes // 2) + 1) * LANES), BF16),
            pltpu.VMEM(head.shape, BF16),
        ),
        in_specs=[hbm] * 6,
        out_specs=(vmem, vmem),
        scratch_shapes=[
            pltpu.VMEM((passes * steps, STEP, width), BF16),
            pltpu.VMEM((2, STEP, 2 * LANES), BF16),
            pltpu.VMEM((passes, SUB, width), F32),
            pltpu.VMEM((padded, LANES), jnp.int32),
            pltpu.VMEM((width // LANES, LANES), BF16),
            pltpu.SMEM((passes,), jnp.int32),
            pltpu.SMEM((group,), jnp.int32),
            pltpu.SMEM((passes * steps,), jnp.int32),
            pltpu.SemaphoreType.DMA((passes * steps,)),
            pltpu.SemaphoreType.DMA,
            pltpu.SemaphoreType.DMA((4,)),
        ],
        compiler_params=pltpu.CompilerParams(vmem_limit_bytes=hidden.size * 2 + 6 * 2**20),
        name="pool",
    )(
        far(lengths), far(list_ids), far(hidden), far(list_slot.reshape(-1, LANES)),
        far(gain.reshape(-1, LANES)), far(head),
    )


def per_device(hidden, lengths, list_ids, gain, head, list_slot, centroids, rotation):
    passes, length, width = hidden.shape
    owners = lax.axis_size("chip") * lax.axis_size("core")
    peers = lax.axis_size("mp")
    group = list_ids.shape[0]
    lists_own = centroids.shape[0]
    capacity = max(2, 2 * group // owners)
    cols = head.shape[1]
    lead = -(-owners // SUB) * SUB
    vmem = pl.BlockSpec(memory_space=pltpu.VMEM)
    hbm = pl.BlockSpec(memory_space=pl.ANY)
    blocks, head = pool_call(
        lengths, list_ids, hidden, list_slot, gain, head,
        owners=owners, peers=peers, lists_own=lists_own,
    )
    got = lax.all_to_all(blocks, ("chip", "core", "mp"), 0, 0, tiled=True)
    half = owners // CORES * group
    own, other, rotation = pl.pallas_call(
        functools.partial(
            project_kernel, owners=owners, peers=peers, passes=passes, capacity=capacity
        ),
        out_shape=(
            pltpu.VMEM((half, cols), F32),
            pltpu.VMEM((half, cols), BF16),
            pltpu.VMEM(rotation.shape, BF16),
        ),
        in_specs=[vmem, vmem, hbm, hbm],
        out_specs=(vmem, vmem, vmem),
        scratch_shapes=[
            pltpu.VMEM((3, lead, LANES), jnp.int32),
            pltpu.SMEM((3, lead, LANES), jnp.int32),
            pltpu.VMEM((owners * capacity, SUB, cols), BF16),
            pltpu.SemaphoreType.DMA,
            pltpu.SemaphoreType.DMA,
            pltpu.SemaphoreType.DMA,
        ],
        compiler_params=pltpu.CompilerParams(vmem_limit_bytes=8 * 2**20),
        name="project",
    )(near(got), near(head), far(centroids), far(rotation))
    other = lax.ppermute(other, "core", [(c, (c + 1) % CORES) for c in range(CORES)])
    parts = pl.pallas_call(
        functools.partial(rotate_kernel, peers=peers),
        out_shape=pltpu.VMEM((owners // CORES * peers, group, cols), BF16),
        in_specs=[vmem, vmem, vmem],
        out_specs=vmem,
        compiler_params=pltpu.CompilerParams(vmem_limit_bytes=8 * 2**20),
        name="rotate",
    )(near(own), near(other), near(rotation))
    parts = lax.all_to_all(parts, ("chip", "mp"), 0, 0, tiled=True)
    codes, scales = pl.pallas_call(
        quantize_kernel,
        out_shape=(
            jax.ShapeDtypeStruct((group, cols), BF16),
            jax.ShapeDtypeStruct((cols // BLOCK, group), BF16),
        ),
        in_specs=[vmem],
        out_specs=(hbm, hbm),
        scratch_shapes=[
            pltpu.VMEM((group, cols), BF16),
            pltpu.VMEM((cols // BLOCK, group), BF16),
            pltpu.SemaphoreType.DMA((2,)),
        ],
        compiler_params=pltpu.CompilerParams(vmem_limit_bytes=8 * 2**20),
        name="quantize",
    )(near(parts))
    return codes, scales.T


def solution(mesh):
    dp, mp = mesh.shape["dp"], mesh.shape["mp"]
    split = Mesh(mesh.devices.reshape(dp // CORES, CORES, mp), ("chip", "core", "mp"))
    rows = ("chip", "core")
    in_specs = (
        P(("chip", "core", "mp"), None, None),
        P(("chip", "core", "mp")),
        P(rows),
        P(),
        P(rows, "mp"),
        P(),
        P(rows, None),
        P("mp", None),
    )
    out_specs = (P(rows, "mp"), P(rows, "mp"))
    return jax.shard_map(
        per_device, mesh=split, in_specs=in_specs, out_specs=out_specs, check_vma=False
    )
```
